32 devices in a mesh: seq: 8 (over z, x), fsdp: 4 (over y, core).
Axes of the slice: x: 2, y: 2, z: 4, core: 2. Of those that a mesh axis runs over, the one named last changes fastest.
Arguments:
- tokens: bfloat16 [4, 2048, 1024], P('fsdp', 'seq'), may hold values from -6 to 6
- cotangent: bfloat16 [4, 2048, 1024], P('fsdp', 'seq'), may hold values from -6 to 6
- offsets: int32 [4, 16], P('fsdp'), may hold values from 0 to 2047, as said below
- gain_in: bfloat16 [1024], P('fsdp'), may hold values from 0.5 to 1.5
- w_query: bfloat16 [1024, 1024], P('fsdp'), may hold values from -0.1875 to 0.1875
- w_key: bfloat16 [1024, 2048], P('fsdp'), may hold values from -0.1875 to 0.1875
- w_value: bfloat16 [1024, 2048], P('fsdp'), may hold values from -0.1875 to 0.1875
- w_beta: bfloat16 [1024, 16], P('fsdp'), may hold values from -0.1875 to 0.1875
- w_decay: bfloat16 [1024, 8], P('fsdp'), may hold values from -0.1875 to 0.1875
- w_outgate: bfloat16 [1024, 1024], P('fsdp'), may hold values from -0.1875 to 0.1875
- conv_query: bfloat16 [4, 1024], P(None, 'fsdp'), may hold values from -3 to 3
- conv_key: bfloat16 [4, 2048], P(None, 'fsdp'), may hold values from -3 to 3
- conv_value: bfloat16 [4, 2048], P(None, 'fsdp'), may hold values from -3 to 3
- decay_scale: float32 [8], replicated, may hold values from 0.001953125 to 0.0078125
- gain_head: bfloat16 [128], P('fsdp'), may hold values from 0.5 to 1.5
- w_out: bfloat16 [1024, 1024], P('fsdp'), may hold values from -0.375 to 0.375
- gain_ffn: bfloat16 [1024], P('fsdp'), may hold values from 0.5 to 1.5
- w_gate: bfloat16 [1024, 2816], P('fsdp'), may hold values from -0.1875 to 0.1875
- w_up: bfloat16 [1024, 2816], P('fsdp'), may hold values from -0.1875 to 0.1875
- w_down: bfloat16 [2816, 1024], P('fsdp'), may hold values from -0.109375 to 0.109375
Outputs:
- layer_out: bfloat16 [4, 2048, 1024], P('fsdp', 'seq')
- input_grad: bfloat16 [4, 2048, 1024], P('fsdp', 'seq')
- grad_gain_in: float32 [1024], P('fsdp')
- grad_query: float32 [1024, 1024], P('fsdp')
- grad_key: float32 [1024, 2048], P('fsdp')
- grad_value: float32 [1024, 2048], P('fsdp')
- grad_beta: float32 [1024, 16], P('fsdp')
- grad_decay: float32 [1024, 8], P('fsdp')
- grad_outgate: float32 [1024, 1024], P('fsdp')
- grad_conv_query: float32 [4, 1024], P(None, 'fsdp')
- grad_conv_key: float32 [4, 2048], P(None, 'fsdp')
- grad_conv_value: float32 [4, 2048], P(None, 'fsdp')
- grad_decay_scale: float32 [8], replicated
- grad_gain_head: float32 [128], P('fsdp')
- grad_out: float32 [1024, 1024], P('fsdp')
- grad_gain_ffn: float32 [1024], P('fsdp')
- grad_gate: float32 [1024, 2816], P('fsdp')
- grad_up: float32 [1024, 2816], P('fsdp')
- grad_down: float32 [2816, 1024], P('fsdp')
The draws below stay inside these ranges and needn't reach their ends.
Inputs may be any that keep to these rules, and one draw needn't show every extreme that they name: offsets[s, 0] is 0 and each row rises strictly; offsets[s, j] for 1 <= j <= 7 lie below 128, the later ones at 1920 or beyond.
All inputs are finite; a program needn't handle non-finite values.
Results may differ from the reference program's by a relative error of at most 0.035.
Values may be sent and summed in bfloat16 or wider, within the bound.
No kernel may reach another device: no remote copies, remote signals or barrier semaphores. Data moves between devices by JAX's collectives and lax.ppermute only.
A program may use at most 320 MiB of HBM per device.

```python
import math
import jax
import jax.numpy as jnp
from jax import lax

D = 1024
HEADS = 8
HEAD = 128
FF = 2816
STEPS = 2
CONV = 4
SPAN = 64
TOK_DEV = 256
DOCS = 16
LENGTH = 2048
NSEQS = 4


def draw_offsets(key, part):
    early_count = (DOCS - 1) // 2
    late_count = DOCS - 1 - early_count
    half_dev = TOK_DEV // 2

    def one_sequence(seq_index):
        seq_key = jax.random.fold_in(jax.random.fold_in(key, 41), seq_index)
        early_cuts = jax.random.permutation(jax.random.fold_in(seq_key, 1), half_dev - 1)[:early_count].astype(jnp.int32) + 1
        late_cuts = jax.random.permutation(jax.random.fold_in(seq_key, 2), half_dev)[:late_count].astype(jnp.int32) + (LENGTH - half_dev)
        all_cuts = jnp.sort(jnp.concatenate([early_cuts, late_cuts]))
        return jnp.concatenate([jnp.zeros((1,), jnp.int32), all_cuts.astype(jnp.int32)])
    return jax.vmap(one_sequence)(jnp.arange(NSEQS, dtype=jnp.int32))


def shard_levels(key, shape, pieces, least, high):
    def one(dim, blocks):
        steps = jax.random.uniform(jax.random.fold_in(jax.random.fold_in(key, 6), dim), (blocks,), jnp.float32, least / len(pieces), high / len(pieces))
        return jnp.repeat(jnp.exp(steps), shape[dim] // blocks).reshape((-1,) + (1,) * (len(shape) - dim - 1))

    factor_of = one(*pieces[0])
    for cut in pieces[1:]:
        factor_of = factor_of * one(*cut)
    return factor_of


def centred(own_key, shape, deviation, limit, pieces=(), held_as=jnp.bfloat16):
    drawn = deviation * jax.random.normal(own_key, shape, jnp.float32)
    if pieces:
        drawn = drawn * shard_levels(own_key, shape, pieces, -0.22, 0.18)
    return jnp.clip(drawn, -limit, limit).astype(held_as)


def setup_inputs(seed: int = 0) -> dict:
    key_list = jax.random.split(jax.random.key(seed), 21)
    tokens = centred(key_list[0], (NSEQS, LENGTH, D), 1.0, 6.0, ((0, 4), (1, 8)))
    cotangent = centred(key_list[1], (NSEQS, LENGTH, D), 1.0, 6.0, ((0, 4), (1, 8)))
    offsets = draw_offsets(jax.random.fold_in(key_list[20], 71), 0)
    gain_in = jnp.clip(1.0 + 0.1 * jax.random.normal(key_list[3], (D,), jnp.float32), 0.5, 1.5).astype(jnp.bfloat16)
    w_query = centred(key_list[4], (D, D), D ** -0.5, 0.1875, ((0, 4),))
    w_key = centred(key_list[5], (D, STEPS * D), D ** -0.5, 0.1875, ((0, 4),))
    w_value = centred(key_list[6], (D, STEPS * D), D ** -0.5, 0.1875, ((0, 4),))
    w_beta = centred(key_list[7], (D, STEPS * HEADS), D ** -0.5, 0.1875, ((0, 4),))
    w_decay = centred(key_list[8], (D, HEADS), D ** -0.5, 0.1875, ((0, 4),))
    w_outgate = centred(key_list[9], (D, D), D ** -0.5, 0.1875, ((0, 4),))
    conv_query = centred(key_list[10], (CONV, D), 0.5, 3.0, ((1, 4),))
    conv_key = centred(key_list[11], (CONV, STEPS * D), 0.5, 3.0, ((1, 4),))
    conv_value = centred(key_list[12], (CONV, STEPS * D), 0.5, 3.0, ((1, 4),))
    decay_scale = jnp.clip(jnp.exp(jax.random.uniform(key_list[13], (HEADS,), jnp.float32, math.log(0.001953125), math.log(0.0078125))), 0.001953125, 0.0078125)
    gain_head = jnp.clip(1.0 + 0.1 * jax.random.normal(key_list[14], (HEAD,), jnp.float32), 0.5, 1.5).astype(jnp.bfloat16)
    w_out = centred(key_list[15], (D, D), (D // 4) ** -0.5, 0.375, ((0, 4),))
    gain_ffn = jnp.clip(1.0 + 0.1 * jax.random.normal(key_list[16], (D,), jnp.float32), 0.5, 1.5).astype(jnp.bfloat16)
    w_gate = centred(key_list[17], (D, FF), D ** -0.5, 0.1875, ((0, 4),))
    w_up = centred(key_list[18], (D, FF), D ** -0.5, 0.1875, ((0, 4),))
    w_down = centred(key_list[19], (FF, D), FF ** -0.5, 0.109375, ((0, 4),))
    return {"tokens": tokens, "cotangent": cotangent, "offsets": offsets, "gain_in": gain_in, "w_query": w_query, "w_key": w_key, "w_value": w_value, "w_beta": w_beta, "w_decay": w_decay, "w_outgate": w_outgate, "conv_query": conv_query, "conv_key": conv_key, "conv_value": conv_value, "decay_scale": decay_scale, "gain_head": gain_head, "w_out": w_out, "gain_ffn": gain_ffn, "w_gate": w_gate, "w_up": w_up, "w_down": w_down}


EPSILON = 1e-06
EXACT = lax.Precision.HIGHEST

@jax.custom_vjp
def low(v):
    return lax.optimization_barrier(v.astype(jnp.bfloat16)).astype(jnp.float32)

@jax.custom_vjp
def low_back(v):
    return v

def low_keep(v):
    return (low(v), None)

def low_pass(kept, grad):
    return (grad,)

def back_keep(v):
    return (v, None)

def back_low(kept, grad):
    return (low(grad),)
low.defvjp(low_keep, low_pass)
low_back.defvjp(back_keep, back_low)

def rms_scale(values, gain_vec):
    return values * lax.rsqrt(lax.optimization_barrier(jnp.mean(values * values, axis=-1, keepdims=True)) + EPSILON) * gain_vec

def unit_rows(values):
    return values * lax.rsqrt(lax.optimization_barrier(jnp.sum(values * values, axis=-1, keepdims=True)) + EPSILON)

def doc_marks(doc_offsets, position, tap_count):
    doc_count = doc_offsets.shape[0]
    seg_ids = lax.optimization_barrier(jnp.sum((doc_offsets[None, 1:] <= position[:, None]).astype(jnp.int32), axis=1)).astype(jnp.int32)
    member = seg_ids[:, None] == jnp.arange(doc_count, dtype=jnp.int32)[None, :]
    doc_begin = lax.optimization_barrier(jnp.sum(jnp.where(member, doc_offsets[None, :], 0), axis=1)).astype(jnp.int32)
    starts = (position == doc_begin).astype(jnp.float32)
    lag_ids = jnp.arange(tap_count, dtype=jnp.int32)
    tap_valid = (position[:, None] - lag_ids[None, :] >= doc_begin[:, None]).astype(jnp.float32)
    return (starts, tap_valid)

def causal_conv(inputs, edge_rows, weights, tap_valid):
    tap_count = weights.shape[0]
    length = inputs.shape[0]
    padded = jnp.concatenate([edge_rows, inputs], axis=0)
    result = jnp.zeros_like(inputs)
    for lag_step in range(tap_count):
        begin_row = tap_count - 1 - lag_step
        result = result + weights[lag_step][None, :] * padded[begin_row:begin_row + length] * tap_valid[:, lag_step:lag_step + 1]
    return result

def mixer_inputs(pre_query, pre_key, pre_value, edge_query, edge_key, edge_value, conv_query, conv_key, conv_value, pre_beta, pre_decay, rate_scale, tap_valid):
    tokens_here = pre_query.shape[0]
    head_count = rate_scale.shape[0]
    model_width = pre_query.shape[1]
    head_dim = model_width // head_count
    step_count = pre_key.shape[1] // model_width
    queries = unit_rows(jax.nn.silu(causal_conv(pre_query, edge_query, conv_query, tap_valid)).reshape(tokens_here, head_count, head_dim))
    key_rows = unit_rows(jax.nn.silu(causal_conv(pre_key, edge_key, conv_key, tap_valid)).reshape(tokens_here, step_count, head_count, head_dim))
    value_rows = jax.nn.silu(causal_conv(pre_value, edge_value, conv_value, tap_valid)).reshape(tokens_here, step_count, head_count, head_dim)
    beta_rows = jax.nn.sigmoid(pre_beta).reshape(tokens_here, step_count, head_count)
    log_decay = -rate_scale[None, :] * jax.nn.softplus(pre_decay)
    return (queries, key_rows, value_rows, beta_rows, log_decay)

def delta_block(carry_state, block_data):
    queries, key_rows, value_rows, beta_rows, log_decay, starts = block_data
    block_len, step_count, head_count, key_dim = key_rows.shape
    value_dim = value_rows.shape[-1]
    row_count = block_len * step_count
    head_keys = jnp.transpose(key_rows, (2, 0, 1, 3)).reshape(head_count, row_count, key_dim)
    head_values = jnp.transpose(value_rows, (2, 0, 1, 3)).reshape(head_count, row_count, value_dim)
    head_beta = jnp.transpose(beta_rows, (2, 0, 1)).reshape(head_count, row_count)
    step_log = jnp.concatenate([log_decay[:, None, :], jnp.zeros((block_len, step_count - 1, head_count), jnp.float32)], axis=1)
    log_total = jnp.cumsum(jnp.transpose(step_log, (2, 0, 1)).reshape(head_count, row_count), axis=1)
    row_starts = jnp.concatenate([starts[:, None], jnp.zeros((block_len, step_count - 1), jnp.float32)], axis=1).reshape(row_count)
    resets = jnp.cumsum(row_starts)
    row_order = jnp.arange(row_count)
    same_doc = resets[:, None] == resets[None, :]
    lower_mask = ((row_order[:, None] >= row_order[None, :]) & same_doc)[None]
    strict = ((row_order[:, None] > row_order[None, :]) & same_doc)[None]
    spread = log_total[:, :, None] - log_total[:, None, :]
    decay_mask = jnp.where(lower_mask, jnp.exp(jnp.where(lower_mask, spread, 0.0)), 0.0)
    key_inner = jnp.einsum('hrd,hjd->hrj', head_keys, head_keys, precision=EXACT)
    system = jnp.eye(row_count, dtype=jnp.float32)[None] + jnp.where(strict, head_beta[:, :, None] * decay_mask * key_inner, 0.0)
    carry_in = jnp.exp(log_total) * (resets == 0.0).astype(jnp.float32)[None, :]
    recall = jnp.einsum('hrd,hdw->hrw', head_keys, carry_state, precision=EXACT)
    target = head_beta[:, :, None] * (head_values - carry_in[:, :, None] * recall)
    update = jax.scipy.linalg.solve_triangular(system, target, lower=True, unit_diagonal=True)
    head_query = jnp.transpose(queries, (1, 0, 2))
    scores = jnp.einsum('hcd,hjd->hcj', head_query, head_keys, precision=EXACT) * decay_mask[:, step_count - 1::step_count, :]
    outputs = jnp.einsum('hcj,hjw->hcw', scores, update, precision=EXACT)
    outputs = outputs + carry_in[:, step_count - 1::step_count, None] * jnp.einsum('hcd,hdw->hcw', head_query, carry_state, precision=EXACT)
    new_state = carry_in[:, -1, None, None] * carry_state + jnp.einsum('hrd,hrw->hdw', head_keys * decay_mask[:, -1, :, None], update, precision=EXACT)
    return (new_state, jnp.transpose(outputs, (1, 0, 2)))

def delta_scan(queries, key_rows, value_rows, beta_rows, log_decay, starts, carry_state):
    tokens_here = queries.shape[0]
    block_total = tokens_here // SPAN

    def block_split(values):
        return values.reshape((block_total, SPAN) + values.shape[1:])
    last_state, outputs = lax.scan(jax.checkpoint(delta_block), carry_state, (block_split(queries), block_split(key_rows), block_split(value_rows), block_split(beta_rows), block_split(log_decay), block_split(starts)))
    return (outputs.reshape((tokens_here,) + outputs.shape[2:]), last_state)

def gated_out(mixed_heads, gate_pre, gain_vec):
    tokens_here, head_count, head_dim = mixed_heads.shape
    gated_rows = rms_scale(mixed_heads, gain_vec) * jax.nn.silu(gate_pre.reshape(tokens_here, head_count, head_dim))
    return gated_rows.reshape(tokens_here, head_count * head_dim)

def dot_exact(left, right):
    return jnp.dot(left.astype(jnp.float32), right.astype(jnp.float32), precision=EXACT, preferred_element_type=jnp.float32)

def layer(inputs, params, starts, tap_valid):
    gain_in, w_query, w_key, w_value, w_beta, w_decay, w_outgate, conv_query, conv_key, conv_value, decay_scale, gain_head, w_out, gain_ffn, w_gate, w_up, w_down = params
    normed_in = low(rms_scale(inputs, gain_in))
    pre_query = low_back(low(dot_exact(normed_in, w_query)))
    pre_key = low_back(low(dot_exact(normed_in, w_key)))
    pre_value = low_back(low(dot_exact(normed_in, w_value)))
    pre_beta = low_back(dot_exact(normed_in, w_beta))
    pre_decay = low_back(dot_exact(normed_in, w_decay))
    pre_gate = low_back(dot_exact(normed_in, w_outgate))
    tap_count = conv_query.shape[0]
    edge_query = jnp.zeros((tap_count - 1, pre_query.shape[1]), jnp.float32)
    edge_key = jnp.zeros((tap_count - 1, pre_key.shape[1]), jnp.float32)
    edge_value = jnp.zeros((tap_count - 1, pre_value.shape[1]), jnp.float32)
    queries, key_rows, value_rows, beta_rows, log_decay = mixer_inputs(pre_query, pre_key, pre_value, edge_query, edge_key, edge_value, conv_query, conv_key, conv_value, pre_beta, pre_decay, decay_scale, tap_valid)
    head_count = decay_scale.shape[0]
    head_dim = pre_query.shape[1] // head_count
    mixed_heads, last_state = delta_scan(queries, key_rows, value_rows, beta_rows, log_decay, starts, jnp.zeros((head_count, head_dim, head_dim), jnp.float32))
    gated_low = low(gated_out(mixed_heads, pre_gate, gain_head))
    mixer_res = inputs + low_back(dot_exact(gated_low, w_out))
    mid_low = low(rms_scale(mixer_res, gain_ffn))
    gate_pre = low_back(dot_exact(mid_low, w_gate))
    up_pre = low_back(dot_exact(mid_low, w_up))
    hidden = low(jax.nn.silu(gate_pre) * up_pre)
    return mixer_res + dot_exact(hidden, w_down)

def reference(tokens, cotangent, offsets, gain_in, w_query, w_key, w_value, w_beta, w_decay, w_outgate, conv_query, conv_key, conv_value, decay_scale, gain_head, w_out, gain_ffn, w_gate, w_up, w_down):
    params = tuple((param_in.astype(jnp.float32) for param_in in (gain_in, w_query, w_key, w_value, w_beta, w_decay, w_outgate, conv_query, conv_key, conv_value, decay_scale, gain_head, w_out, gain_ffn, w_gate, w_up, w_down)))
    position = jnp.arange(tokens.shape[1], dtype=jnp.int32)
    tap_count = conv_query.shape[0]

    def one_sequence(running_sum, seq_item):
        seq_tokens, seq_cotangent, seq_offsets = seq_item
        starts, tap_valid = doc_marks(seq_offsets, position, tap_count)

        def forward(layer_in, layer_params):
            return layer(layer_in, layer_params, starts, tap_valid)
        layer_out, pull_back = jax.vjp(forward, seq_tokens.astype(jnp.float32), params)
        input_grad, param_grads = pull_back(seq_cotangent.astype(jnp.float32))
        running_sum = tuple((summed_grad + new_grad for summed_grad, new_grad in zip(running_sum, param_grads)))
        return (running_sum, (layer_out.astype(jnp.bfloat16), input_grad.astype(jnp.bfloat16)))
    zero_sums = tuple((jnp.zeros_like(param_in) for param_in in params))
    grad_sums, (layer_out, input_grad) = lax.scan(one_sequence, zero_sums, (tokens, cotangent, offsets))
    return (layer_out, input_grad, grad_sums[0], grad_sums[1], grad_sums[2], grad_sums[3], grad_sums[4], grad_sums[5], grad_sums[6], grad_sums[7], grad_sums[8], grad_sums[9], grad_sums[10], grad_sums[11], grad_sums[12], grad_sums[13], grad_sums[14], grad_sums[15], grad_sums[16])
```

```python
import functools

import jax
import jax.numpy as jnp
from jax import lax
from jax.experimental import pallas as pl
from jax.experimental.pallas import tpu as pltpu
from jax.sharding import PartitionSpec as P

SPAN = 64
ROWS = 128
HEAD = 128
EPSILON = 1e-06
LOW = jnp.bfloat16
WIDE = jnp.float32
VMEM_LIMIT = 56 * 1024 * 1024


def contract(left, right, left_dim, right_dim):
    return lax.dot_general(
        left, right, (((left_dim,), (right_dim,)), ((), ())), preferred_element_type=WIDE
    )


def halves(value):
    high = value.astype(LOW)
    return high, (value - high.astype(WIDE)).astype(LOW)


def mm(left, right, left_dim=1, right_dim=0):
    return contract(left.astype(LOW), right.astype(LOW), left_dim, right_dim)


def mm3(left, right, left_dim=1, right_dim=0):
    lh, ll = halves(left)
    rh, rl = halves(right)
    return (
        contract(lh, rh, left_dim, right_dim)
        + contract(lh, rl, left_dim, right_dim)
        + contract(ll, rh, left_dim, right_dim)
    )


def stack(*parts):
    return jnp.concatenate(parts, axis=0)


def row_maps():
    row = lax.broadcasted_iota(jnp.int32, (ROWS, ROWS), 0)
    col = lax.broadcasted_iota(jnp.int32, (ROWS, ROWS), 1)
    tok, step = row & (SPAN - 1), row >> 6
    tok_c, step_c = col & (SPAN - 1), col >> 6
    return tok, step, tok_c, step_c


def span_tokens(offs_ref, doc_count, first):
    place = first + lax.broadcasted_iota(jnp.int32, (SPAN, 1), 0)
    begin = jnp.zeros((SPAN, 1), jnp.int32)
    for j in range(doc_count):
        start = offs_ref[0, j]
        begin = jnp.where(place >= start, start, begin)
    return place - begin


def softplus(value):
    return jnp.maximum(value, 0.0) + jnp.log1p(jnp.exp(-jnp.abs(value)))


def decay_sums(small, rate):
    logs = -rate * softplus(small)
    tok = lax.broadcasted_iota(jnp.int32, (SPAN, SPAN), 0)
    tok_c = lax.broadcasted_iota(jnp.int32, (SPAN, SPAN), 1)
    lower = jnp.where(tok >= tok_c, 1.0, 0.0).astype(LOW)
    tok_w = lax.broadcasted_iota(jnp.int32, (SPAN, ROWS), 0)
    tok_wc = lax.broadcasted_iota(jnp.int32, (SPAN, ROWS), 1) & (SPAN - 1)
    upper = jnp.where(tok_w <= tok_wc, 1.0, 0.0).astype(LOW)
    high, rest = halves(logs)
    cols = contract(lower, high, 1, 0) + contract(lower, rest, 1, 0)
    rows = contract(high, upper, 0, 0) + contract(rest, upper, 0, 0)
    return cols[:, 2:3], rows[2:3, :]


def unit(values):
    scale = lax.rsqrt(jnp.sum(values * values, axis=1, keepdims=True) + EPSILON)
    return values * scale, scale


def span_factors(small, rate, pos):
    sig = jax.nn.sigmoid(small)
    cum, cum_row = decay_sums(small, rate)
    beta = stack(sig[:, 0:1], sig[:, 1:2])
    cum2, pos2 = stack(cum, cum), stack(pos, pos)
    tok, step, tok_c, step_c = row_maps()
    before = tok > tok_c
    here = tok == tok_c
    reach = (before | (here & (step >= step_c))) & (tok - tok_c <= pos2)
    decay = jnp.where(reach, jnp.exp(jnp.where(reach, cum2 - cum_row, 0.0)), 0.0)
    strict = before | (here & (step > step_c))
    tok1 = tok[:, 0:1]
    carry = jnp.where(pos2 > tok1, jnp.exp(cum2), 0.0)
    end, end_pos = cum[SPAN - 1 : SPAN], pos[SPAN - 1 : SPAN]
    leave = jnp.where(SPAN - 1 - tok1 <= end_pos, jnp.exp(end - cum2), 0.0)
    carry_all = jnp.where(end_pos >= SPAN, jnp.exp(end), 0.0)
    return beta, decay, strict, carry, leave, carry_all, tok ^ tok_c


def unit_lower_inverse(strict_part, apart):
    row = lax.broadcasted_iota(jnp.int32, (ROWS, ROWS), 0)
    col = lax.broadcasted_iota(jnp.int32, (ROWS, ROWS), 1)
    inverse = jnp.where(row == col, 1.0, 0.0) - jnp.where(apart == 0, strict_part, 0.0)
    for level in range(6):
        block = jnp.where((apart >> level) == 1, strict_part, 0.0)
        inverse = inverse - mm(mm(inverse, block), inverse)
    return inverse


def forward_kernel(
    span_count, doc_count, group,
    offs_ref, rate_ref, pre_ref, gs_ref, edge_ref, taps_ref, gain_ref, state_ref,
    gated_ref, mixed_ref, conv_ref, t_ref, u_ref, sc_ref, qh_ref, a_ref, s_ref, end_ref,
    w_scr, u0_scr, b_scr, o0_scr,
):
    base = offs_ref[0, doc_count]
    rate = rate_ref[0, 0]

    def local(c):
        lo = pl.multiple_of(c * SPAN, SPAN)
        here = pre_ref[pl.ds(lo, SPAN), :].astype(WIDE)
        prior_at = pl.multiple_of(jnp.maximum(lo - 16, 0), 16)
        prior = pre_ref[pl.ds(prior_at, 16), :].astype(WIDE)
        prior = jnp.where(c == 0, edge_ref[...].astype(WIDE), prior)
        rows = stack(prior, here)
        pos = span_tokens(offs_ref, doc_count, base + lo)
        conv = taps_ref[0:1, :] * here
        for lag in range(1, 4):
            shifted = rows[16 - lag : 16 - lag + SPAN]
            conv = conv + jnp.where(pos >= lag, taps_ref[lag : lag + 1, :] * shifted, 0.0)
        conv_ref[pl.ds(lo, SPAN), :] = conv
        act = conv * jax.nn.sigmoid(conv)
        query, _ = unit(act[:, 0:128])
        key0, _ = unit(act[:, 128:256])
        key1, _ = unit(act[:, 256:384])
        keys = stack(key0, key1)
        values = stack(act[:, 384:512], act[:, 512:640])
        small = gs_ref[pl.ds(lo, SPAN), 128:256]
        beta, decay, strict, carry, leave, carry_all, apart = span_factors(small, rate, pos)
        inner = mm(keys, keys, 1, 1)
        inverse = unit_lower_inverse(jnp.where(strict, beta * decay * inner, 0.0), apart)
        t_ref[c] = inverse.astype(LOW)
        both = mm(inverse, jnp.concatenate([(beta * carry) * keys, beta * values], axis=1))
        weight, fresh = both[:, :HEAD], both[:, HEAD:]
        w_scr[c] = weight.astype(LOW)
        u0_scr[c] = fresh
        leaving = (keys * leave).astype(LOW)
        row = lax.broadcasted_iota(jnp.int32, (HEAD, HEAD), 0)
        col = lax.broadcasted_iota(jnp.int32, (HEAD, HEAD), 1)
        a_ref[c] = jnp.where(row == col, carry_all, 0.0) - mm(leaving, weight, 0, 0)
        b_scr[c] = mm(fresh, leaving, 0, 0)
        scores = mm(query, keys, 1, 1) * decay[SPAN:, :]
        sc_ref[c] = scores.astype(LOW)
        mixed_both = mm(scores, both)
        qh_ref[c] = (carry[SPAN:] * query - mixed_both[:, :HEAD]).astype(LOW)
        o0_scr[c] = mixed_both[:, HEAD:]

    def locals_step(i, none):
        for u in range(group):
            local(i * group + u)
        return none

    lax.fori_loop(0, span_count // group, locals_step, 0)

    def chain(c, state):
        s_ref[c] = state
        u_ref[c] = (u0_scr[c] - mm(w_scr[c], state, 1, 1)).astype(LOW)
        mixed = o0_scr[c] + mm(qh_ref[c], state, 1, 1)
        lo = pl.multiple_of(c * SPAN, SPAN)
        mixed_ref[pl.ds(lo, SPAN), :] = mixed
        gate = gs_ref[pl.ds(lo, SPAN), 0:128]
        scale = lax.rsqrt(jnp.mean(mixed * mixed, axis=1, keepdims=True) + EPSILON)
        gated_ref[pl.ds(lo, SPAN), :] = (
            mixed * scale * gain_ref[...] * (gate * jax.nn.sigmoid(gate))
        ).astype(LOW)
        return mm3(state, a_ref[c], 1, 1) + b_scr[c]

    def chain_step(i, state):
        for u in range(group):
            state = chain(i * group + u, state)
        return state

    end_ref[...] = lax.fori_loop(0, span_count // group, chain_step, state_ref[...])


def backward_kernel(
    span_count, doc_count, group,
    offs_ref, rate_ref, pre_ref, gs_ref, edge_ref, taps_ref, gain_ref,
    mixed_ref, conv_ref, t_ref, u_ref, sc_ref, qh_ref, a_ref, s_ref, dgated_ref, dend_ref,
    dy_ref, dtaps_ref, dgain_ref, drate_ref, dedge_ref, dbegin_ref,
    do_scr, f_scr, ds_scr, next_scr,
):
    base = offs_ref[0, doc_count]
    rate = rate_ref[0, 0]
    dgain_ref[...] = jnp.zeros_like(dgain_ref)
    dtaps_ref[...] = jnp.zeros_like(dtaps_ref)
    drate_ref[...] = jnp.zeros_like(drate_ref)
    next_scr[...] = jnp.zeros_like(next_scr)

    def gate_back(c):
        lo = pl.multiple_of(c * SPAN, SPAN)
        mixed = mixed_ref[pl.ds(lo, SPAN), :]
        gate = gs_ref[pl.ds(lo, SPAN), 0:128]
        scale = lax.rsqrt(jnp.mean(mixed * mixed, axis=1, keepdims=True) + EPSILON)
        normed = mixed * scale
        sig = jax.nn.sigmoid(gate)
        grad = dgated_ref[pl.ds(lo, SPAN), :].astype(WIDE)
        by_gain = grad * normed
        dy_ref[pl.ds(lo, SPAN), 640:768] = (
            by_gain * gain_ref[...] * (sig * (1.0 + gate * (1.0 - sig)))
        ).astype(LOW)
        dgain_ref[...] += jnp.sum(by_gain * (gate * sig), axis=0, keepdims=True)
        dn = grad * (gate * sig) * gain_ref[...]
        dmixed = scale * (dn - normed * jnp.mean(dn * normed, axis=1, keepdims=True))
        do_low = dmixed.astype(LOW)
        do_scr[c] = do_low
        f_scr[c] = contract(do_low, qh_ref[c], 0, 0)

    def gate_step(i, none):
        for u in range(group):
            gate_back(i * group + u)
        return none

    lax.fori_loop(0, span_count // group, gate_step, 0)

    def chain_step(i, grad):
        for u in range(group):
            c = span_count - 1 - (i * group + u)
            ds_scr[c] = grad
            grad = mm3(grad, a_ref[c]) + f_scr[c]
        return grad

    dbegin_ref[...] = lax.fori_loop(0, span_count // group, chain_step, dend_ref[...])

    def local(c):
        lo = pl.multiple_of(c * SPAN, SPAN)
        pos = span_tokens(offs_ref, doc_count, base + lo)
        conv = conv_ref[pl.ds(lo, SPAN), :]
        sig = jax.nn.sigmoid(conv)
        act = conv * sig
        query, scale_q = unit(act[:, 0:128])
        key0, scale_0 = unit(act[:, 128:256])
        key1, scale_1 = unit(act[:, 256:384])
        keys = stack(key0, key1)
        values = stack(act[:, 384:512], act[:, 512:640])
        small = gs_ref[pl.ds(lo, SPAN), 128:256]
        beta, decay, strict, carry, leave, carry_all, _ = span_factors(small, rate, pos)
        state, dstate = s_ref[c], ds_scr[c]
        state_l, dstate_l = state.astype(LOW), dstate.astype(LOW)
        upd, out_grad, keys_l = u_ref[c], do_scr[c], keys.astype(LOW)
        dupd = contract(sc_ref[c], out_grad, 0, 0) + mm(keys * leave, dstate_l, 1, 1)
        dtarget = mm(t_ref[c], dupd, 0, 0)
        pair = stack(dtarget.astype(LOW), out_grad)
        by_upd = contract(pair, upd, 1, 1)
        by_state = contract(pair, state_l, 1, 0)
        dinner = jnp.where(strict, -by_upd[:ROWS] * decay, 0.0)
        dscore = by_upd[ROWS:] * decay[SPAN:, :]
        both = stack(dinner, dscore).astype(LOW)
        reading = contract(both, keys_l, 1, 0)
        read_key = reading[:ROWS] - carry * by_state[:ROWS]
        dquery = reading[ROWS:] + carry[SPAN:] * by_state[ROWS:]
        dleave = leave * contract(upd, dstate_l, 1, 0)
        write_key = contract(both, stack(beta * keys, query).astype(LOW), 0, 0) + dleave
        key_read = jnp.sum(keys * read_key, axis=1, keepdims=True)
        dbeta = jnp.sum(dtarget * values, axis=1, keepdims=True) + key_read
        dcum = beta * key_read - jnp.sum(keys * write_key, axis=1, keepdims=True)
        dcum = dcum[:SPAN] + dcum[SPAN:] + jnp.sum(query * dquery, axis=1, keepdims=True)
        through = jnp.sum(keys * dleave, axis=0, keepdims=True) + carry_all * jnp.sum(
            dstate * state, axis=0, keepdims=True
        )
        through = jnp.sum(through, axis=1, keepdims=True)
        tok1 = lax.broadcasted_iota(jnp.int32, (SPAN, 1), 0)
        dcum = dcum + jnp.where(tok1 == SPAN - 1, through, 0.0)
        tok = lax.broadcasted_iota(jnp.int32, (SPAN, SPAN), 0)
        tok_c = lax.broadcasted_iota(jnp.int32, (SPAN, SPAN), 1)
        upper = jnp.where(tok <= tok_c, 1.0, 0.0).astype(LOW)
        high, rest = halves(jnp.broadcast_to(dcum, (SPAN, 128)))
        dlog = contract(upper, high, 1, 0) + contract(upper, rest, 1, 0)
        soft = softplus(small)
        sig_small = jax.nn.sigmoid(small)
        lane = lax.broadcasted_iota(jnp.int32, (SPAN, 128), 1)
        drate_ref[...] += jnp.sum(jnp.where(lane == 2, -dlog * soft, 0.0), axis=0, keepdims=True)
        dsig = jnp.where(lane == 0, dbeta[:SPAN], dbeta[SPAN:]) * sig_small * (1.0 - sig_small)
        dsmall = jnp.where(lane < 2, dsig, jnp.where(lane == 2, -rate * dlog * sig_small, 0.0))
        dy_ref[pl.ds(lo, SPAN), 768:896] = dsmall.astype(LOW)
        dkey = beta * read_key + write_key
        dvalue = beta * dtarget

        def unit_back(grad, normed, scale):
            return scale * (grad - normed * jnp.sum(grad * normed, axis=1, keepdims=True))

        dact = jnp.concatenate(
            [
                unit_back(dquery, query, scale_q),
                unit_back(dkey[:SPAN], key0, scale_0),
                unit_back(dkey[SPAN:], key1, scale_1),
                dvalue[:SPAN],
                dvalue[SPAN:],
            ],
            axis=1,
        )
        dconv = dact * (sig * (1.0 + conv * (1.0 - sig)))
        here = pre_ref[pl.ds(lo, SPAN), :].astype(WIDE)
        prior_at = pl.multiple_of(jnp.maximum(lo - 16, 0), 16)
        prior = pre_ref[pl.ds(prior_at, 16), :].astype(WIDE)
        prior = jnp.where(c == 0, edge_ref[...].astype(WIDE), prior)
        rows = stack(prior, here)
        dpre = taps_ref[0:1, :] * dconv
        dtaps_ref[0:1, :] += jnp.sum(dconv * here, axis=0, keepdims=True)
        for lag in range(1, 4):
            kept = jnp.where(pos >= lag, dconv, 0.0)
            shifted = rows[16 - lag : 16 - lag + SPAN]
            dtaps_ref[lag : lag + 1, :] += jnp.sum(kept * shifted, axis=0, keepdims=True)
            kept = kept * taps_ref[lag : lag + 1, :]
            dpre = dpre + stack(kept, next_scr[lag])[lag : lag + SPAN]
            next_scr[lag] = kept[0:8]
        dy_ref[pl.ds(lo, SPAN), 0:640] = dpre.astype(LOW)

    def local_step(i, none):
        for u in range(group):
            local(span_count - 1 - (i * group + u))
        return none

    lax.fori_loop(0, span_count // group, local_step, 0)

    none = jnp.zeros((16, 640), WIDE)
    dedge = none
    for lag in range(1, 4):
        dedge = dedge + stack(none, next_scr[lag])[lag : lag + 16]
    dedge_ref[...] = dedge


def vmem_spec():
    return pl.BlockSpec(memory_space=pltpu.VMEM)


def smem_spec():
    return pl.BlockSpec(memory_space=pltpu.SMEM)


def run_forward(offs, rate, pre, gs, edge, taps, gain, state):
    tokens = pre.shape[0]
    spans = tokens // SPAN
    shape = jax.ShapeDtypeStruct
    outs = (
        shape((tokens, HEAD), LOW),
        shape((tokens, HEAD), WIDE),
        shape((tokens, 640), WIDE),
        shape((spans, ROWS, ROWS), LOW),
        shape((spans, ROWS, HEAD), LOW),
        shape((spans, SPAN, ROWS), LOW),
        shape((spans, SPAN, HEAD), LOW),
        shape((spans, HEAD, HEAD), WIDE),
        shape((spans, HEAD, HEAD), WIDE),
        shape((HEAD, HEAD), WIDE),
    )
    return pl.pallas_call(
        functools.partial(forward_kernel, spans, offs.shape[1] - 1, 4),
        out_shape=outs,
        in_specs=[smem_spec(), smem_spec()] + [vmem_spec()] * 6,
        out_specs=[vmem_spec()] * len(outs),
        scratch_shapes=[
            pltpu.VMEM((spans, ROWS, HEAD), LOW),
            pltpu.VMEM((spans, ROWS, HEAD), WIDE),
            pltpu.VMEM((spans, HEAD, HEAD), WIDE),
            pltpu.VMEM((spans, SPAN, HEAD), WIDE),
        ],
        compiler_params=pltpu.CompilerParams(vmem_limit_bytes=VMEM_LIMIT),
        cost_estimate=pl.CostEstimate(
            flops=spans * 60 * 2 * 128**3, bytes_accessed=24 * 1024 * 1024, transcendentals=0
        ),
        name="delta_forward",
    )(offs, rate, pre, gs, edge, taps, gain, state)


def run_backward(offs, rate, pre, gs, edge, taps, gain, saved, dgated, dend):
    tokens = pre.shape[0]
    spans = tokens // SPAN
    shape = jax.ShapeDtypeStruct
    outs = (
        shape((tokens, 896), LOW),
        shape((8, 640), WIDE),
        shape((1, HEAD), WIDE),
        shape((1, HEAD), WIDE),
        shape((16, 640), WIDE),
        shape((HEAD, HEAD), WIDE),
    )
    return pl.pallas_call(
        functools.partial(backward_kernel, spans, offs.shape[1] - 1, 2),
        out_shape=outs,
        in_specs=[smem_spec(), smem_spec()] + [vmem_spec()] * 15,
        out_specs=[vmem_spec()] * len(outs),
        scratch_shapes=[
            pltpu.VMEM((spans, SPAN, HEAD), LOW),
            pltpu.VMEM((spans, HEAD, HEAD), WIDE),
            pltpu.VMEM((spans, HEAD, HEAD), WIDE),
            pltpu.VMEM((4, 8, 640), WIDE),
        ],
        compiler_params=pltpu.CompilerParams(vmem_limit_bytes=VMEM_LIMIT),
        cost_estimate=pl.CostEstimate(
            flops=spans * 80 * 2 * 128**3, bytes_accessed=24 * 1024 * 1024, transcendentals=0
        ),
        name="delta_backward",
    )(offs, rate, pre, gs, edge, taps, gain, *saved, dgated, dend)


def rms_parts(values):
    return values * lax.rsqrt(jnp.mean(values * values, axis=-1, keepdims=True) + EPSILON)


def rms_back(grad_scaled, values):
    scale = lax.rsqrt(jnp.mean(values * values, axis=-1, keepdims=True) + EPSILON)
    normed = values * scale
    return scale * (
        grad_scaled - normed * jnp.mean(grad_scaled * normed, axis=-1, keepdims=True)
    )


def dot_plain(left, right, kind=WIDE):
    return jnp.dot(left, right, preferred_element_type=kind)


def dot_left(left, right, kind=WIDE):
    return contract(left, right, 0, 0).astype(kind)


def dot_right(left, right):
    return contract(left, right, 1, 1)


def per_device(
    tokens, cotangent, offsets, gain_in, w_query, w_key, w_value, w_beta, w_decay, w_outgate,
    conv_query, conv_key, conv_value, decay_scale, gain_head, w_out, gain_ffn, w_gate, w_up,
    w_down,
):
    seq, fsdp = lax.axis_size("seq"), lax.axis_size("fsdp")
    heads = decay_scale.shape[0]
    taps = conv_query.shape[0]
    own_rows = tokens.shape[1]
    shard = w_query.shape[0]
    width = shard * fsdp
    teams = seq // heads
    assert teams * heads == seq and width == heads * HEAD
    place = lax.axis_index("seq")
    head, team = place % heads, place // heads
    member = lax.axis_index("fsdp")
    if teams == 1:
        team_groups, head_groups = None, None
    else:
        team_groups = [[t * heads + h for h in range(heads)] for t in range(teams)]
        head_groups = [[t * heads + h for t in range(teams)] for h in range(heads)]

    def gather_rows(value):
        return lax.all_gather(value, "fsdp", axis=0, tiled=True)

    seq_tokens = lax.all_gather(
        tokens[0], "seq", axis=0, tiled=True, axis_index_groups=team_groups
    )
    length = seq_tokens.shape[0]

    def head_columns(weights, step):
        return lax.dynamic_slice_in_dim(weights, step * width + head * HEAD, HEAD, axis=1)

    small_columns = jnp.concatenate(
        [
            lax.dynamic_slice_in_dim(w_beta, head, 1, axis=1),
            lax.dynamic_slice_in_dim(w_beta, heads + head, 1, axis=1),
            lax.dynamic_slice_in_dim(w_decay, head, 1, axis=1),
            jnp.zeros((shard, HEAD - 3), LOW),
        ],
        axis=1,
    )
    packed = jnp.concatenate(
        [
            head_columns(w_query, 0),
            head_columns(w_key, 0),
            head_columns(w_key, 1),
            head_columns(w_value, 0),
            head_columns(w_value, 1),
            head_columns(w_outgate, 0),
            small_columns,
        ],
        axis=1,
    )
    full_packed = gather_rows(packed)
    vectors = jnp.concatenate(
        [
            gain_in[None],
            gain_ffn[None],
            jnp.pad(gain_head, (0, shard - gain_head.shape[0]))[None],
            conv_query,
            conv_key[:, :shard],
            conv_key[:, shard:],
            conv_value[:, :shard],
            conv_value[:, shard:],
        ],
        axis=0,
    )
    vectors = lax.all_gather(vectors, "fsdp", axis=0)
    full_gain_in = vectors[:, 0].reshape(width).astype(WIDE)
    full_gain_ffn = vectors[:, 1].reshape(width).astype(WIDE)
    full_gain_head = vectors[:, 2, : gain_head.shape[0]].reshape(1, HEAD).astype(WIDE)

    def full_taps(at, pieces):
        part = vectors[:, at : at + pieces * taps].reshape(fsdp, pieces, taps, shard)
        return jnp.transpose(part, (2, 0, 1, 3)).reshape(taps, fsdp * pieces * shard)

    conv_q = full_taps(3, 1)
    conv_k = full_taps(3 + taps, 2)
    conv_v = full_taps(3 + 3 * taps, 2)
    head_taps = jnp.concatenate(
        [
            head_columns(conv_q, 0),
            head_columns(conv_k, 0),
            head_columns(conv_k, 1),
            head_columns(conv_v, 0),
            head_columns(conv_v, 1),
        ],
        axis=1,
    ).astype(WIDE)
    head_taps = jnp.pad(head_taps, ((0, 8 - taps), (0, 0)))
    full_out = gather_rows(w_out)

    def to_columns(value):
        return lax.all_to_all(value, "fsdp", 1, 0, tiled=True)

    cols_gate, cols_up = to_columns(w_gate), to_columns(w_up)
    group_cot = gather_rows(cotangent[0])

    seq_wide = seq_tokens.astype(WIDE)
    normed_low = (rms_parts(seq_wide) * full_gain_in).astype(LOW)
    pre = dot_plain(normed_low, full_packed[:, :640]).astype(LOW)
    gate_small = dot_plain(normed_low, full_packed[:, 640:])
    offs = jnp.concatenate(
        [offsets, jnp.broadcast_to(team * length, (1, 1)).astype(jnp.int32)], axis=1
    )
    rate = lax.dynamic_slice_in_dim(decay_scale, head, 1).reshape(1, 1)
    zero_state = jnp.zeros((HEAD, HEAD), WIDE)
    if teams == 1:
        edge = jnp.zeros((16, 640), LOW)
    else:
        forth = [(i, i + heads) for i in range(seq - heads)]
        back = [(i + heads, i) for i in range(seq - heads)]
        edge = lax.ppermute(pre[-16:], "seq", forth)

    def forward_from(state):
        return run_forward(
            offs, rate, pre, gate_small, edge, head_taps, full_gain_head, state
        )

    state_in = zero_state
    if teams > 1:
        trial = forward_from(zero_state)
        steps, end = trial[7], trial[9]

        def along(c, total):
            return jnp.dot(total, steps[c].T, precision=lax.Precision.HIGHEST)

        whole_map = lax.fori_loop(0, steps.shape[0], along, jnp.eye(HEAD, dtype=WIDE))
        for _ in range(teams - 1):
            out = jnp.dot(state_in, whole_map, precision=lax.Precision.HIGHEST) + end
            state_in = lax.ppermute(out.astype(LOW), "seq", forth).astype(WIDE)
    gated, *saved, _ = forward_from(state_in)

    gated_own = lax.all_to_all(
        gated, "seq", 0, 1, tiled=True, axis_index_groups=team_groups
    )
    inputs = tokens[0].astype(WIDE)
    mixer_res = inputs + dot_plain(gated_own, full_out)

    mid_normed = rms_parts(mixer_res)
    mid_low = (mid_normed * full_gain_ffn).astype(LOW)
    group_mid = gather_rows(mid_low)
    gate_pre = dot_plain(group_mid, cols_gate)
    up_pre = dot_plain(group_mid, cols_up)
    sig = jax.nn.sigmoid(gate_pre)
    act = gate_pre * sig
    hidden = (act * up_pre).astype(LOW)
    grad_hidden = dot_right(group_cot, w_down)
    grad_gate_pre = (grad_hidden * up_pre * (sig * (1.0 + gate_pre * (1.0 - sig)))).astype(LOW)
    grad_up_pre = (grad_hidden * act).astype(LOW)
    grad_mid = dot_right(grad_gate_pre, cols_gate) + dot_right(grad_up_pre, cols_up)
    grad_mid = lax.psum_scatter(
        grad_mid.astype(LOW), "fsdp", scatter_dimension=0, tiled=True
    ).astype(WIDE)
    down_part = lax.psum_scatter(
        dot_plain(hidden, w_down).astype(LOW), "fsdp", scatter_dimension=0, tiled=True
    )
    layer_out = (mixer_res + down_part.astype(WIDE)).astype(LOW)

    grad_res = cotangent[0].astype(WIDE) + rms_back(grad_mid * full_gain_ffn, mixer_res)
    grad_gain_ffn = jnp.sum(grad_mid * mid_normed, axis=0)
    res_low = grad_res.astype(LOW)
    grad_gated = dot_right(res_low, full_out).astype(LOW)
    dgated = lax.all_to_all(
        grad_gated, "seq", 1, 0, tiled=True, axis_index_groups=team_groups
    )

    grad_down = dot_left(hidden, group_cot, LOW)
    grad_gate = dot_left(group_mid, grad_gate_pre, LOW)
    grad_up = dot_left(group_mid, grad_up_pre, LOW)
    grad_out = dot_left(gated_own, res_low, LOW)

    def share(value):
        return lax.psum_scatter(value, "seq", scatter_dimension=0, tiled=True)

    def whole(value):
        return lax.all_gather(value, "seq", axis=0, tiled=True)

    def columns_done(value):
        part = value.reshape(fsdp, seq, shard // seq, value.shape[1])
        part = lax.psum_scatter(part, "seq", scatter_dimension=1, tiled=True)
        part = part.reshape(shard // seq * fsdp, value.shape[1])
        part = lax.all_to_all(part, "fsdp", 0, 1, tiled=True)
        return whole(part).astype(WIDE)

    out_gate, out_up = columns_done(grad_gate), columns_done(grad_up)
    out_down = whole(share(grad_down)).astype(WIDE)
    grad_out = lax.psum_scatter(grad_out, "fsdp", scatter_dimension=0, tiled=True)
    out_out = lax.psum(grad_out, "seq").astype(WIDE)

    def backward_from(dend):
        return run_backward(
            offs, rate, pre, gate_small, edge, head_taps, full_gain_head, saved, dgated, dend
        )

    dend = zero_state
    if teams > 1:
        begin = backward_from(zero_state)[5]
        for _ in range(teams - 1):
            out = lax.dot_general(
                dend, whole_map, (((1,), (1,)), ((), ())), precision=lax.Precision.HIGHEST
            )
            dend = lax.ppermute((out + begin).astype(LOW), "seq", back).astype(WIDE)
    dy, dtaps, dgain, drate, dedge, _ = backward_from(dend)
    if teams > 1:
        from_next = lax.ppermute(dedge.astype(LOW), "seq", back).astype(WIDE)
        tail = (dy[-16:, :640].astype(WIDE) + from_next).astype(LOW)
        dy = lax.dynamic_update_slice(dy, tail, (length - 16, 0))

    grad_normed = dot_right(dy, full_packed)
    grad_gain_in = jnp.sum(grad_normed * rms_parts(seq_wide), axis=0)
    grad_normed = lax.psum_scatter(
        grad_normed.astype(LOW), "seq", scatter_dimension=0, tiled=True,
        axis_index_groups=team_groups,
    ).astype(WIDE)
    input_grad = (grad_res + rms_back(grad_normed * full_gain_in, inputs)).astype(LOW)

    grad_packed = dot_left(normed_low, dy)
    extra = jnp.zeros((fsdp, 16, 896), WIDE)
    extra = extra.at[:, 0, :shard].set(grad_gain_in.reshape(fsdp, shard))
    extra = extra.at[:, 1, :shard].set(grad_gain_ffn.reshape(fsdp, shard))
    gh = gain_head.shape[0]
    extra = extra.at[:, 2, :gh].set(dgain.reshape(fsdp, gh))
    extra = extra.at[:, 3, :HEAD].set(drate)
    extra = extra.at[:, 4 : 4 + taps, :640].set(dtaps[None, :taps])
    combined = jnp.concatenate(
        [grad_packed.reshape(fsdp, shard, 896), extra], axis=1
    ).astype(LOW)
    combined = lax.psum_scatter(
        combined.reshape(fsdp * (shard + 16), 896), "fsdp", scatter_dimension=0, tiled=True
    )
    if teams > 1:
        combined = lax.psum(combined, "seq", axis_index_groups=head_groups)
    combined = lax.all_gather(combined, "seq", axis=0, axis_index_groups=team_groups)

    def by_head(at):
        return jnp.transpose(combined[:, :shard, at : at + HEAD], (1, 0, 2)).reshape(shard, width)

    out_query = by_head(0).astype(WIDE)
    out_key = jnp.concatenate([by_head(128), by_head(256)], axis=1).astype(WIDE)
    out_value = jnp.concatenate([by_head(384), by_head(512)], axis=1).astype(WIDE)
    out_gatew = by_head(640).astype(WIDE)
    smalls = jnp.transpose(combined[:, :shard, 768:771], (1, 2, 0))
    out_beta = smalls[:, 0:2].reshape(shard, 2 * heads).astype(WIDE)
    out_decay = smalls[:, 2].astype(WIDE)
    extras = combined[:, shard:].astype(WIDE)
    if teams > 1:
        pass
    out_gain_in = jnp.sum(extras[:, 0, :shard], axis=0)
    out_gain_ffn = jnp.sum(extras[:, 1, :shard], axis=0)
    out_gain_head = jnp.sum(extras[:, 2, :gh], axis=0)
    out_rate = extras[:, 3, 2]
    tap_rows = extras[:, 4 : 4 + taps]

    def own_taps(at, steps):
        part = jnp.stack(
            [tap_rows[:, :, at + i * HEAD : at + (i + 1) * HEAD] for i in range(steps)], axis=0
        )
        part = jnp.transpose(part, (2, 0, 1, 3)).reshape(taps, steps * width)
        size = steps * shard
        return lax.dynamic_slice_in_dim(part, member * size, size, axis=1)

    return (
        layer_out[None],
        input_grad[None],
        out_gain_in,
        out_query,
        out_key,
        out_value,
        out_beta,
        out_decay,
        out_gatew,
        own_taps(0, 1),
        own_taps(128, 2),
        own_taps(384, 2),
        out_rate,
        out_gain_head,
        out_out,
        out_gain_ffn,
        out_gate,
        out_up,
        out_down,
    )


def solution(mesh):
    rows, lanes = P("fsdp", None), P(None, "fsdp")
    block = P("fsdp", "seq", None)
    return jax.shard_map(
        per_device,
        mesh=mesh,
        in_specs=(
            block, block, rows, P("fsdp"), rows, rows, rows, rows, rows, rows,
            lanes, lanes, lanes, P(), P("fsdp"), rows, P("fsdp"), rows, rows, rows,
        ),
        out_specs=(
            block, block, P("fsdp"), rows, rows, rows, rows, rows, rows,
            lanes, lanes, lanes, P(), P("fsdp"), rows, P("fsdp"), rows, rows, rows,
        ),
        check_vma=False,
    )
```

```python
import functools

import jax
import jax.numpy as jnp
from jax import lax
from jax.experimental import pallas as pl
from jax.experimental.pallas import tpu as pltpu
from jax.sharding import PartitionSpec as P

SPAN = 64
ROWS = 128
HEAD = 128
EPSILON = 1e-06
LOW = jnp.bfloat16
WIDE = jnp.float32
VMEM_LIMIT = 56 * 1024 * 1024


def contract(left, right, left_dim, right_dim):
    return lax.dot_general(
        left, right, (((left_dim,), (right_dim,)), ((), ())), preferred_element_type=WIDE
    )


def halves(value):
    high = value.astype(LOW)
    return high, (value - high.astype(WIDE)).astype(LOW)


def mm(left, right, left_dim=1, right_dim=0):
    return contract(left.astype(LOW), right.astype(LOW), left_dim, right_dim)


def mm3(left, right, left_dim=1, right_dim=0):
    lh, ll = halves(left)
    rh, rl = halves(right)
    return (
        contract(lh, rh, left_dim, right_dim)
        + contract(lh, rl, left_dim, right_dim)
        + contract(ll, rh, left_dim, right_dim)
    )


def stack(*parts):
    return jnp.concatenate(parts, axis=0)


def row_maps():
    row = lax.broadcasted_iota(jnp.int32, (ROWS, ROWS), 0)
    col = lax.broadcasted_iota(jnp.int32, (ROWS, ROWS), 1)
    tok, step = row & (SPAN - 1), row >> 6
    tok_c, step_c = col & (SPAN - 1), col >> 6
    return tok, step, tok_c, step_c


def span_tokens(offs_ref, doc_count, first):
    place = first + lax.broadcasted_iota(jnp.int32, (SPAN, 1), 0)
    begin = jnp.zeros((SPAN, 1), jnp.int32)
    for j in range(doc_count):
        start = offs_ref[0, j]
        begin = jnp.where(place >= start, start, begin)
    return place - begin


def softplus(value):
    return jnp.maximum(value, 0.0) + jnp.log1p(jnp.exp(-jnp.abs(value)))


def decay_sums(small, rate):
    logs = -rate * softplus(small)
    tok = lax.broadcasted_iota(jnp.int32, (SPAN, SPAN), 0)
    tok_c = lax.broadcasted_iota(jnp.int32, (SPAN, SPAN), 1)
    lower = jnp.where(tok >= tok_c, 1.0, 0.0).astype(LOW)
    tok_w = lax.broadcasted_iota(jnp.int32, (SPAN, ROWS), 0)
    tok_wc = lax.broadcasted_iota(jnp.int32, (SPAN, ROWS), 1) & (SPAN - 1)
    upper = jnp.where(tok_w <= tok_wc, 1.0, 0.0).astype(LOW)
    high, rest = halves(logs)
    cols = contract(lower, high, 1, 0) + contract(lower, rest, 1, 0)
    rows = contract(high, upper, 0, 0) + contract(rest, upper, 0, 0)
    return cols[:, 2:3], rows[2:3, :]


def unit(values):
    scale = lax.rsqrt(jnp.sum(values * values, axis=1, keepdims=True) + EPSILON)
    return values * scale, scale


def span_factors(small, rate, pos):
    sig = jax.nn.sigmoid(small)
    cum, cum_row = decay_sums(small, rate)
    beta = stack(sig[:, 0:1], sig[:, 1:2])
    cum2, pos2 = stack(cum, cum), stack(pos, pos)
    tok, step, tok_c, step_c = row_maps()
    before = tok > tok_c
    here = tok == tok_c
    reach = (before | (here & (step >= step_c))) & (tok - tok_c <= pos2)
    decay = jnp.where(reach, jnp.exp(jnp.where(reach, cum2 - cum_row, 0.0)), 0.0)
    strict = before | (here & (step > step_c))
    tok1 = tok[:, 0:1]
    carry = jnp.where(pos2 > tok1, jnp.exp(cum2), 0.0)
    end, end_pos = cum[SPAN - 1 : SPAN], pos[SPAN - 1 : SPAN]
    leave = jnp.where(SPAN - 1 - tok1 <= end_pos, jnp.exp(end - cum2), 0.0)
    carry_all = jnp.where(end_pos >= SPAN, jnp.exp(end), 0.0)
    return beta, decay, strict, carry, leave, carry_all, tok ^ tok_c


def unit_lower_inverse(strict_part, apart):
    row = lax.broadcasted_iota(jnp.int32, (ROWS, ROWS), 0)
    col = lax.broadcasted_iota(jnp.int32, (ROWS, ROWS), 1)
    inverse = jnp.where(row == col, 1.0, 0.0) - jnp.where(apart == 0, strict_part, 0.0)
    for level in range(6):
        block = jnp.where((apart >> level) == 1, strict_part, 0.0)
        inverse = inverse - mm(mm(inverse, block), inverse)
    return inverse


def forward_kernel(
    span_count, doc_count, group,
    offs_ref, rate_ref, pre_ref, gs_ref, edge_ref, taps_ref, gain_ref, state_ref,
    gated_ref, mixed_ref, conv_ref, t_ref, u_ref, sc_ref, qh_ref, a_ref, s_ref, end_ref,
    w_scr, u0_scr, b_scr, o0_scr,
):
    base = offs_ref[0, doc_count]
    rate = rate_ref[0, 0]

    def local(c):
        lo = pl.multiple_of(c * SPAN, SPAN)
        here = pre_ref[pl.ds(lo, SPAN), :].astype(WIDE)
        prior_at = pl.multiple_of(jnp.maximum(lo - 16, 0), 16)
        prior = pre_ref[pl.ds(prior_at, 16), :].astype(WIDE)
        prior = jnp.where(c == 0, edge_ref[...].astype(WIDE), prior)
        rows = stack(prior, here)
        pos = span_tokens(offs_ref, doc_count, base + lo)
        conv = taps_ref[0:1, :] * here
        for lag in range(1, 4):
            shifted = rows[16 - lag : 16 - lag + SPAN]
            conv = conv + jnp.where(pos >= lag, taps_ref[lag : lag + 1, :] * shifted, 0.0)
        conv_ref[pl.ds(lo, SPAN), :] = conv
        act = conv * jax.nn.sigmoid(conv)
        query, _ = unit(act[:, 0:128])
        key0, _ = unit(act[:, 128:256])
        key1, _ = unit(act[:, 256:384])
        keys = stack(key0, key1)
        values = stack(act[:, 384:512], act[:, 512:640])
        small = gs_ref[pl.ds(lo, SPAN), 128:256]
        beta, decay, strict, carry, leave, carry_all, apart = span_factors(small, rate, pos)
        inner = mm(keys, keys, 1, 1)
        inverse = unit_lower_inverse(jnp.where(strict, beta * decay * inner, 0.0), apart)
        t_ref[c] = inverse.astype(LOW)
        both = mm(inverse, jnp.concatenate([(beta * carry) * keys, beta * values], axis=1))
        weight, fresh = both[:, :HEAD], both[:, HEAD:]
        w_scr[c] = weight.astype(LOW)
        u0_scr[c] = fresh
        leaving = (keys * leave).astype(LOW)
        row = lax.broadcasted_iota(jnp.int32, (HEAD, HEAD), 0)
        col = lax.broadcasted_iota(jnp.int32, (HEAD, HEAD), 1)
        a_ref[c] = jnp.where(row == col, carry_all, 0.0) - mm(leaving, weight, 0, 0)
        b_scr[c] = mm(fresh, leaving, 0, 0)
        scores = mm(query, keys, 1, 1) * decay[SPAN:, :]
        sc_ref[c] = scores.astype(LOW)
        mixed_both = mm(scores, both)
        qh_ref[c] = (carry[SPAN:] * query - mixed_both[:, :HEAD]).astype(LOW)
        o0_scr[c] = mixed_both[:, HEAD:]

    def locals_step(i, none):
        for u in range(group):
            local(i * group + u)
        return none

    lax.fori_loop(0, span_count // group, locals_step, 0)

    def chain(c, state):
        s_ref[c] = state
        u_ref[c] = (u0_scr[c] - mm(w_scr[c], state, 1, 1)).astype(LOW)
        mixed = o0_scr[c] + mm(qh_ref[c], state, 1, 1)
        lo = pl.multiple_of(c * SPAN, SPAN)
        mixed_ref[pl.ds(lo, SPAN), :] = mixed
        gate = gs_ref[pl.ds(lo, SPAN), 0:128]
        scale = lax.rsqrt(jnp.mean(mixed * mixed, axis=1, keepdims=True) + EPSILON)
        gated_ref[pl.ds(lo, SPAN), :] = (
            mixed * scale * gain_ref[...] * (gate * jax.nn.sigmoid(gate))
        ).astype(LOW)
        return mm3(state, a_ref[c], 1, 1) + b_scr[c]

    def chain_step(i, state):
        for u in range(group):
            state = chain(i * group + u, state)
        return state

    end_ref[...] = lax.fori_loop(0, span_count // group, chain_step, state_ref[...])


def backward_kernel(
    span_count, doc_count, group,
    offs_ref, rate_ref, pre_ref, gs_ref, edge_ref, taps_ref, gain_ref,
    mixed_ref, conv_ref, t_ref, u_ref, sc_ref, qh_ref, a_ref, s_ref, dgated_ref, dend_ref,
    dy_ref, dtaps_ref, dgain_ref, drate_ref, dedge_ref, dbegin_ref,
    do_scr, f_scr, ds_scr, next_scr,
):
    base = offs_ref[0, doc_count]
    rate = rate_ref[0, 0]
    dgain_ref[...] = jnp.zeros_like(dgain_ref)
    dtaps_ref[...] = jnp.zeros_like(dtaps_ref)
    drate_ref[...] = jnp.zeros_like(drate_ref)
    next_scr[...] = jnp.zeros_like(next_scr)

    def gate_back(c):
        lo = pl.multiple_of(c * SPAN, SPAN)
        mixed = mixed_ref[pl.ds(lo, SPAN), :]
        gate = gs_ref[pl.ds(lo, SPAN), 0:128]
        scale = lax.rsqrt(jnp.mean(mixed * mixed, axis=1, keepdims=True) + EPSILON)
        normed = mixed * scale
        sig = jax.nn.sigmoid(gate)
        grad = dgated_ref[pl.ds(lo, SPAN), :].astype(WIDE)
        by_gain = grad * normed
        dy_ref[pl.ds(lo, SPAN), 640:768] = (
            by_gain * gain_ref[...] * (sig * (1.0 + gate * (1.0 - sig)))
        ).astype(LOW)
        dgain_ref[...] += jnp.sum(by_gain * (gate * sig), axis=0, keepdims=True)
        dn = grad * (gate * sig) * gain_ref[...]
        dmixed = scale * (dn - normed * jnp.mean(dn * normed, axis=1, keepdims=True))
        do_low = dmixed.astype(LOW)
        do_scr[c] = do_low
        f_scr[c] = contract(do_low, qh_ref[c], 0, 0)

    def gate_step(i, none):
        for u in range(group):
            gate_back(i * group + u)
        return none

    lax.fori_loop(0, span_count // group, gate_step, 0)

    def chain_step(i, grad):
        for u in range(group):
            c = span_count - 1 - (i * group + u)
            ds_scr[c] = grad
            grad = mm3(grad, a_ref[c]) + f_scr[c]
        return grad

    dbegin_ref[...] = lax.fori_loop(0, span_count // group, chain_step, dend_ref[...])

    def local(c):
        lo = pl.multiple_of(c * SPAN, SPAN)
        pos = span_tokens(offs_ref, doc_count, base + lo)
        conv = conv_ref[pl.ds(lo, SPAN), :]
        sig = jax.nn.sigmoid(conv)
        act = conv * sig
        query, scale_q = unit(act[:, 0:128])
        key0, scale_0 = unit(act[:, 128:256])
        key1, scale_1 = unit(act[:, 256:384])
        keys = stack(key0, key1)
        values = stack(act[:, 384:512], act[:, 512:640])
        small = gs_ref[pl.ds(lo, SPAN), 128:256]
        beta, decay, strict, carry, leave, carry_all, _ = span_factors(small, rate, pos)
        state, dstate = s_ref[c], ds_scr[c]
        state_l, dstate_l = state.astype(LOW), dstate.astype(LOW)
        upd, out_grad, keys_l = u_ref[c], do_scr[c], keys.astype(LOW)
        dupd = contract(sc_ref[c], out_grad, 0, 0) + mm(keys * leave, dstate_l, 1, 1)
        dtarget = mm(t_ref[c], dupd, 0, 0)
        pair = stack(dtarget.astype(LOW), out_grad)
        by_upd = contract(pair, upd, 1, 1)
        by_state = contract(pair, state_l, 1, 0)
        dinner = jnp.where(strict, -by_upd[:ROWS] * decay, 0.0)
        dscore = by_upd[ROWS:] * decay[SPAN:, :]
        both = stack(dinner, dscore).astype(LOW)
        reading = contract(both, keys_l, 1, 0)
        read_key = reading[:ROWS] - carry * by_state[:ROWS]
        dquery = reading[ROWS:] + carry[SPAN:] * by_state[ROWS:]
        dleave = leave * contract(upd, dstate_l, 1, 0)
        write_key = contract(both, stack(beta * keys, query).astype(LOW), 0, 0) + dleave
        key_read = jnp.sum(keys * read_key, axis=1, keepdims=True)
        dbeta = jnp.sum(dtarget * values, axis=1, keepdims=True) + key_read
        dcum = beta * key_read - jnp.sum(keys * write_key, axis=1, keepdims=True)
        dcum = dcum[:SPAN] + dcum[SPAN:] + jnp.sum(query * dquery, axis=1, keepdims=True)
        through = jnp.sum(keys * dleave, axis=0, keepdims=True) + carry_all * jnp.sum(
            dstate * state, axis=0, keepdims=True
        )
        through = jnp.sum(through, axis=1, keepdims=True)
        tok1 = lax.broadcasted_iota(jnp.int32, (SPAN, 1), 0)
        dcum = dcum + jnp.where(tok1 == SPAN - 1, through, 0.0)
        tok = lax.broadcasted_iota(jnp.int32, (SPAN, SPAN), 0)
        tok_c = lax.broadcasted_iota(jnp.int32, (SPAN, SPAN), 1)
        upper = jnp.where(tok <= tok_c, 1.0, 0.0).astype(LOW)
        high, rest = halves(jnp.broadcast_to(dcum, (SPAN, 128)))
        dlog = contract(upper, high, 1, 0) + contract(upper, rest, 1, 0)
        soft = softplus(small)
        sig_small = jax.nn.sigmoid(small)
        lane = lax.broadcasted_iota(jnp.int32, (SPAN, 128), 1)
        drate_ref[...] += jnp.sum(jnp.where(lane == 2, -dlog * soft, 0.0), axis=0, keepdims=True)
        dsig = jnp.where(lane == 0, dbeta[:SPAN], dbeta[SPAN:]) * sig_small * (1.0 - sig_small)
        dsmall = jnp.where(lane < 2, dsig, jnp.where(lane == 2, -rate * dlog * sig_small, 0.0))
        dy_ref[pl.ds(lo, SPAN), 768:896] = dsmall.astype(LOW)
        dkey = beta * read_key + write_key
        dvalue = beta * dtarget

        def unit_back(grad, normed, scale):
            return scale * (grad - normed * jnp.sum(grad * normed, axis=1, keepdims=True))

        dact = jnp.concatenate(
            [
                unit_back(dquery, query, scale_q),
                unit_back(dkey[:SPAN], key0, scale_0),
                unit_back(dkey[SPAN:], key1, scale_1),
                dvalue[:SPAN],
                dvalue[SPAN:],
            ],
            axis=1,
        )
        dconv = dact * (sig * (1.0 + conv * (1.0 - sig)))
        here = pre_ref[pl.ds(lo, SPAN), :].astype(WIDE)
        prior_at = pl.multiple_of(jnp.maximum(lo - 16, 0), 16)
        prior = pre_ref[pl.ds(prior_at, 16), :].astype(WIDE)
        prior = jnp.where(c == 0, edge_ref[...].astype(WIDE), prior)
        rows = stack(prior, here)
        dpre = taps_ref[0:1, :] * dconv
        dtaps_ref[0:1, :] += jnp.sum(dconv * here, axis=0, keepdims=True)
        for lag in range(1, 4):
            kept = jnp.where(pos >= lag, dconv, 0.0)
            shifted = rows[16 - lag : 16 - lag + SPAN]
            dtaps_ref[lag : lag + 1, :] += jnp.sum(kept * shifted, axis=0, keepdims=True)
            kept = kept * taps_ref[lag : lag + 1, :]
            dpre = dpre + stack(kept, next_scr[lag])[lag : lag + SPAN]
            next_scr[lag] = kept[0:8]
        dy_ref[pl.ds(lo, SPAN), 0:640] = dpre.astype(LOW)

    def local_step(i, none):
        for u in range(group):
            local(span_count - 1 - (i * group + u))
        return none

    lax.fori_loop(0, span_count // group, local_step, 0)

    none = jnp.zeros((16, 640), WIDE)
    dedge = none
    for lag in range(1, 4):
        dedge = dedge + stack(none, next_scr[lag])[lag : lag + 16]
    dedge_ref[...] = dedge


def vmem_spec():
    return pl.BlockSpec(memory_space=pltpu.VMEM)


def smem_spec():
    return pl.BlockSpec(memory_space=pltpu.SMEM)


def run_forward(offs, rate, pre, gs, edge, taps, gain, state):
    tokens = pre.shape[0]
    spans = tokens // SPAN
    shape = jax.ShapeDtypeStruct
    outs = (
        shape((tokens, HEAD), LOW),
        shape((tokens, HEAD), WIDE),
        shape((tokens, 640), WIDE),
        shape((spans, ROWS, ROWS), LOW),
        shape((spans, ROWS, HEAD), LOW),
        shape((spans, SPAN, ROWS), LOW),
        shape((spans, SPAN, HEAD), LOW),
        shape((spans, HEAD, HEAD), WIDE),
        shape((spans, HEAD, HEAD), WIDE),
        shape((HEAD, HEAD), WIDE),
    )
    return pl.pallas_call(
        functools.partial(forward_kernel, spans, offs.shape[1] - 1, 4),
        out_shape=outs,
        in_specs=[smem_spec(), smem_spec()] + [vmem_spec()] * 6,
        out_specs=[vmem_spec()] * len(outs),
        scratch_shapes=[
            pltpu.VMEM((spans, ROWS, HEAD), LOW),
            pltpu.VMEM((spans, ROWS, HEAD), WIDE),
            pltpu.VMEM((spans, HEAD, HEAD), WIDE),
            pltpu.VMEM((spans, SPAN, HEAD), WIDE),
        ],
        compiler_params=pltpu.CompilerParams(vmem_limit_bytes=VMEM_LIMIT),
        cost_estimate=pl.CostEstimate(
            flops=spans * 60 * 2 * 128**3, bytes_accessed=24 * 1024 * 1024, transcendentals=0
        ),
        name="delta_forward",
    )(offs, rate, pre, gs, edge, taps, gain, state)


def run_backward(offs, rate, pre, gs, edge, taps, gain, saved, dgated, dend):
    tokens = pre.shape[0]
    spans = tokens // SPAN
    shape = jax.ShapeDtypeStruct
    outs = (
        shape((tokens, 896), LOW),
        shape((8, 640), WIDE),
        shape((1, HEAD), WIDE),
        shape((1, HEAD), WIDE),
        shape((16, 640), WIDE),
        shape((HEAD, HEAD), WIDE),
    )
    return pl.pallas_call(
        functools.partial(backward_kernel, spans, offs.shape[1] - 1, 2),
        out_shape=outs,
        in_specs=[smem_spec(), smem_spec()] + [vmem_spec()] * 15,
        out_specs=[vmem_spec()] * len(outs),
        scratch_shapes=[
            pltpu.VMEM((spans, SPAN, HEAD), LOW),
            pltpu.VMEM((spans, HEAD, HEAD), WIDE),
            pltpu.VMEM((spans, HEAD, HEAD), WIDE),
            pltpu.VMEM((4, 8, 640), WIDE),
        ],
        compiler_params=pltpu.CompilerParams(vmem_limit_bytes=VMEM_LIMIT),
        cost_estimate=pl.CostEstimate(
            flops=spans * 80 * 2 * 128**3, bytes_accessed=24 * 1024 * 1024, transcendentals=0
        ),
        name="delta_backward",
    )(offs, rate, pre, gs, edge, taps, gain, *saved, dgated, dend)


def rms_parts(values):
    return values * lax.rsqrt(jnp.mean(values * values, axis=-1, keepdims=True) + EPSILON)


def rms_back(grad_scaled, values):
    scale = lax.rsqrt(jnp.mean(values * values, axis=-1, keepdims=True) + EPSILON)
    normed = values * scale
    return scale * (
        grad_scaled - normed * jnp.mean(grad_scaled * normed, axis=-1, keepdims=True)
    )


def dot_plain(left, right, kind=WIDE):
    return jnp.dot(left, right, preferred_element_type=kind)


def dot_left(left, right, kind=WIDE):
    return contract(left, right, 0, 0).astype(kind)


def dot_right(left, right):
    return contract(left, right, 1, 1)


def exchanged(value, axis, bit):
    size = lax.axis_size(axis)
    return lax.ppermute(value, axis, [(i, i ^ bit) for i in range(size)])


def near_order(size):
    order, bit = [0], size // 2
    while bit:
        order = order + [o ^ bit for o in order]
        bit //= 2
    return order


def near_gather(value, axis):
    bit = lax.axis_size(axis) // 2
    while bit:
        value = stack(value, exchanged(value, axis, bit))
        bit //= 2
    return value


def near_scatter(value, axis):
    size, bit = lax.axis_size(axis), 1
    while bit < size:
        half = value.shape[0] // 2
        came = exchanged(value[half:].astype(LOW), axis, bit).astype(WIDE)
        value = value[:half].astype(WIDE) + came
        bit *= 2
    return value


def near_blocks(value, axis):
    size, me = lax.axis_size(axis), lax.axis_index(axis)
    return stack(
        *[lax.dynamic_index_in_dim(value, me ^ o, 0, False) for o in near_order(size)]
    )


def ordered_gather(value, axis):
    bit, me = lax.axis_size(axis) // 2, lax.axis_index(axis)
    value = value[None]
    while bit:
        other = exchanged(value, axis, bit)
        pair = jnp.where(
            (me & bit) == 0, jnp.stack([value, other], 1), jnp.stack([other, value], 1)
        )
        value = pair.reshape((pair.shape[0] * 2,) + value.shape[1:])
        bit //= 2
    return value


def team_step(value, team, move):
    size = lax.axis_size("seq")
    pairs = [(t + i, t + move(i)) for t in range(0, size, team) for i in range(team)]
    return lax.ppermute(value, "seq", pairs)


def spread_gather(value, team):
    me = lax.axis_index("seq") % team
    found = []
    for k in range(team // 2):
        turned = value if k == 0 else team_step(value, team, lambda i: (i + 2 * k) % team)
        across = team_step(turned, team, lambda i: i ^ 1)
        found.append(((me - 2 * k) % team, turned))
        found.append((((me ^ 1) - 2 * k) % team, across))
    return found


def spread_scatter(block, team):
    me = lax.axis_index("seq") % team
    half = team // 2
    total = None
    for k in sorted(range(half), key=lambda k: -min(k, half - k)):
        came = team_step(block(((me ^ 1) + 2 * k) % team), team, lambda i: i ^ 1)
        pair = block((me + 2 * k) % team).astype(WIDE) + came.astype(WIDE)
        if k:
            pair = team_step(pair.astype(LOW), team, lambda i: (i + 2 * k) % team).astype(WIDE)
        total = pair if total is None else total + pair
    return total


def mixer_outputs_kernel(heads, shard, place_ref, *refs):
    got_refs, (q_ref, k_ref, v_ref, g_ref, b_ref, d_ref, x_ref) = refs[:heads], refs[heads:]
    width = heads * HEAD
    lane_b = lax.broadcasted_iota(jnp.int32, (shard, 2 * heads), 1)
    lane_d = lax.broadcasted_iota(jnp.int32, (shard, heads), 1)
    betas = jnp.zeros((shard, 2 * heads), WIDE)
    decays = jnp.zeros((shard, heads), WIDE)
    for n in range(heads):
        got_ref = got_refs[n]
        h = place_ref[0, n]

        def columns(step):
            return pl.ds(pl.multiple_of(step * width + h * HEAD, HEAD), HEAD)

        q_ref[:, columns(0)] = got_ref[:shard, 0:128].astype(WIDE)
        for i in range(2):
            k_ref[:, columns(i)] = got_ref[:shard, 128 + i * 128 : 256 + i * 128].astype(WIDE)
            v_ref[:, columns(i)] = got_ref[:shard, 384 + i * 128 : 512 + i * 128].astype(WIDE)
        g_ref[:, columns(0)] = got_ref[:shard, 640:768].astype(WIDE)
        last = got_ref[:shard, 768:896].astype(WIDE)
        betas = jnp.where(lane_b == h, last[:, 0:1], betas)
        betas = jnp.where(lane_b == heads + h, last[:, 1:2], betas)
        decays = jnp.where(lane_d == h, last[:, 2:3], decays)
        x_ref[h] = got_ref[shard:, :].astype(WIDE)
    b_ref[...] = betas
    d_ref[...] = decays


def mixer_outputs(found, shard):
    heads = len(found)
    places = jnp.stack([place for place, _ in found])[None].astype(jnp.int32)
    rows = found[0][1].shape[0]
    width = heads * HEAD
    shape = jax.ShapeDtypeStruct
    outs = (
        shape((shard, width), WIDE),
        shape((shard, 2 * width), WIDE),
        shape((shard, 2 * width), WIDE),
        shape((shard, width), WIDE),
        shape((shard, 2 * heads), WIDE),
        shape((shard, heads), WIDE),
        shape((heads, rows - shard, 896), WIDE),
    )
    return pl.pallas_call(
        functools.partial(mixer_outputs_kernel, heads, shard),
        out_shape=outs,
        in_specs=[smem_spec()] + [vmem_spec()] * heads,
        out_specs=[vmem_spec()] * len(outs),
        compiler_params=pltpu.CompilerParams(vmem_limit_bytes=VMEM_LIMIT),
        cost_estimate=pl.CostEstimate(flops=0, bytes_accessed=12 * 2**20, transcendentals=0),
        name="mixer_outputs",
    )(places, *(value for _, value in found))


def ff_outputs_kernel(seq, slab, shard, got_ref, gate_ref, up_ref, down_ref):
    pieces = [got_ref[s].astype(WIDE) for s in range(seq)]
    for ref, at in ((gate_ref, 0), (up_ref, slab)):
        columns = [
            p[at : at + slab, k * shard : (k + 1) * shard] for k in range(2) for p in pieces
        ]
        ref[...] = jnp.concatenate(columns, axis=0).T
    down_ref[...] = jnp.concatenate([p[2 * slab :] for p in pieces], axis=0)


def ff_outputs(got, slab, shard, fsdp):
    seq, rows, width = got.shape
    own = seq * slab
    if slab % 8 or (2 * own) % 128 or (2 * shard) % 128 or fsdp % 2:
        wide = got.astype(WIDE)

        def turned(at):
            part = wide[:, at : at + slab].reshape(seq, slab, fsdp, shard)
            return jnp.transpose(part, (3, 2, 0, 1)).reshape(shard, fsdp * own)

        return (
            turned(0),
            turned(slab),
            wide[:, 2 * slab :].reshape(own, width),
        )
    shape = jax.ShapeDtypeStruct
    return pl.pallas_call(
        functools.partial(ff_outputs_kernel, seq, slab, shard),
        out_shape=(
            shape((shard, fsdp * own), WIDE),
            shape((shard, fsdp * own), WIDE),
            shape((own, width), WIDE),
        ),
        grid=(fsdp // 2,),
        in_specs=[pl.BlockSpec((seq, rows, 2 * shard), lambda i: (0, 0, i))],
        out_specs=(
            pl.BlockSpec((shard, 2 * own), lambda i: (0, i)),
            pl.BlockSpec((shard, 2 * own), lambda i: (0, i)),
            pl.BlockSpec((own, 2 * shard), lambda i: (0, i)),
        ),
        compiler_params=pltpu.CompilerParams(vmem_limit_bytes=VMEM_LIMIT),
        cost_estimate=pl.CostEstimate(flops=0, bytes_accessed=15 * 2**20, transcendentals=0),
        name="ff_outputs",
    )(got)


def per_device(
    tokens, cotangent, offsets, gain_in, w_query, w_key, w_value, w_beta, w_decay, w_outgate,
    conv_query, conv_key, conv_value, decay_scale, gain_head, w_out, gain_ffn, w_gate, w_up,
    w_down,
):
    seq, fsdp = lax.axis_size("seq"), lax.axis_size("fsdp")
    heads = decay_scale.shape[0]
    taps = conv_query.shape[0]
    own_rows = tokens.shape[1]
    shard = w_query.shape[0]
    width = shard * fsdp
    teams = seq // heads
    assert teams * heads == seq and width == heads * HEAD
    place = lax.axis_index("seq")
    head, team = place % heads, place // heads
    member = lax.axis_index("fsdp")
    if teams == 1:
        team_groups, head_groups = None, None
    else:
        team_groups = [[t * heads + h for h in range(heads)] for t in range(teams)]
        head_groups = [[t * heads + h for t in range(teams)] for h in range(heads)]

    def gather_rows(value):
        return lax.all_gather(value, "fsdp", axis=0, tiled=True)

    found = spread_gather(tokens[0], heads)
    length = heads * own_rows

    def head_columns(weights, step):
        return lax.dynamic_slice_in_dim(weights, step * width + head * HEAD, HEAD, axis=1)

    small_columns = jnp.concatenate(
        [
            lax.dynamic_slice_in_dim(w_beta, head, 1, axis=1),
            lax.dynamic_slice_in_dim(w_beta, heads + head, 1, axis=1),
            lax.dynamic_slice_in_dim(w_decay, head, 1, axis=1),
            jnp.zeros((shard, HEAD - 3), LOW),
        ],
        axis=1,
    )
    packed = jnp.concatenate(
        [
            head_columns(w_query, 0),
            head_columns(w_key, 0),
            head_columns(w_key, 1),
            head_columns(w_value, 0),
            head_columns(w_value, 1),
            head_columns(w_outgate, 0),
            small_columns,
        ],
        axis=1,
    )

    vectors = jnp.concatenate(
        [
            gain_in[None],
            gain_ffn[None],
            jnp.pad(gain_head, (0, shard - gain_head.shape[0]))[None],
            conv_query,
            conv_key[:, :shard],
            conv_key[:, shard:],
            conv_value[:, :shard],
            conv_value[:, shard:],
        ],
        axis=0,
    )
    extra_rows = 32
    vectors = jnp.pad(vectors, ((0, extra_rows - vectors.shape[0]), (0, 896 - shard)))
    got = ordered_gather(stack(packed, vectors), "fsdp")
    full_packed = got[:, :shard].reshape(width, 896)
    vectors = got[:, shard:, :shard]
    full_gain_in = vectors[:, 0].reshape(width).astype(WIDE)
    full_gain_ffn = vectors[:, 1].reshape(width).astype(WIDE)
    full_gain_head = vectors[:, 2, : gain_head.shape[0]].reshape(1, HEAD).astype(WIDE)

    def full_taps(at, pieces):
        part = vectors[:, at : at + pieces * taps].reshape(fsdp, pieces, taps, shard)
        return jnp.transpose(part, (2, 0, 1, 3)).reshape(taps, fsdp * pieces * shard)

    conv_q = full_taps(3, 1)
    conv_k = full_taps(3 + taps, 2)
    conv_v = full_taps(3 + 3 * taps, 2)
    head_taps = jnp.concatenate(
        [
            head_columns(conv_q, 0),
            head_columns(conv_k, 0),
            head_columns(conv_k, 1),
            head_columns(conv_v, 0),
            head_columns(conv_v, 1),
        ],
        axis=1,
    ).astype(WIDE)
    head_taps = jnp.pad(head_taps, ((0, 8 - taps), (0, 0)))
    full_out = ordered_gather(w_out, "fsdp").reshape(width, width)

    def to_columns(value):
        return lax.all_to_all(value, "fsdp", 1, 0, tiled=True)

    cols_gate, cols_up = to_columns(w_gate), to_columns(w_up)
    group_cot = near_gather(cotangent[0], "fsdp")

    seq_tokens = jnp.zeros((length, width), LOW)
    for at, rows in found:
        seq_tokens = lax.dynamic_update_slice(seq_tokens, rows, (at * own_rows, 0))
    seq_wide = seq_tokens.astype(WIDE)
    normed_low = (rms_parts(seq_wide) * full_gain_in).astype(LOW)
    pre = dot_plain(normed_low, full_packed[:, :640]).astype(LOW)
    gate_small = dot_plain(normed_low, full_packed[:, 640:])
    pre, full_out, cols_gate, cols_up, group_cot = lax.optimization_barrier(
        (pre, full_out, cols_gate, cols_up, group_cot)
    )
    offs = jnp.concatenate(
        [offsets, jnp.broadcast_to(team * length, (1, 1)).astype(jnp.int32)], axis=1
    )
    rate = lax.dynamic_slice_in_dim(decay_scale, head, 1).reshape(1, 1)
    zero_state = jnp.zeros((HEAD, HEAD), WIDE)
    if teams == 1:
        edge = jnp.zeros((16, 640), LOW)
    else:
        forth = [(i, i + heads) for i in range(seq - heads)]
        back = [(i + heads, i) for i in range(seq - heads)]
        edge = lax.ppermute(pre[-16:], "seq", forth)

    def forward_from(state):
        return run_forward(
            offs, rate, pre, gate_small, edge, head_taps, full_gain_head, state
        )

    state_in = zero_state
    if teams > 1:
        trial = forward_from(zero_state)
        steps, end = trial[7], trial[9]

        def along(c, total):
            return jnp.dot(total, steps[c].T, precision=lax.Precision.HIGHEST)

        whole_map = lax.fori_loop(0, steps.shape[0], along, jnp.eye(HEAD, dtype=WIDE))
        for _ in range(teams - 1):
            out = jnp.dot(state_in, whole_map, precision=lax.Precision.HIGHEST) + end
            state_in = lax.ppermute(out.astype(LOW), "seq", forth).astype(WIDE)
    gated, *saved, _ = forward_from(state_in)

    gated_own = lax.all_to_all(
        gated, "seq", 0, 1, tiled=True, axis_index_groups=team_groups
    )
    inputs = tokens[0].astype(WIDE)
    mixer_res = inputs + dot_plain(gated_own, full_out)

    mid_normed = rms_parts(mixer_res)
    mid_low = (mid_normed * full_gain_ffn).astype(LOW)
    group_mid = near_gather(mid_low, "fsdp")
    gate_pre = dot_plain(group_mid, cols_gate)
    up_pre = dot_plain(group_mid, cols_up)
    sig = jax.nn.sigmoid(gate_pre)
    act = gate_pre * sig
    hidden = (act * up_pre).astype(LOW)
    grad_hidden = dot_right(group_cot, w_down)
    grad_gate_pre = (grad_hidden * up_pre * (sig * (1.0 + gate_pre * (1.0 - sig)))).astype(LOW)
    grad_up_pre = (grad_hidden * act).astype(LOW)
    grad_mid = dot_right(grad_gate_pre, cols_gate) + dot_right(grad_up_pre, cols_up)
    grad_mid = near_scatter(grad_mid, "fsdp")
    down_part = near_scatter(dot_plain(hidden, w_down), "fsdp")
    layer_out = (mixer_res + down_part).astype(LOW)

    grad_res = cotangent[0].astype(WIDE) + rms_back(grad_mid * full_gain_ffn, mixer_res)
    grad_gain_ffn = jnp.sum(grad_mid * mid_normed, axis=0)
    res_low = grad_res.astype(LOW)
    grad_gated = dot_right(res_low, full_out).astype(LOW)
    dgated = lax.all_to_all(
        grad_gated, "seq", 1, 0, tiled=True, axis_index_groups=team_groups
    )

    own_ff = w_down.shape[0]
    slab = own_ff // seq
    slabs = jnp.concatenate(
        [
            dot_left(grad_gate_pre, group_mid, LOW).reshape(seq, slab, width),
            dot_left(grad_up_pre, group_mid, LOW).reshape(seq, slab, width),
            dot_left(hidden, group_cot, LOW).reshape(seq, slab, width),
        ],
        axis=1,
    )
    summed = lax.psum_scatter(
        slabs.reshape(seq * 3 * slab, width), "seq", scatter_dimension=0, tiled=True
    )
    turned = lax.all_to_all(summed[: 2 * slab], "fsdp", 1, 1, tiled=True)
    summed = stack(turned, summed[2 * slab :])
    slabs = lax.all_gather(summed, "seq", axis=0)
    out_gate, out_up, out_down = ff_outputs(slabs, slab, shard, fsdp)
    grad_out = dot_left(gated_own, res_low, LOW).reshape(fsdp, shard, width)
    grad_out = near_scatter(near_blocks(grad_out, "fsdp"), "fsdp").astype(LOW)

    def backward_from(dend):
        return run_backward(
            offs, rate, pre, gate_small, edge, head_taps, full_gain_head, saved, dgated, dend
        )

    dend = zero_state
    if teams > 1:
        begin = backward_from(zero_state)[5]
        for _ in range(teams - 1):
            out = lax.dot_general(
                dend, whole_map, (((1,), (1,)), ((), ())), precision=lax.Precision.HIGHEST
            )
            dend = lax.ppermute((out + begin).astype(LOW), "seq", back).astype(WIDE)
    dy, dtaps, dgain, drate, dedge, _ = backward_from(dend)
    if teams > 1:
        from_next = lax.ppermute(dedge.astype(LOW), "seq", back).astype(WIDE)
        tail = (dy[-16:, :640].astype(WIDE) + from_next).astype(LOW)
        dy = lax.dynamic_update_slice(dy, tail, (length - 16, 0))

    grad_packed = dot_left(normed_low, dy)
    grad_gain_in = (
        jnp.sum(grad_packed * full_packed.astype(WIDE), axis=1) / full_gain_in
    )
    out_rows = shard // heads

    def token_block(at):
        rows = lax.dynamic_slice_in_dim(dy, at * own_rows, own_rows, axis=0)
        outs = lax.dynamic_slice_in_dim(grad_out, at * out_rows, out_rows, axis=0)
        return stack(dot_right(rows, full_packed).astype(LOW), outs)

    joined = spread_scatter(token_block, heads)
    grad_normed, own_out = joined[:own_rows], joined[own_rows:].astype(LOW)
    input_grad = (grad_res + rms_back(grad_normed * full_gain_in, inputs)).astype(LOW)
    if teams > 1:
        own_out = lax.psum(own_out, "seq", axis_index_groups=head_groups)
    out_out = lax.all_to_all(
        jnp.broadcast_to(own_out[None], (heads, out_rows, width)), "seq", 0, 0,
        axis_index_groups=team_groups,
    ).reshape(shard, width).astype(WIDE)

    extra = jnp.zeros((fsdp, 16, 896), WIDE)
    extra = extra.at[:, 0, :shard].set(grad_gain_in.reshape(fsdp, shard))
    extra = extra.at[:, 1, :shard].set(grad_gain_ffn.reshape(fsdp, shard))
    gh = gain_head.shape[0]
    extra = extra.at[:, 2, :gh].set(dgain.reshape(fsdp, gh))
    extra = extra.at[:, 3, :HEAD].set(drate)
    extra = extra.at[:, 4 : 4 + taps, :640].set(dtaps[None, :taps])
    combined = jnp.concatenate([grad_packed.reshape(fsdp, shard, 896), extra], axis=1)
    combined = near_scatter(near_blocks(combined.astype(LOW), "fsdp"), "fsdp").astype(LOW)
    if teams > 1:
        combined = lax.psum(combined, "seq", axis_index_groups=head_groups)
    out_query, out_key, out_value, out_gatew, out_beta, out_decay, extras = mixer_outputs(
        spread_gather(combined, heads), shard
    )
    out_gain_in = jnp.sum(extras[:, 0, :shard], axis=0)
    out_gain_ffn = jnp.sum(extras[:, 1, :shard], axis=0)
    out_gain_head = jnp.sum(extras[:, 2, :gh], axis=0)
    out_rate = extras[:, 3, 2]
    tap_rows = extras[:, 4 : 4 + taps]

    def own_taps(at, steps):
        part = jnp.stack(
            [tap_rows[:, :, at + i * HEAD : at + (i + 1) * HEAD] for i in range(steps)], axis=0
        )
        part = jnp.transpose(part, (2, 0, 1, 3)).reshape(taps, steps * width)
        size = steps * shard
        return lax.dynamic_slice_in_dim(part, member * size, size, axis=1)

    return (
        layer_out[None],
        input_grad[None],
        out_gain_in,
        out_query,
        out_key,
        out_value,
        out_beta,
        out_decay,
        out_gatew,
        own_taps(0, 1),
        own_taps(128, 2),
        own_taps(384, 2),
        out_rate,
        out_gain_head,
        out_out,
        out_gain_ffn,
        out_gate,
        out_up,
        out_down,
    )


def solution(mesh):
    rows, lanes = P("fsdp", None), P(None, "fsdp")
    block = P("fsdp", "seq", None)
    return jax.shard_map(
        per_device,
        mesh=mesh,
        in_specs=(
            block, block, rows, P("fsdp"), rows, rows, rows, rows, rows, rows,
            lanes, lanes, lanes, P(), P("fsdp"), rows, P("fsdp"), rows, rows, rows,
        ),
        out_specs=(
            block, block, P("fsdp"), rows, rows, rows, rows, rows, rows,
            lanes, lanes, lanes, P(), P("fsdp"), rows, P("fsdp"), rows, rows, rows,
        ),
        check_vma=False,
    )
```

```python
import functools

import jax
import jax.numpy as jnp
from jax import lax
from jax.experimental import pallas as pl
from jax.experimental.pallas import tpu as pltpu
from jax.sharding import PartitionSpec as P

SPAN = 64
ROWS = 128
HEAD = 128
EPSILON = 1e-06
LOW = jnp.bfloat16
WIDE = jnp.float32
VMEM_LIMIT = 56 * 1024 * 1024


def contract(left, right, left_dim, right_dim):
    return lax.dot_general(
        left, right, (((left_dim,), (right_dim,)), ((), ())), preferred_element_type=WIDE
    )


def halves(value):
    high = value.astype(LOW)
    return high, (value - high.astype(WIDE)).astype(LOW)


def mm(left, right, left_dim=1, right_dim=0):
    return contract(left.astype(LOW), right.astype(LOW), left_dim, right_dim)


def mm3(left, right, left_dim=1, right_dim=0):
    lh, ll = halves(left)
    rh, rl = halves(right)
    return (
        contract(lh, rh, left_dim, right_dim)
        + contract(lh, rl, left_dim, right_dim)
        + contract(ll, rh, left_dim, right_dim)
    )


def stack(*parts):
    return jnp.concatenate(parts, axis=0)


def row_maps():
    row = lax.broadcasted_iota(jnp.int32, (ROWS, ROWS), 0)
    col = lax.broadcasted_iota(jnp.int32, (ROWS, ROWS), 1)
    tok, step = row & (SPAN - 1), row >> 6
    tok_c, step_c = col & (SPAN - 1), col >> 6
    return tok, step, tok_c, step_c


def span_tokens(offs_ref, doc_count, first):
    place = first + lax.broadcasted_iota(jnp.int32, (SPAN, 1), 0)
    begin = jnp.zeros((SPAN, 1), jnp.int32)
    for j in range(doc_count):
        start = offs_ref[0, j]
        begin = jnp.where(place >= start, start, begin)
    return place - begin


def softplus(value):
    return jnp.maximum(value, 0.0) + jnp.log1p(jnp.exp(-jnp.abs(value)))


def decay_sums(small, rate):
    logs = -rate * softplus(small)
    tok = lax.broadcasted_iota(jnp.int32, (SPAN, SPAN), 0)
    tok_c = lax.broadcasted_iota(jnp.int32, (SPAN, SPAN), 1)
    lower = jnp.where(tok >= tok_c, 1.0, 0.0).astype(LOW)
    tok_w = lax.broadcasted_iota(jnp.int32, (SPAN, ROWS), 0)
    tok_wc = lax.broadcasted_iota(jnp.int32, (SPAN, ROWS), 1) & (SPAN - 1)
    upper = jnp.where(tok_w <= tok_wc, 1.0, 0.0).astype(LOW)
    high, rest = halves(logs)
    cols = contract(lower, high, 1, 0) + contract(lower, rest, 1, 0)
    rows = contract(high, upper, 0, 0) + contract(rest, upper, 0, 0)
    return cols[:, 2:3], rows[2:3, :]


def unit(values):
    scale = lax.rsqrt(jnp.sum(values * values, axis=1, keepdims=True) + EPSILON)
    return values * scale, scale


def span_factors(small, rate, pos):
    sig = jax.nn.sigmoid(small)
    cum, cum_row = decay_sums(small, rate)
    beta = stack(sig[:, 0:1], sig[:, 1:2])
    cum2, pos2 = stack(cum, cum), stack(pos, pos)
    tok, step, tok_c, step_c = row_maps()
    before = tok > tok_c
    here = tok == tok_c
    reach = (before | (here & (step >= step_c))) & (tok - tok_c <= pos2)
    decay = jnp.where(reach, jnp.exp(jnp.where(reach, cum2 - cum_row, 0.0)), 0.0)
    strict = before | (here & (step > step_c))
    tok1 = tok[:, 0:1]
    carry = jnp.where(pos2 > tok1, jnp.exp(cum2), 0.0)
    end, end_pos = cum[SPAN - 1 : SPAN], pos[SPAN - 1 : SPAN]
    leave = jnp.where(SPAN - 1 - tok1 <= end_pos, jnp.exp(end - cum2), 0.0)
    carry_all = jnp.where(end_pos >= SPAN, jnp.exp(end), 0.0)
    return beta, decay, strict, carry, leave, carry_all, tok ^ tok_c


def unit_lower_inverse(strict_part, apart):
    row = lax.broadcasted_iota(jnp.int32, (ROWS, ROWS), 0)
    col = lax.broadcasted_iota(jnp.int32, (ROWS, ROWS), 1)
    inverse = jnp.where(row == col, 1.0, 0.0) - jnp.where(apart == 0, strict_part, 0.0)
    for level in range(6):
        block = jnp.where((apart >> level) == 1, strict_part, 0.0)
        inverse = inverse - mm(mm(inverse, block), inverse)
    return inverse


def conv_rows(prior, here):
    return stack(prior.astype(WIDE), here.astype(WIDE))


def forward_kernel(
    span_count, doc_count, group,
    offs_ref, rate_ref, pre_ref, prior_ref, small_ref, gate_ref, edge_ref, taps_ref, gain_ref,
    state_ref,
    conv_ref, t_ref, sc_ref, qh_ref, a_ref, gated_ref, mixed_ref, u_ref, s_ref, end_ref,
    w_scr, u0_scr, b_scr, o0_scr, a_scr, qh_scr,
):
    step = pl.program_id(0)
    base = offs_ref[0, doc_count]
    rate = rate_ref[0, 0]
    prior = jnp.where(step == 0, edge_ref[...].astype(WIDE), prior_ref[...].astype(WIDE))

    for u in range(group):
        c = step * group + u
        here = pre_ref[u * SPAN : (u + 1) * SPAN, :].astype(WIDE)
        if u:
            prior = pre_ref[u * SPAN - 16 : u * SPAN, :].astype(WIDE)
        rows = stack(prior, here)
        pos = span_tokens(offs_ref, doc_count, base + c * SPAN)
        conv = taps_ref[0:1, :] * here
        for lag in range(1, 4):
            shifted = rows[16 - lag : 16 - lag + SPAN]
            conv = conv + jnp.where(pos >= lag, taps_ref[lag : lag + 1, :] * shifted, 0.0)
        conv_ref[u * SPAN : (u + 1) * SPAN, :] = conv
        act = conv * jax.nn.sigmoid(conv)
        query, _ = unit(act[:, 0:128])
        key0, _ = unit(act[:, 128:256])
        key1, _ = unit(act[:, 256:384])
        keys = stack(key0, key1)
        values = stack(act[:, 384:512], act[:, 512:640])
        small = small_ref[u * SPAN : (u + 1) * SPAN, :]
        beta, decay, strict, carry, leave, carry_all, apart = span_factors(small, rate, pos)
        inner = mm(keys, keys, 1, 1)
        inverse = unit_lower_inverse(jnp.where(strict, beta * decay * inner, 0.0), apart)
        t_ref[u] = inverse.astype(LOW)
        both = mm(inverse, jnp.concatenate([(beta * carry) * keys, beta * values], axis=1))
        weight, fresh = both[:, :HEAD], both[:, HEAD:]
        w_scr[c] = weight.astype(LOW)
        u0_scr[c] = fresh
        leaving = (keys * leave).astype(LOW)
        row = lax.broadcasted_iota(jnp.int32, (HEAD, HEAD), 0)
        col = lax.broadcasted_iota(jnp.int32, (HEAD, HEAD), 1)
        step_map = jnp.where(row == col, carry_all, 0.0) - mm(leaving, weight, 0, 0)
        a_ref[u] = step_map
        a_scr[c] = step_map
        b_scr[c] = mm(fresh, leaving, 0, 0)
        scores = mm(query, keys, 1, 1) * decay[SPAN:, :]
        sc_ref[u] = scores.astype(LOW)
        mixed_both = mm(scores, both)
        reach = (carry[SPAN:] * query - mixed_both[:, :HEAD]).astype(LOW)
        qh_ref[u] = reach
        qh_scr[c] = reach
        o0_scr[c] = mixed_both[:, HEAD:]

    def chain(c, state):
        s_ref[c] = state
        low = state.astype(LOW)
        u_ref[c] = (u0_scr[c] - contract(w_scr[c], low, 1, 1)).astype(LOW)
        mixed = o0_scr[c] + contract(qh_scr[c], low, 1, 1)
        lo = pl.multiple_of(c * SPAN, SPAN)
        mixed_ref[pl.ds(lo, SPAN), :] = mixed
        gate = gate_ref[pl.ds(lo, SPAN), :]
        scale = lax.rsqrt(jnp.mean(mixed * mixed, axis=1, keepdims=True) + EPSILON)
        gated_ref[pl.ds(lo, SPAN), :] = (
            mixed * scale * gain_ref[...] * (gate * jax.nn.sigmoid(gate))
        ).astype(LOW)
        return mm3(state, a_scr[c], 1, 1) + b_scr[c]

    def chain_step(i, state):
        for u in range(4):
            state = chain(i * 4 + u, state)
        return state

    @pl.when(step == pl.num_programs(0) - 1)
    def _():
        end_ref[...] = lax.fori_loop(0, span_count // 4, chain_step, state_ref[...])


def gate_back_kernel(
    span_count,
    gate_ref, gain_ref, mixed_ref, qh_ref, a_ref, dgated_ref, dend_ref,
    do_ref, ds_ref, dgate_ref, dgain_ref, dbegin_ref,
    f_scr,
):
    dgain_ref[...] = jnp.zeros_like(dgain_ref)

    def gate_back(c):
        lo = pl.multiple_of(c * SPAN, SPAN)
        mixed = mixed_ref[pl.ds(lo, SPAN), :]
        gate = gate_ref[pl.ds(lo, SPAN), :]
        scale = lax.rsqrt(jnp.mean(mixed * mixed, axis=1, keepdims=True) + EPSILON)
        normed = mixed * scale
        sig = jax.nn.sigmoid(gate)
        grad = dgated_ref[pl.ds(lo, SPAN), :].astype(WIDE)
        by_gain = grad * normed
        dgate_ref[pl.ds(lo, SPAN), :] = (
            by_gain * gain_ref[...] * (sig * (1.0 + gate * (1.0 - sig)))
        ).astype(LOW)
        dgain_ref[...] += jnp.sum(by_gain * (gate * sig), axis=0, keepdims=True)
        dn = grad * (gate * sig) * gain_ref[...]
        dmixed = scale * (dn - normed * jnp.mean(dn * normed, axis=1, keepdims=True))
        do_low = dmixed.astype(LOW)
        do_ref[c] = do_low
        f_scr[c] = contract(do_low, qh_ref[c], 0, 0)

    def gate_step(i, none):
        for u in range(4):
            gate_back(i * 4 + u)
        return none

    lax.fori_loop(0, span_count // 4, gate_step, 0)

    def chain_step(i, grad):
        for u in range(4):
            c = span_count - 1 - (i * 4 + u)
            ds_ref[c] = grad
            grad = mm3(grad, a_ref[c]) + f_scr[c]
        return grad

    dbegin_ref[...] = lax.fori_loop(0, span_count // 4, chain_step, dend_ref[...])


def backward_kernel(
    at_block, doc_count,
    offs_ref, rate_ref, pre_ref, prior_ref, small_ref, edge_ref, taps_ref,
    conv_ref, t_ref, u_ref, sc_ref, s_ref, do_ref, ds_ref, dgate_ref,
    next_in, dtaps_in, drate_in, *refs,
):
    dy_ref, next_ref, dtaps_ref, drate_ref = refs[-4:]
    block = at_block(pl.program_id(0))
    base = offs_ref[0, doc_count]
    rate = rate_ref[0, 0]

    @pl.when(pl.program_id(0) == 0)
    def _():
        next_ref[...] = next_in[...]
        dtaps_ref[...] = dtaps_in[...]
        drate_ref[...] = drate_in[...]

    dy_ref[:, 640:768] = dgate_ref[...]
    for n in (1, 0):
        lo, hi = n * SPAN, (n + 1) * SPAN
        pos = span_tokens(offs_ref, doc_count, base + block * 2 * SPAN + lo)
        conv = conv_ref[lo:hi, :]
        sig = jax.nn.sigmoid(conv)
        act = conv * sig
        query, scale_q = unit(act[:, 0:128])
        key0, scale_0 = unit(act[:, 128:256])
        key1, scale_1 = unit(act[:, 256:384])
        keys = stack(key0, key1)
        values = stack(act[:, 384:512], act[:, 512:640])
        small = small_ref[lo:hi, :]
        beta, decay, strict, carry, leave, carry_all, _ = span_factors(small, rate, pos)
        state, dstate = s_ref[n], ds_ref[n]
        state_l, dstate_l = state.astype(LOW), dstate.astype(LOW)
        upd, out_grad, keys_l = u_ref[n], do_ref[n], keys.astype(LOW)
        dupd = contract(sc_ref[n], out_grad, 0, 0) + mm(keys * leave, dstate_l, 1, 1)
        dtarget = mm(t_ref[n], dupd, 0, 0)
        pair = stack(dtarget.astype(LOW), out_grad)
        by_upd = contract(pair, upd, 1, 1)
        by_state = contract(pair, state_l, 1, 0)
        dinner = jnp.where(strict, -by_upd[:ROWS] * decay, 0.0)
        dscore = by_upd[ROWS:] * decay[SPAN:, :]
        both = stack(dinner, dscore).astype(LOW)
        reading = contract(both, keys_l, 1, 0)
        read_key = reading[:ROWS] - carry * by_state[:ROWS]
        dquery = reading[ROWS:] + carry[SPAN:] * by_state[ROWS:]
        dleave = leave * contract(upd, dstate_l, 1, 0)
        write_key = contract(both, stack(beta * keys, query).astype(LOW), 0, 0) + dleave
        key_read = jnp.sum(keys * read_key, axis=1, keepdims=True)
        dbeta = jnp.sum(dtarget * values, axis=1, keepdims=True) + key_read
        dcum = beta * key_read - jnp.sum(keys * write_key, axis=1, keepdims=True)
        dcum = dcum[:SPAN] + dcum[SPAN:] + jnp.sum(query * dquery, axis=1, keepdims=True)
        through = jnp.sum(keys * dleave, axis=0, keepdims=True) + carry_all * jnp.sum(
            dstate * state, axis=0, keepdims=True
        )
        through = jnp.sum(through, axis=1, keepdims=True)
        tok1 = lax.broadcasted_iota(jnp.int32, (SPAN, 1), 0)
        dcum = dcum + jnp.where(tok1 == SPAN - 1, through, 0.0)
        tok = lax.broadcasted_iota(jnp.int32, (SPAN, SPAN), 0)
        tok_c = lax.broadcasted_iota(jnp.int32, (SPAN, SPAN), 1)
        upper = jnp.where(tok <= tok_c, 1.0, 0.0).astype(LOW)
        high, rest = halves(jnp.broadcast_to(dcum, (SPAN, 128)))
        dlog = contract(upper, high, 1, 0) + contract(upper, rest, 1, 0)
        soft = softplus(small)
        sig_small = jax.nn.sigmoid(small)
        lane = lax.broadcasted_iota(jnp.int32, (SPAN, 128), 1)
        drate_ref[...] += jnp.sum(jnp.where(lane == 2, -dlog * soft, 0.0), axis=0, keepdims=True)
        dsig = jnp.where(lane == 0, dbeta[:SPAN], dbeta[SPAN:]) * sig_small * (1.0 - sig_small)
        dsmall = jnp.where(lane < 2, dsig, jnp.where(lane == 2, -rate * dlog * sig_small, 0.0))
        dy_ref[lo:hi, 768:896] = dsmall.astype(LOW)
        dkey = beta * read_key + write_key
        dvalue = beta * dtarget

        def unit_back(grad, normed, scale):
            return scale * (grad - normed * jnp.sum(grad * normed, axis=1, keepdims=True))

        dact = jnp.concatenate(
            [
                unit_back(dquery, query, scale_q),
                unit_back(dkey[:SPAN], key0, scale_0),
                unit_back(dkey[SPAN:], key1, scale_1),
                dvalue[:SPAN],
                dvalue[SPAN:],
            ],
            axis=1,
        )
        dconv = dact * (sig * (1.0 + conv * (1.0 - sig)))
        here = pre_ref[lo:hi, :].astype(WIDE)
        if n:
            prior = pre_ref[lo - 16 : lo, :].astype(WIDE)
        else:
            prior = jnp.where(
                block == 0, edge_ref[...].astype(WIDE), prior_ref[...].astype(WIDE)
            )
        rows = stack(prior, here)
        dpre = taps_ref[0:1, :] * dconv
        dtaps_ref[0:1, :] += jnp.sum(dconv * here, axis=0, keepdims=True)
        for lag in range(1, 4):
            kept = jnp.where(pos >= lag, dconv, 0.0)
            shifted = rows[16 - lag : 16 - lag + SPAN]
            dtaps_ref[lag : lag + 1, :] += jnp.sum(kept * shifted, axis=0, keepdims=True)
            kept = kept * taps_ref[lag : lag + 1, :]
            dpre = dpre + stack(kept, next_ref[lag])[lag : lag + SPAN]
            next_ref[lag] = kept[0:8]
        dy_ref[lo:hi, 0:640] = dpre.astype(LOW)


def vmem_spec():
    return pl.BlockSpec(memory_space=pltpu.VMEM)


def smem_spec():
    return pl.BlockSpec(memory_space=pltpu.SMEM)


def fixed(shape):
    return pl.BlockSpec(shape, lambda *_: (0,) * len(shape))


def estimate(flops, mib):
    return pl.CostEstimate(flops=int(flops), bytes_accessed=int(mib * 2**20), transcendentals=0)


def run_forward(offs, rate, pre, gs, edge, taps, gain, state):
    tokens = pre.shape[0]
    spans = tokens // SPAN
    group = 4
    shape = jax.ShapeDtypeStruct
    outs = (
        (shape((tokens, 640), WIDE), pl.BlockSpec((group * SPAN, 640), lambda i: (i, 0))),
        (shape((spans, ROWS, ROWS), LOW), pl.BlockSpec((group, ROWS, ROWS), lambda i: (i, 0, 0))),
        (shape((spans, SPAN, ROWS), LOW), pl.BlockSpec((group, SPAN, ROWS), lambda i: (i, 0, 0))),
        (shape((spans, SPAN, HEAD), LOW), pl.BlockSpec((group, SPAN, HEAD), lambda i: (i, 0, 0))),
        (shape((spans, HEAD, HEAD), WIDE), pl.BlockSpec((group, HEAD, HEAD), lambda i: (i, 0, 0))),
        (shape((tokens, HEAD), LOW), fixed((tokens, HEAD))),
        (shape((tokens, HEAD), WIDE), fixed((tokens, HEAD))),
        (shape((spans, ROWS, HEAD), LOW), fixed((spans, ROWS, HEAD))),
        (shape((spans, HEAD, HEAD), WIDE), fixed((spans, HEAD, HEAD))),
        (shape((HEAD, HEAD), WIDE), fixed((HEAD, HEAD))),
    )
    return pl.pallas_call(
        functools.partial(forward_kernel, spans, offs.shape[1] - 1, group),
        out_shape=[o for o, _ in outs],
        grid=(spans // group,),
        in_specs=[
            smem_spec(),
            smem_spec(),
            pl.BlockSpec((group * SPAN, 640), lambda i: (i, 0)),
            pl.BlockSpec((16, 640), lambda i: (jnp.maximum(i * (group * SPAN // 16) - 1, 0), 0)),
            pl.BlockSpec((group * SPAN, HEAD), lambda i: (i, 1)),
            fixed((tokens, HEAD)),
            fixed((16, 640)),
            fixed((8, 640)),
            fixed((1, HEAD)),
            fixed((HEAD, HEAD)),
        ],
        out_specs=[b for _, b in outs],
        scratch_shapes=[
            pltpu.VMEM((spans, ROWS, HEAD), LOW),
            pltpu.VMEM((spans, ROWS, HEAD), WIDE),
            pltpu.VMEM((spans, HEAD, HEAD), WIDE),
            pltpu.VMEM((spans, SPAN, HEAD), WIDE),
            pltpu.VMEM((spans, HEAD, HEAD), WIDE),
            pltpu.VMEM((spans, SPAN, HEAD), LOW),
        ],
        compiler_params=pltpu.CompilerParams(vmem_limit_bytes=VMEM_LIMIT),
        cost_estimate=estimate(70e9, 24),
        name="delta_forward",
    )(offs, rate, pre, pre, gs, gs, edge, taps, gain, state)


def run_gate_back(gs, gain, mixed, qh, steps, dgated, dend):
    tokens = mixed.shape[0]
    spans = tokens // SPAN
    shape = jax.ShapeDtypeStruct
    return pl.pallas_call(
        functools.partial(gate_back_kernel, spans),
        out_shape=(
            shape((spans, SPAN, HEAD), LOW),
            shape((spans, HEAD, HEAD), WIDE),
            shape((tokens, HEAD), LOW),
            shape((1, HEAD), WIDE),
            shape((HEAD, HEAD), WIDE),
        ),
        grid=(1,),
        in_specs=[
            fixed((tokens, HEAD)),
            fixed((1, HEAD)),
            fixed((tokens, HEAD)),
            fixed((spans, SPAN, HEAD)),
            fixed((spans, HEAD, HEAD)),
            fixed((tokens, HEAD)),
            fixed((HEAD, HEAD)),
        ],
        out_specs=(
            fixed((spans, SPAN, HEAD)),
            fixed((spans, HEAD, HEAD)),
            fixed((tokens, HEAD)),
            fixed((1, HEAD)),
            fixed((HEAD, HEAD)),
        ),
        scratch_shapes=[pltpu.VMEM((spans, HEAD, HEAD), WIDE)],
        compiler_params=pltpu.CompilerParams(vmem_limit_bytes=VMEM_LIMIT),
        cost_estimate=estimate(15e9, 8),
        name="delta_gate_back",
    )(gs, gain, mixed, qh, steps, dgated, dend)


def run_backward(last, steps, offs, rate, pre, gs, edge, taps, saved, carried, dy):
    conv, inverse, upd, scores, states, do, ds, dgate = saved
    tokens = pre.shape[0]

    def at(i):
        return last - i

    def rows(columns, lane=0):
        return pl.BlockSpec((2 * SPAN, columns), lambda i: (at(i), lane))

    def spans(a, b):
        return pl.BlockSpec((2, a, b), lambda i: (at(i), 0, 0))

    shape = jax.ShapeDtypeStruct
    carried_specs = [fixed((4, 8, 640)), fixed((8, 640)), fixed((1, HEAD))]
    operands = [offs, rate, pre, pre, gs, edge, taps, conv, inverse, upd, scores, states, do, ds]
    operands += [dgate, *carried]
    in_specs = [
        smem_spec(),
        smem_spec(),
        rows(640),
        pl.BlockSpec((16, 640), lambda i: (jnp.maximum(at(i) * (2 * SPAN // 16) - 1, 0), 0)),
        rows(HEAD, 1),
        fixed((16, 640)),
        fixed((8, 640)),
        rows(640),
        spans(ROWS, ROWS),
        spans(ROWS, HEAD),
        spans(SPAN, ROWS),
        spans(HEAD, HEAD),
        spans(SPAN, HEAD),
        spans(HEAD, HEAD),
        rows(HEAD),
        *carried_specs,
    ]
    aliases = {}
    if dy is not None:
        aliases = {len(operands): 0}
        operands.append(dy)
        in_specs.append(pl.BlockSpec(memory_space=pl.ANY))
    dy, *carried = pl.pallas_call(
        functools.partial(backward_kernel, at, offs.shape[1] - 1),
        out_shape=(
            shape((tokens, 896), LOW),
            shape((4, 8, 640), WIDE),
            shape((8, 640), WIDE),
            shape((1, HEAD), WIDE),
        ),
        grid=(steps,),
        in_specs=in_specs,
        out_specs=(rows(896), *carried_specs),
        input_output_aliases=aliases,
        compiler_params=pltpu.CompilerParams(vmem_limit_bytes=VMEM_LIMIT),
        cost_estimate=estimate(4e9 * steps, 1.3 * steps),
        name="delta_backward",
    )(*operands)
    return dy, carried


def input_blocks_kernel(at_ref, dy_ref, out_ref, w_ref, send_ref, keep_ref):
    count = dy_ref.shape[0]
    block = contract(dy_ref[...], w_ref[...], 1, 1).astype(LOW)
    for n, to_ref in enumerate((send_ref, keep_ref)):

        @pl.when(pl.program_id(0) == n)
        def _():
            to_ref[:count, :] = block
            to_ref[count:, :] = out_ref[...]


def input_blocks(places, dy, grad_out, weights, count, out_rows):
    width = weights.shape[0]
    return pl.pallas_call(
        input_blocks_kernel,
        out_shape=[jax.ShapeDtypeStruct((count + out_rows, width), LOW)] * 2,
        grid_spec=pltpu.PrefetchScalarGridSpec(
            num_scalar_prefetch=1,
            grid=(2,),
            in_specs=[
                pl.BlockSpec((count, 896), lambda i, p: (p[i], 0)),
                pl.BlockSpec((out_rows, width), lambda i, p: (p[i], 0)),
                fixed(weights.shape),
            ],
            out_specs=[fixed((count + out_rows, width))] * 2,
        ),
        compiler_params=pltpu.CompilerParams(vmem_limit_bytes=VMEM_LIMIT),
        cost_estimate=estimate(4 * count * width * 896, 4),
        name="input_blocks",
    )(jnp.stack(places).astype(jnp.int32), dy, grad_out, weights)


def pack_kernel(
    heads, taps,
    place_ref, q_ref, k0_ref, k1_ref, v0_ref, v1_ref, g_ref, beta_ref, decay_ref, gin_ref,
    gff_ref, gh_ref, cq_ref, ck_ref, cv_ref, out_ref,
):
    h = place_ref[0]
    shard = q_ref.shape[0]
    for i, ref in enumerate((q_ref, k0_ref, k1_ref, v0_ref, v1_ref, g_ref)):
        out_ref[:shard, i * HEAD : (i + 1) * HEAD] = ref[...]
    beta, decay = beta_ref[...].astype(WIDE), decay_ref[...].astype(WIDE)

    def row_of(values, at):
        row = lax.broadcasted_iota(jnp.int32, values.shape, 0)
        return jnp.sum(jnp.where(row == at, values, 0.0), axis=0, keepdims=True)

    row = lax.broadcasted_iota(jnp.int32, (HEAD, shard), 0)
    small = jnp.where(row == 0, row_of(beta, h), 0.0)
    small = jnp.where(row == 1, row_of(beta, heads + h), small)
    small = jnp.where(row == 2, row_of(decay, h), small)
    out_ref[:shard, 6 * HEAD :] = small.T.astype(LOW)
    out_ref[shard:, :] = jnp.zeros((out_ref.shape[0] - shard, out_ref.shape[1]), LOW)
    vectors = stack(
        *[ref[...].astype(WIDE) for ref in (gin_ref, gff_ref, gh_ref, cq_ref)],
        *[
            ref[:, i * shard : (i + 1) * shard].astype(WIDE)
            for ref in (ck_ref, cv_ref)
            for i in range(2)
        ],
        jnp.zeros((32 - 3 - 5 * taps, shard), WIDE),
    )
    out_ref[shard:, :shard] = vectors.astype(LOW)


def pack_weights(
    head, w_query, w_key, w_value, w_outgate, w_beta, w_decay, gain_in, gain_ffn, gain_head,
    conv_query, conv_key, conv_value,
):
    shard, heads = w_decay.shape
    taps = conv_query.shape[0]

    def part(step):
        return pl.BlockSpec((shard, HEAD), lambda i, h: (0, step * heads + h[0]))

    small = (
        w_beta.T, w_decay.T, gain_in[None], gain_ffn[None],
        jnp.pad(gain_head, (0, shard - gain_head.shape[0]))[None],
        conv_query, conv_key, conv_value,
    )
    return pl.pallas_call(
        functools.partial(pack_kernel, heads, taps),
        out_shape=jax.ShapeDtypeStruct((shard + 32, 896), LOW),
        grid_spec=pltpu.PrefetchScalarGridSpec(
            num_scalar_prefetch=1,
            grid=(1,),
            in_specs=[part(0), part(0), part(1), part(0), part(1), part(0)]
            + [fixed(a.shape) for a in small],
            out_specs=fixed((shard + 32, 896)),
        ),
        compiler_params=pltpu.CompilerParams(vmem_limit_bytes=VMEM_LIMIT),
        cost_estimate=estimate(0, 2),
        name="pack_weights",
    )(head.reshape(1), w_query, w_key, w_key, w_value, w_value, w_outgate, *small)


def project_kernel(place_ref, tok_ref, other_ref, gain_ref, w_ref, *refs):
    low_ref, pre_ref, gs_ref = refs[-3:]
    values = jnp.where(pl.program_id(0) == 0, tok_ref[...], other_ref[...]).astype(WIDE)
    scale = lax.rsqrt(jnp.mean(values * values, axis=1, keepdims=True) + EPSILON)
    normed = (values * scale * gain_ref[...]).astype(LOW)
    low_ref[...] = normed
    pre_ref[...] = contract(normed, w_ref[:, :640], 1, 0).astype(LOW)
    gs_ref[...] = contract(normed, w_ref[:, 640:], 1, 0)


def project(places, rows, other, gain, weights, length, filled):
    count, width = rows.shape
    shape = jax.ShapeDtypeStruct
    operands = [places, rows, other, gain, weights]
    in_specs = [fixed(a.shape) for a in operands[1:]]
    aliases = {}
    if filled is not None:
        aliases = {len(operands) + i: i for i in range(3)}
        operands += filled
        in_specs += [pl.BlockSpec(memory_space=pl.ANY)] * 3
    return pl.pallas_call(
        project_kernel,
        out_shape=[shape((length, n), t) for n, t in ((width, LOW), (640, LOW), (256, WIDE))],
        grid_spec=pltpu.PrefetchScalarGridSpec(
            num_scalar_prefetch=1,
            grid=(2,),
            in_specs=in_specs,
            out_specs=[
                pl.BlockSpec((count, n), lambda i, p: (p[i], 0)) for n in (width, 640, 256)
            ],
        ),
        input_output_aliases=aliases,
        compiler_params=pltpu.CompilerParams(vmem_limit_bytes=VMEM_LIMIT),
        cost_estimate=estimate(4 * count * width * 896, 6),
        name="project",
    )(*operands)


def rms_parts(values):
    return values * lax.rsqrt(jnp.mean(values * values, axis=-1, keepdims=True) + EPSILON)


def rms_back(grad_scaled, values):
    scale = lax.rsqrt(jnp.mean(values * values, axis=-1, keepdims=True) + EPSILON)
    normed = values * scale
    return scale * (
        grad_scaled - normed * jnp.mean(grad_scaled * normed, axis=-1, keepdims=True)
    )


def dot_plain(left, right, kind=WIDE):
    return jnp.dot(left, right, preferred_element_type=kind)


def dot_left(left, right, kind=WIDE):
    return contract(left, right, 0, 0).astype(kind)


def dot_right(left, right):
    return contract(left, right, 1, 1)


def exchanged(value, axis, bit):
    size = lax.axis_size(axis)
    return lax.ppermute(value, axis, [(i, i ^ bit) for i in range(size)])


def near_order(size):
    order, bit = [0], size // 2
    while bit:
        order = order + [o ^ bit for o in order]
        bit //= 2
    return order


def near_gather(value, axis, first=None):
    bit = lax.axis_size(axis) // 2
    while bit:
        value = stack(value, exchanged(value, axis, bit) if first is None else first)
        first = None
        bit //= 2
    return value


def near_scatter(value, axis):
    size, bit = lax.axis_size(axis), 1
    while bit < size:
        half = value.shape[0] // 2
        came = exchanged(value[half:].astype(LOW), axis, bit).astype(WIDE)
        value = value[:half].astype(WIDE) + came
        bit *= 2
    return value


def near_blocks(value, axis):
    size, me = lax.axis_size(axis), lax.axis_index(axis)
    return stack(
        *[lax.dynamic_index_in_dim(value, me ^ o, 0, False) for o in near_order(size)]
    )


def ordered_step(value, other, axis, bit):
    mine_first = (lax.axis_index(axis) & bit) == 0
    pair = jnp.where(mine_first, jnp.stack([value, other], 1), jnp.stack([other, value], 1))
    return pair.reshape((pair.shape[0] * 2,) + value.shape[1:])


def ordered_gather(value, axis, first=None):
    bit = lax.axis_size(axis) // 2
    value = value[None]
    while bit:
        other = exchanged(value, axis, bit) if first is None else first[None]
        value = ordered_step(value, other, axis, bit)
        first = None
        bit //= 2
    return value


def far_exchange(value, axis):
    return exchanged(value, axis, lax.axis_size(axis) // 2)


def after(value, *done):
    return lax.optimization_barrier((value, *done))[0]


def team_step(value, team, move):
    size = lax.axis_size("seq")
    pairs = [(t + i, t + move(i)) for t in range(0, size, team) for i in range(team)]
    return lax.ppermute(value, "seq", pairs)


def turn(value, team, by):
    return team_step(value, team, lambda i: (i + 2 * by) % team)


def cross(value, team):
    return team_step(value, team, lambda i: i ^ 1)


def turns(team):
    half = team // 2
    return [0] + [k for n in range(1, half // 2 + 1) for k in dict.fromkeys((n, half - n))]


def gather_stages(value, team, ties=()):
    me = lax.axis_index("seq") % team
    half = team // 2
    turned, found, before = {0: value}, [], ()
    if half > 1:
        turned[1] = turn(value, team, 1)
    if half > 2:
        turned[half - 1] = turn(value, team, -1)
    for k in turns(team):
        across = cross(after(turned[k], *before, *ties), team)
        stage = [across]
        for n in (k + 1, k - 1):
            if 0 < n < half and n not in turned and k:
                turned[n] = turn(turned[k], team, 1 if n > k else -1)
                stage.append(turned[n])
        before = (across,)
        found.append(((me - 2 * k) % team, turned[k], ((me ^ 1) - 2 * k) % team, across))
        yield stage
    yield found


def last_of(stages):
    for stage in stages:
        pass
    return stage


def team_places(team):
    me = lax.axis_index("seq") % team
    return [
        (((me ^ 1) + 2 * k) % team, (me + 2 * k) % team) for k in reversed(turns(team))
    ]


def scatter_stages(blocks, team, ties=()):
    half = team // 2
    passing, leaving, before = {}, None, ()
    for (send, keep), k in zip(blocks, reversed(turns(team))):
        came = cross(after(send, *before, *ties), team)
        stage = [came]
        if leaving is not None:
            pair, n = leaving
            forward = 2 * n <= half
            to = n - 1 if forward else (n + 1) % half
            moved = turn(pair.astype(LOW), team, 1 if forward else -1)
            stage.append(moved)
            passing[to] = passing.get(to, []) + [moved]
        yield stage
        before = (came,)
        pair = keep.astype(WIDE) + came.astype(WIDE)
        for moved in passing.pop(k, []):
            pair = pair + moved.astype(WIDE)
        leaving = (pair, k)
    yield pair


def mixer_outputs_kernel(heads, taps, fsdp, place_ref, *refs):
    got_refs, out_refs, refs = refs[:heads], refs[heads : 2 * heads], refs[2 * heads :]
    (q_ref, k_ref, v_ref, g_ref, b_ref, d_ref, gin_ref, gff_ref, gh_ref, rate_ref, cq_ref,
     ck_ref, cv_ref, out_ref) = refs
    member = place_ref[0, heads]
    shard = q_ref.shape[0]
    gains = gh_ref.shape[1]
    width = heads * HEAD
    lane_r = lax.broadcasted_iota(jnp.int32, (1, heads), 1)
    rates = jnp.zeros((1, heads), WIDE)
    vectors = jnp.zeros((8, shard), WIDE)
    for n in range(heads):
        got_ref = got_refs[n]
        h = place_ref[0, n]

        def columns(step):
            return pl.ds(pl.multiple_of(step * width + h * HEAD, HEAD), HEAD)

        q_ref[:, columns(0)] = got_ref[:shard, 0:128].astype(WIDE)
        for i in range(2):
            k_ref[:, columns(i)] = got_ref[:shard, 128 + i * 128 : 256 + i * 128].astype(WIDE)
            v_ref[:, columns(i)] = got_ref[:shard, 384 + i * 128 : 512 + i * 128].astype(WIDE)
        g_ref[:, columns(0)] = got_ref[:shard, 640:768].astype(WIDE)
        last = got_ref[:shard, 768:896].astype(WIDE).T
        b_ref[pl.ds(h, 1), :] = last[0:1]
        b_ref[pl.ds(heads + h, 1), :] = last[1:2]
        d_ref[pl.ds(h, 1), :] = last[2:3]
        extra = got_ref[shard:, :].astype(WIDE)
        vectors = vectors + extra[0:8, :shard]
        rates = jnp.where(lane_r == h, extra[3:4, 2:3], rates)
        rows = out_refs[n].shape[0]
        out_ref[pl.ds(pl.multiple_of(h * rows, rows), rows), :] = out_refs[n][...].astype(WIDE)
        for ref, at, steps in ((cq_ref, 0, 1), (ck_ref, 128, 2), (cv_ref, 384, 2)):
            per = ref.shape[1] // HEAD
            for i in range(steps):
                slot = i * heads + h - member * per

                @pl.when((slot >= 0) & (slot < per))
                def _():
                    to = pl.ds(pl.multiple_of(slot * HEAD, HEAD), HEAD)
                    ref[:, to] = extra[4 : 4 + taps, at + i * HEAD : at + (i + 1) * HEAD]

    rate_ref[...] = rates
    gin_ref[...] = vectors[0:1]
    gff_ref[...] = vectors[1:2]
    gh_ref[...] = vectors[2:3, :gains]


def mixer_outputs(found, found_out, shard, gains, taps, fsdp, member):
    found, found_out = (
        [one for a, x, b, y in pairs for one in ((a, x), (b, y))] for pairs in (found, found_out)
    )
    heads = len(found)
    places = jnp.stack([place for place, _ in found] + [member])[None].astype(jnp.int32)
    width = heads * HEAD
    shape = jax.ShapeDtypeStruct
    outs = (
        shape((shard, width), WIDE),
        shape((shard, 2 * width), WIDE),
        shape((shard, 2 * width), WIDE),
        shape((shard, width), WIDE),
        shape((2 * heads, shard), WIDE),
        shape((heads, shard), WIDE),
        shape((1, shard), WIDE),
        shape((1, shard), WIDE),
        shape((1, gains), WIDE),
        shape((1, heads), WIDE),
        shape((taps, shard), WIDE),
        shape((taps, 2 * shard), WIDE),
        shape((taps, 2 * shard), WIDE),
        shape((shard, width), WIDE),
    )
    return pl.pallas_call(
        functools.partial(mixer_outputs_kernel, heads, taps, fsdp),
        out_shape=outs,
        in_specs=[smem_spec()] + [vmem_spec()] * (2 * heads),
        out_specs=[vmem_spec()] * len(outs),
        compiler_params=pltpu.CompilerParams(vmem_limit_bytes=VMEM_LIMIT),
        cost_estimate=estimate(0, 12),
        name="mixer_outputs",
    )(places, *(value for _, value in found), *(value for _, value in found_out))


def ff_outputs_kernel(count, slab, shard, place_ref, *refs):
    got_refs, (gate_ref, up_ref, down_ref), held = refs[:count], refs[count : count + 3], refs[-1]
    own = count * slab
    for n, got_ref in enumerate(got_refs):
        at = place_ref[n] * slab
        piece = got_ref[...].astype(WIDE)
        for m in range(2):
            for k in range(2):
                to = pl.multiple_of(k * own + at, 8)
                held[m, pl.ds(to, slab), :] = piece[
                    m * slab : (m + 1) * slab, k * shard : (k + 1) * shard
                ]
        down_ref[pl.ds(pl.multiple_of(at, 8), slab), :] = piece[2 * slab :]
    gate_ref[...] = held[0].T
    up_ref[...] = held[1].T


def ff_outputs(found, slab, shard, fsdp):
    found = [one for a, x, b, y in found for one in ((a, x), (b, y))]
    count, (rows, width) = len(found), found[0][1].shape
    own = count * slab
    shape = jax.ShapeDtypeStruct
    return pl.pallas_call(
        functools.partial(ff_outputs_kernel, count, slab, shard),
        out_shape=(
            shape((shard, fsdp * own), WIDE),
            shape((shard, fsdp * own), WIDE),
            shape((own, width), WIDE),
        ),
        grid_spec=pltpu.PrefetchScalarGridSpec(
            num_scalar_prefetch=1,
            grid=(fsdp // 2,),
            in_specs=[pl.BlockSpec((rows, 2 * shard), lambda i, p: (0, i))] * count,
            out_specs=(
                pl.BlockSpec((shard, 2 * own), lambda i, p: (0, i)),
                pl.BlockSpec((shard, 2 * own), lambda i, p: (0, i)),
                pl.BlockSpec((own, 2 * shard), lambda i, p: (0, i)),
            ),
            scratch_shapes=[pltpu.VMEM((2, 2 * own, shard), WIDE)],
        ),
        compiler_params=pltpu.CompilerParams(vmem_limit_bytes=VMEM_LIMIT),
        cost_estimate=estimate(0, 15),
        name="ff_outputs",
    )(jnp.stack([p for p, _ in found]).astype(jnp.int32), *(x for _, x in found))


def ff_outputs_plain(got, slab, shard, fsdp):
    seq, rows, width = got.shape
    own = seq * slab
    wide = got.astype(WIDE)

    def turned(at):
        part = wide[:, at : at + slab].reshape(seq, slab, fsdp, shard)
        return jnp.transpose(part, (3, 2, 0, 1)).reshape(shard, fsdp * own)

    return turned(0), turned(slab), wide[:, 2 * slab :].reshape(own, width)


def per_device(
    tokens, cotangent, offsets, gain_in, w_query, w_key, w_value, w_beta, w_decay, w_outgate,
    conv_query, conv_key, conv_value, decay_scale, gain_head, w_out, gain_ffn, w_gate, w_up,
    w_down,
):
    seq, fsdp = lax.axis_size("seq"), lax.axis_size("fsdp")
    heads = decay_scale.shape[0]
    taps = conv_query.shape[0]
    own_rows = tokens.shape[1]
    shard = w_query.shape[0]
    width = shard * fsdp
    teams = seq // heads
    assert teams * heads == seq and width == heads * HEAD
    place = lax.axis_index("seq")
    head, team = place % heads, place // heads
    member = lax.axis_index("fsdp")
    if teams == 1:
        team_groups, head_groups = None, None
    else:
        team_groups = [[t * heads + h for h in range(heads)] for t in range(teams)]
        head_groups = [[t * heads + h for t in range(teams)] for h in range(heads)]

    def gather_rows(value):
        return lax.all_gather(value, "fsdp", axis=0, tiled=True)

    found = last_of(gather_stages(tokens[0], heads))
    length = heads * own_rows

    near = found[0][3]
    packed = pack_weights(
        head, after(w_query, near), w_key, w_value, w_outgate, w_beta, w_decay, gain_in,
        gain_ffn, gain_head, conv_query, conv_key, conv_value,
    )
    far_packed = far_exchange(packed, "fsdp")
    far_packed = after(far_packed, *(rows for _, rows, _, _ in found[1:-1]))
    got = ordered_gather(packed, "fsdp", far_packed)
    full_packed = got[:, :shard].reshape(width, 896)
    vectors = got[:, shard:, :shard]
    full_gain_in = vectors[:, 0].reshape(width).astype(WIDE)
    full_gain_ffn = vectors[:, 1].reshape(width).astype(WIDE)
    full_gain_head = vectors[:, 2, : gain_head.shape[0]].reshape(1, HEAD).astype(WIDE)

    def head_taps_of(row, pieces, step):
        column = step * width + head * HEAD
        inside = column % (pieces * shard)
        at = (column // (pieces * shard), row + inside // shard * taps, inside % shard)
        return lax.dynamic_slice(vectors, at, (1, taps, HEAD))[0]

    head_taps = jnp.concatenate(
        [head_taps_of(3, 1, 0)]
        + [head_taps_of(3 + taps, 2, i) for i in range(2)]
        + [head_taps_of(3 + 3 * taps, 2, i) for i in range(2)],
        axis=1,
    ).astype(WIDE)
    head_taps = jnp.pad(head_taps, ((0, 8 - taps), (0, 0)))
    def column_blocks(value):
        return jnp.transpose(value.reshape(shard, fsdp, value.shape[1] // fsdp), (1, 0, 2))

    gate_blocks, up_blocks = column_blocks(after(w_gate, near)), column_blocks(after(w_up, near))
    full_packed, gate_blocks, up_blocks = lax.optimization_barrier(
        (full_packed, gate_blocks, up_blocks)
    )
    filled = None
    for n, (at, rows, at_other, other) in enumerate(found):
        places = jnp.stack([at, at_other]).astype(jnp.int32)
        filled = project(places, rows, other, full_gain_in[None], full_packed, length, filled)
        if n == 0:
            w_out, gate_blocks, up_blocks, cot, *filled = lax.optimization_barrier(
                (w_out, gate_blocks, up_blocks, cotangent[0], *filled)
            )
            cols_gate = lax.all_to_all(gate_blocks, "fsdp", 0, 0)
            cols_up = lax.all_to_all(up_blocks, "fsdp", 0, 0)
            far_out, far_cot = far_exchange(w_out, "fsdp"), far_exchange(cot, "fsdp")
    normed_low, pre, gate_small = filled
    offs = jnp.concatenate(
        [offsets, jnp.broadcast_to(team * length, (1, 1)).astype(jnp.int32)], axis=1
    )
    rate = lax.dynamic_slice_in_dim(decay_scale, head, 1).reshape(1, 1)
    zero_state = jnp.zeros((HEAD, HEAD), WIDE)
    if teams == 1:
        edge = jnp.zeros((16, 640), LOW)
    else:
        forth = [(i, i + heads) for i in range(seq - heads)]
        back = [(i + heads, i) for i in range(seq - heads)]
        edge = lax.ppermute(pre[-16:], "seq", forth)

    def forward_from(state):
        return run_forward(
            offs, rate, pre, gate_small, edge, head_taps, full_gain_head, state
        )

    state_in = zero_state
    if teams > 1:
        trial = forward_from(zero_state)
        steps, end = trial[4], trial[9]

        def along(c, total):
            return jnp.dot(total, steps[c].T, precision=lax.Precision.HIGHEST)

        whole_map = lax.fori_loop(0, steps.shape[0], along, jnp.eye(HEAD, dtype=WIDE))
        for _ in range(teams - 1):
            out = jnp.dot(state_in, whole_map, precision=lax.Precision.HIGHEST) + end
            state_in = lax.ppermute(out.astype(LOW), "seq", forth).astype(WIDE)
    conv, inverse, scores, reach, steps, gated, mixed, upd, states, _ = forward_from(state_in)
    gated, far_out, cols_gate, cols_up, far_cot = lax.optimization_barrier(
        (gated, far_out, cols_gate, cols_up, far_cot)
    )
    full_out = ordered_gather(w_out, "fsdp", far_out).reshape(width, width)
    group_cot = near_gather(cot, "fsdp", far_cot)
    cols_gate, cols_up = (a.reshape(width, a.shape[2]) for a in (cols_gate, cols_up))

    gated_own = lax.all_to_all(
        gated, "seq", 0, 1, tiled=True, axis_index_groups=team_groups
    )
    inputs = tokens[0].astype(WIDE)
    mixer_res = inputs + dot_plain(gated_own, full_out)

    mid_normed = rms_parts(mixer_res)
    mid_low = (mid_normed * full_gain_ffn).astype(LOW)
    group_mid = near_gather(mid_low, "fsdp")
    gate_pre = dot_plain(group_mid, cols_gate)
    up_pre = dot_plain(group_mid, cols_up)
    sig = jax.nn.sigmoid(gate_pre)
    act = gate_pre * sig
    hidden = (act * up_pre).astype(LOW)
    grad_hidden = dot_right(group_cot, w_down)
    grad_gate_pre = (grad_hidden * up_pre * (sig * (1.0 + gate_pre * (1.0 - sig)))).astype(LOW)
    grad_up_pre = (grad_hidden * act).astype(LOW)
    grad_mid = dot_right(grad_gate_pre, cols_gate) + dot_right(grad_up_pre, cols_up)
    grad_gate_pre, grad_up_pre, grad_mid = lax.optimization_barrier(
        (grad_gate_pre, grad_up_pre, grad_mid)
    )
    grad_mid = near_scatter(grad_mid, "fsdp")

    grad_res = cotangent[0].astype(WIDE) + rms_back(grad_mid * full_gain_ffn, mixer_res)
    grad_gain_ffn = jnp.sum(grad_mid * mid_normed, axis=0)
    res_low = grad_res.astype(LOW)
    grad_gated = dot_right(res_low, full_out).astype(LOW)
    own_ff = w_down.shape[0]
    slab = own_ff // seq
    slabs = jnp.concatenate(
        [
            dot_left(grad_gate_pre, group_mid, LOW).reshape(seq, slab, width),
            dot_left(grad_up_pre, group_mid, LOW).reshape(seq, slab, width),
            dot_left(hidden, group_cot, LOW).reshape(seq, slab, width),
        ],
        axis=1,
    )
    permuted = teams == 1 and slab % 8 == 0 and own_ff * 2 % HEAD == 0 and fsdp % 2 == 0

    def turned_columns(summed):
        turned = lax.all_to_all(summed[: 2 * slab], "fsdp", 1, 1, tiled=True)
        return stack(turned, summed[2 * slab :])

    def feed_forward_sums():
        if not permuted:
            summed = lax.psum_scatter(
                slabs.reshape(seq * 3 * slab, width), "seq", scatter_dimension=0, tiled=True
            )
            yield [summed]
            slabs_done = lax.all_gather(turned_columns(summed), "seq", axis=0)
            yield ff_outputs_plain(slabs_done, slab, shard, fsdp)
            return
        blocks = [
            [lax.dynamic_index_in_dim(slabs, p, 0, False) for p in pair]
            for pair in team_places(heads)
        ]
        for stage in scatter_stages(blocks, heads, ties):
            if isinstance(stage, list):
                yield stage
        mine = turned_columns(after(stage.astype(LOW), *ties))
        yield [mine]
        for stage in gather_stages(mine, heads, ties):
            if isinstance(stage[0], tuple):
                break
            yield stage
        yield ff_outputs(stage, slab, shard, fsdp)

    ties, sums = [], feed_forward_sums()
    brought = [next(sums)]

    def beside(value):
        if not isinstance(brought[-1], tuple):
            ties[:] = [value]
            brought.append(next(sums))

    def settled(value):
        stage = brought[-1]
        return value if isinstance(stage, tuple) else after(value, *stage)

    beside(grad_gated)
    dgated = lax.all_to_all(
        grad_gated, "seq", 1, 0, tiled=True, axis_index_groups=team_groups
    )
    dgated = settled(dgated)
    beside(dgated)
    down_part = near_scatter(dot_plain(after(hidden, dgated), w_down), "fsdp")
    layer_out = (mixer_res + down_part).astype(LOW)
    grad_out = dot_left(after(gated_own, dgated), res_low, LOW).reshape(fsdp, shard, width)
    grad_out = near_scatter(near_blocks(grad_out, "fsdp"), "fsdp").astype(LOW)

    def gate_back_from(dend):
        return run_gate_back(
            gate_small, full_gain_head, mixed, reach, steps, dgated, dend
        )

    dend = zero_state
    if teams > 1:
        begin = gate_back_from(zero_state)[4]
        for _ in range(teams - 1):
            out = lax.dot_general(
                dend, whole_map, (((1,), (1,)), ((), ())), precision=lax.Precision.HIGHEST
            )
            dend = lax.ppermute((out + begin).astype(LOW), "seq", back).astype(WIDE)
    do, ds, dgate, dgain, _ = gate_back_from(dend)
    carried = [
        jnp.zeros((4, 8, 640), WIDE), jnp.zeros((8, 640), WIDE), jnp.zeros((1, HEAD), WIDE)
    ]
    dy, calls = None, 6
    left = length // (2 * SPAN)
    for call in range(calls, 0, -1):
        steps_here = -(-left // call)
        carried[0] = settled(carried[0] if dy is not None else after(carried[0], do))
        beside(carried[0])
        dy, carried = run_backward(
            left - 1, steps_here, offs, rate, pre, gate_small, edge, head_taps,
            (conv, inverse, upd, scores, states, do, ds, dgate), carried, dy,
        )
        carried = list(carried)
        left -= steps_here
    dy = settled(dy)
    following, dtaps, drate = carried
    if teams > 1:
        none = jnp.zeros((16, 640), WIDE)
        dedge = sum(stack(none, following[lag])[lag : lag + 16] for lag in range(1, 4))
        from_next = lax.ppermute(dedge.astype(LOW), "seq", back).astype(WIDE)
        tail = (dy[-16:, :640].astype(WIDE) + from_next).astype(LOW)
        dy = lax.dynamic_update_slice(dy, tail, (length - 16, 0))

    out_rows = shard // heads

    blocks = [
        list(input_blocks(places, dy, grad_out, full_packed, own_rows, out_rows))
        for places in team_places(heads)
    ]
    while not isinstance(brought[-1], tuple):
        beside(dy)
    out_gate, out_up, out_down = brought[-1]
    sent = scatter_stages(blocks, heads)
    stage = next(sent)
    grad_packed = dot_left(normed_low, after(dy, blocks[0][0]))
    stage = next(sent)
    stage = next(sent)
    stage = next(sent)
    ready = (stage[0],)
    joined = next(sent)
    grad_normed, own_out = joined[:own_rows], joined[own_rows:].astype(LOW)
    input_grad = (grad_res + rms_back(grad_normed * full_gain_in, inputs)).astype(LOW)
    if teams > 1:
        own_out = lax.psum(own_out, "seq", axis_index_groups=head_groups)
    found_out = last_of(gather_stages(own_out, heads))

    grad_gain_in = (
        jnp.sum(grad_packed * full_packed.astype(WIDE), axis=1) / full_gain_in
    )
    extra = jnp.zeros((fsdp, 16, 896), WIDE)
    extra = extra.at[:, 0, :shard].set(grad_gain_in.reshape(fsdp, shard))
    extra = extra.at[:, 1, :shard].set(grad_gain_ffn.reshape(fsdp, shard))
    gh = gain_head.shape[0]
    extra = extra.at[:, 2, :gh].set(dgain.reshape(fsdp, gh))
    extra = extra.at[:, 3, :HEAD].set(drate)
    extra = extra.at[:, 4 : 4 + taps, :640].set(dtaps[None, :taps])
    combined = jnp.concatenate([grad_packed.reshape(fsdp, shard, 896), extra], axis=1)
    combined = near_scatter(near_blocks(combined.astype(LOW), "fsdp"), "fsdp").astype(LOW)
    if teams > 1:
        combined = lax.psum(combined, "seq", axis_index_groups=head_groups)
    (out_query, out_key, out_value, out_gatew, out_beta, out_decay, out_gain_in, out_gain_ffn,
     out_gain_head, out_rate, out_cq, out_ck, out_cv, out_out) = mixer_outputs(
        last_of(gather_stages(after(combined, *ready), heads)), found_out, shard, gain_head.shape[0], taps, fsdp, member
    )

    return (
        layer_out[None],
        input_grad[None],
        out_gain_in[0],
        out_query,
        out_key,
        out_value,
        out_beta.T,
        out_decay.T,
        out_gatew,
        out_cq,
        out_ck,
        out_cv,
        out_rate[0],
        out_gain_head[0],
        out_out,
        out_gain_ffn[0],
        out_gate,
        out_up,
        out_down,
    )


def solution(mesh):
    rows, lanes = P("fsdp", None), P(None, "fsdp")
    block = P("fsdp", "seq", None)
    return jax.shard_map(
        per_device,
        mesh=mesh,
        in_specs=(
            block, block, rows, P("fsdp"), rows, rows, rows, rows, rows, rows,
            lanes, lanes, lanes, P(), P("fsdp"), rows, P("fsdp"), rows, rows, rows,
        ),
        out_specs=(
            block, block, P("fsdp"), rows, rows, rows, rows, rows, rows,
            lanes, lanes, lanes, P(), P("fsdp"), rows, P("fsdp"), rows, rows, rows,
        ),
        check_vma=False,
    )
```

```python
import functools

import jax
import jax.numpy as jnp
from jax import lax
from jax.experimental import pallas as pl
from jax.experimental.pallas import tpu as pltpu
from jax.sharding import PartitionSpec as P

SPAN = 64
PER = 4
ROWS = 128
HEAD = 128
EPSILON = 1e-06
LOW = jnp.bfloat16
WIDE = jnp.float32
VMEM_LIMIT = 56 * 1024 * 1024


def contract(left, right, left_dim, right_dim):
    return lax.dot_general(
        left, right, (((left_dim,), (right_dim,)), ((), ())), preferred_element_type=WIDE
    )


def halves(value):
    high = value.astype(LOW)
    return high, (value - high.astype(WIDE)).astype(LOW)


def mm(left, right, left_dim=1, right_dim=0):
    return contract(left.astype(LOW), right.astype(LOW), left_dim, right_dim)


def stack(*parts):
    return jnp.concatenate(parts, axis=0)


def row_maps():
    row = lax.broadcasted_iota(jnp.int32, (ROWS, ROWS), 0)
    col = lax.broadcasted_iota(jnp.int32, (ROWS, ROWS), 1)
    tok, step = row & (SPAN - 1), row >> 6
    tok_c, step_c = col & (SPAN - 1), col >> 6
    return tok, step, tok_c, step_c


def span_tokens(offs_ref, doc_count, first):
    place = first + lax.broadcasted_iota(jnp.int32, (SPAN, 1), 0)
    begin = jnp.zeros((SPAN, 1), jnp.int32)
    for j in range(doc_count):
        start = offs_ref[0, j]
        begin = jnp.where(place >= start, start, begin)
    return place - begin


def softplus(value):
    return jnp.maximum(value, 0.0) + jnp.log1p(jnp.exp(-jnp.abs(value)))


def decay_sums(small, rate):
    logs = -rate * softplus(small)
    tok = lax.broadcasted_iota(jnp.int32, (SPAN, SPAN), 0)
    tok_c = lax.broadcasted_iota(jnp.int32, (SPAN, SPAN), 1)
    lower = jnp.where(tok >= tok_c, 1.0, 0.0).astype(LOW)
    tok_w = lax.broadcasted_iota(jnp.int32, (SPAN, ROWS), 0)
    tok_wc = lax.broadcasted_iota(jnp.int32, (SPAN, ROWS), 1) & (SPAN - 1)
    upper = jnp.where(tok_w <= tok_wc, 1.0, 0.0).astype(LOW)
    high, rest = halves(logs)
    cols = contract(lower, high, 1, 0) + contract(lower, rest, 1, 0)
    rows = contract(high, upper, 0, 0) + contract(rest, upper, 0, 0)
    return cols[:, 2:3], rows[2:3, :]


def unit(values):
    scale = lax.rsqrt(jnp.sum(values * values, axis=1, keepdims=True) + EPSILON)
    return values * scale, scale


def span_factors(small, rate, pos):
    sig = jax.nn.sigmoid(small)
    cum, cum_row = decay_sums(small, rate)
    beta = stack(sig[:, 0:1], sig[:, 1:2])
    cum2, pos2 = stack(cum, cum), stack(pos, pos)
    tok, step, tok_c, step_c = row_maps()
    before = tok > tok_c
    here = tok == tok_c
    reach = (before | (here & (step >= step_c))) & (tok - tok_c <= pos2)
    decay = jnp.where(reach, jnp.exp(jnp.where(reach, cum2 - cum_row, 0.0)), 0.0)
    strict = before | (here & (step > step_c))
    tok1 = tok[:, 0:1]
    carry = jnp.where(pos2 > tok1, jnp.exp(cum2), 0.0)
    end, end_pos = cum[SPAN - 1 : SPAN], pos[SPAN - 1 : SPAN]
    leave = jnp.where(SPAN - 1 - tok1 <= end_pos, jnp.exp(end - cum2), 0.0)
    carry_all = jnp.where(end_pos >= SPAN, jnp.exp(end), 0.0)
    return beta, decay, strict, carry, leave, carry_all, tok ^ tok_c


def in_turns(bodies):
    bodies = list(bodies)
    while bodies:
        bodies = [body for body in bodies if next(body, "end") != "end"]


def unit_lower_inverse(strict_part, apart):
    row = lax.broadcasted_iota(jnp.int32, (ROWS, ROWS), 0)
    col = lax.broadcasted_iota(jnp.int32, (ROWS, ROWS), 1)
    inverse = jnp.where(row == col, 1.0, 0.0) - jnp.where(apart == 0, strict_part, 0.0)
    for level in range(6):
        block = jnp.where((apart >> level) == 1, strict_part, 0.0)
        low = inverse.astype(LOW)
        half = contract(low, block.astype(LOW), 1, 0).astype(LOW)
        yield
        inverse = inverse - contract(half, low, 1, 0)
        yield
    return inverse


def conv_rows(prior, here):
    return stack(prior.astype(WIDE), here.astype(WIDE))


def forward_kernel(
    span_count, doc_count, group,
    offs_ref, rate_ref, pre_ref, prior_ref, small_ref, gate_ref, edge_ref, taps_ref, gain_ref,
    state_ref,
    conv_ref, t_ref, sc_ref, qh_ref, ah_ref, al_ref, gated_ref, mixed_ref, u_ref, s_ref, end_ref,
    w_scr, u0_scr, b_scr, o0_scr, ah_scr, al_scr, qh_scr,
):
    step = pl.program_id(0)
    base = offs_ref[0, doc_count]
    rate = rate_ref[0, 0]
    prior = jnp.where(step == 0, edge_ref[...].astype(WIDE), prior_ref[...].astype(WIDE))

    def local(u):
        c = step * group + u
        here = pre_ref[u * SPAN : (u + 1) * SPAN, :].astype(WIDE)
        if u:
            before = pre_ref[u * SPAN - 16 : u * SPAN, :].astype(WIDE)
        else:
            before = prior
        rows = stack(before, here)
        pos = span_tokens(offs_ref, doc_count, base + c * SPAN)
        conv = taps_ref[0:1, :] * here
        for lag in range(1, 4):
            shifted = rows[16 - lag : 16 - lag + SPAN]
            conv = conv + jnp.where(pos >= lag, taps_ref[lag : lag + 1, :] * shifted, 0.0)
        conv_ref[u * SPAN : (u + 1) * SPAN, :] = conv
        yield
        act = conv * jax.nn.sigmoid(conv)
        query, _ = unit(act[:, 0:128])
        key0, _ = unit(act[:, 128:256])
        key1, _ = unit(act[:, 256:384])
        keys = stack(key0, key1)
        values = stack(act[:, 384:512], act[:, 512:640])
        small = small_ref[u * SPAN : (u + 1) * SPAN, :]
        beta, decay, strict, carry, leave, carry_all, apart = span_factors(small, rate, pos)
        yield
        inner = mm(keys, keys, 1, 1)
        yield
        inverse = yield from unit_lower_inverse(
            jnp.where(strict, beta * decay * inner, 0.0), apart
        )
        t_ref[u] = inverse.astype(LOW)
        both = mm(inverse, jnp.concatenate([(beta * carry) * keys, beta * values], axis=1))
        yield
        weight, fresh = both[:, :HEAD], both[:, HEAD:]
        w_scr[c] = weight.astype(LOW)
        u0_scr[c] = fresh
        leaving = (keys * leave).astype(LOW)
        row = lax.broadcasted_iota(jnp.int32, (HEAD, HEAD), 0)
        col = lax.broadcasted_iota(jnp.int32, (HEAD, HEAD), 1)
        step_map = jnp.where(row == col, carry_all, 0.0) - mm(leaving, weight, 0, 0)
        map_high, map_rest = halves(step_map)
        ah_ref[u], al_ref[u] = map_high, map_rest
        ah_scr[c], al_scr[c] = map_high, map_rest
        yield
        b_scr[c] = mm(fresh, leaving, 0, 0)
        yield
        scores = mm(query, keys, 1, 1) * decay[SPAN:, :]
        yield
        sc_ref[u] = scores.astype(LOW)
        mixed_both = mm(scores, both)
        yield
        reach = (carry[SPAN:] * query - mixed_both[:, :HEAD]).astype(LOW)
        qh_ref[u] = reach
        qh_scr[c] = reach
        o0_scr[c] = mixed_both[:, HEAD:]

    in_turns(local(u) for u in range(group))

    def chain(i, state):
        for u in range(4):
            c = i * 4 + u
            s_ref[c] = state
            high, rest = halves(state)
            state = (
                contract(high, ah_scr[c], 1, 1)
                + contract(high, al_scr[c], 1, 1)
                + contract(rest, ah_scr[c], 1, 1)
                + b_scr[c]
            )
        return state

    def mixing(c):
        low = s_ref[c].astype(LOW)
        u_ref[c] = (u0_scr[c] - contract(w_scr[c], low, 1, 1)).astype(LOW)
        yield
        mixed = o0_scr[c] + contract(qh_scr[c], low, 1, 1)
        yield
        lo = pl.multiple_of(c * SPAN, SPAN)
        mixed_ref[pl.ds(lo, SPAN), :] = mixed
        scale = lax.rsqrt(jnp.mean(mixed * mixed, axis=1, keepdims=True) + EPSILON)
        yield
        gate = gate_ref[pl.ds(lo, SPAN), :]
        gated_ref[pl.ds(lo, SPAN), :] = (
            mixed * scale * gain_ref[...] * (gate * jax.nn.sigmoid(gate))
        ).astype(LOW)
        yield

    def mixing_step(i, none):
        in_turns(mixing(i * 8 + u) for u in range(8))
        return none

    @pl.when(step == pl.num_programs(0) - 1)
    def _():
        end_ref[...] = lax.fori_loop(0, span_count // 4, chain, state_ref[...])
        lax.fori_loop(0, span_count // 8, mixing_step, 0)


def gate_back_kernel(
    span_count,
    gate_ref, gain_ref, mixed_ref, qh_ref, ah_ref, al_ref, dgated_ref, dend_ref,
    do_ref, ds_ref, dgate_ref, dgain_ref, dbegin_ref,
    f_scr,
):
    dgain_ref[...] = jnp.zeros_like(dgain_ref)

    def gate_back(c):
        lo = pl.multiple_of(c * SPAN, SPAN)
        mixed = mixed_ref[pl.ds(lo, SPAN), :]
        gate = gate_ref[pl.ds(lo, SPAN), :]
        scale = lax.rsqrt(jnp.mean(mixed * mixed, axis=1, keepdims=True) + EPSILON)
        normed = mixed * scale
        yield
        sig = jax.nn.sigmoid(gate)
        grad = dgated_ref[pl.ds(lo, SPAN), :].astype(WIDE)
        by_gain = grad * normed
        dgate_ref[pl.ds(lo, SPAN), :] = (
            by_gain * gain_ref[...] * (sig * (1.0 + gate * (1.0 - sig)))
        ).astype(LOW)
        dgain_ref[...] += jnp.sum(by_gain * (gate * sig), axis=0, keepdims=True)
        yield
        dn = grad * (gate * sig) * gain_ref[...]
        dmixed = scale * (dn - normed * jnp.mean(dn * normed, axis=1, keepdims=True))
        do_low = dmixed.astype(LOW)
        do_ref[c] = do_low
        yield
        f_scr[c] = contract(do_low, qh_ref[c], 0, 0)

    def gate_step(i, none):
        in_turns(gate_back(i * 8 + u) for u in range(8))
        return none

    lax.fori_loop(0, span_count // 8, gate_step, 0)

    def chain_step(i, grad):
        for u in range(4):
            c = span_count - 1 - (i * 4 + u)
            ds_ref[c] = grad
            high, rest = halves(grad)
            grad = (
                contract(high, ah_ref[c], 1, 0)
                + contract(high, al_ref[c], 1, 0)
                + contract(rest, ah_ref[c], 1, 0)
                + f_scr[c]
            )
        return grad

    dbegin_ref[...] = lax.fori_loop(0, span_count // 4, chain_step, dend_ref[...])


def backward_kernel(
    at_block, doc_count,
    offs_ref, rate_ref, pre_ref, prior_ref, small_ref, edge_ref, taps_ref,
    conv_ref, t_ref, u_ref, sc_ref, s_ref, do_ref, ds_ref, dgate_ref,
    next_in, dtaps_in, drate_in, *refs,
):
    dy_ref, next_ref, dtaps_ref, drate_ref = refs[-4:]
    block = at_block(pl.program_id(0))
    base = offs_ref[0, doc_count]
    rate = rate_ref[0, 0]

    @pl.when(pl.program_id(0) == 0)
    def _():
        next_ref[...] = next_in[...]
        dtaps_ref[...] = dtaps_in[...]
        drate_ref[...] = drate_in[...]

    dy_ref[:, 640:768] = dgate_ref[...]

    def local(n):
        lo, hi = n * SPAN, (n + 1) * SPAN
        pos = span_tokens(offs_ref, doc_count, base + block * PER * SPAN + lo)
        conv = conv_ref[lo:hi, :]
        sig = jax.nn.sigmoid(conv)
        act = conv * sig
        query, scale_q = unit(act[:, 0:128])
        key0, scale_0 = unit(act[:, 128:256])
        key1, scale_1 = unit(act[:, 256:384])
        yield
        keys = stack(key0, key1)
        values = stack(act[:, 384:512], act[:, 512:640])
        small = small_ref[lo:hi, :]
        beta, decay, strict, carry, leave, carry_all, _ = span_factors(small, rate, pos)
        yield
        state, dstate = s_ref[n], ds_ref[n]
        state_l, dstate_l = state.astype(LOW), dstate.astype(LOW)
        upd, out_grad, keys_l = u_ref[n], do_ref[n], keys.astype(LOW)
        dupd = contract(sc_ref[n], out_grad, 0, 0) + mm(keys * leave, dstate_l, 1, 1)
        yield
        dtarget = mm(t_ref[n], dupd, 0, 0)
        yield
        pair = stack(dtarget.astype(LOW), out_grad)
        by_upd = contract(pair, upd, 1, 1)
        by_state = contract(pair, state_l, 1, 0)
        yield
        dinner = jnp.where(strict, -by_upd[:ROWS] * decay, 0.0)
        dscore = by_upd[ROWS:] * decay[SPAN:, :]
        both = stack(dinner, dscore).astype(LOW)
        reading = contract(both, keys_l, 1, 0)
        yield
        read_key = reading[:ROWS] - carry * by_state[:ROWS]
        dquery = reading[ROWS:] + carry[SPAN:] * by_state[ROWS:]
        dleave = leave * contract(upd, dstate_l, 1, 0)
        write_key = contract(both, stack(beta * keys, query).astype(LOW), 0, 0) + dleave
        yield
        key_read = jnp.sum(keys * read_key, axis=1, keepdims=True)
        dbeta = jnp.sum(dtarget * values, axis=1, keepdims=True) + key_read
        dcum = beta * key_read - jnp.sum(keys * write_key, axis=1, keepdims=True)
        dcum = dcum[:SPAN] + dcum[SPAN:] + jnp.sum(query * dquery, axis=1, keepdims=True)
        through = jnp.sum(keys * dleave, axis=0, keepdims=True) + carry_all * jnp.sum(
            dstate * state, axis=0, keepdims=True
        )
        through = jnp.sum(through, axis=1, keepdims=True)
        tok1 = lax.broadcasted_iota(jnp.int32, (SPAN, 1), 0)
        dcum = dcum + jnp.where(tok1 == SPAN - 1, through, 0.0)
        tok = lax.broadcasted_iota(jnp.int32, (SPAN, SPAN), 0)
        tok_c = lax.broadcasted_iota(jnp.int32, (SPAN, SPAN), 1)
        upper = jnp.where(tok <= tok_c, 1.0, 0.0).astype(LOW)
        high, rest = halves(jnp.broadcast_to(dcum, (SPAN, 128)))
        dlog = contract(upper, high, 1, 0) + contract(upper, rest, 1, 0)
        yield
        soft = softplus(small)
        sig_small = jax.nn.sigmoid(small)
        lane = lax.broadcasted_iota(jnp.int32, (SPAN, 128), 1)
        drate_ref[...] += jnp.sum(jnp.where(lane == 2, -dlog * soft, 0.0), axis=0, keepdims=True)
        dsig = jnp.where(lane == 0, dbeta[:SPAN], dbeta[SPAN:]) * sig_small * (1.0 - sig_small)
        dsmall = jnp.where(lane < 2, dsig, jnp.where(lane == 2, -rate * dlog * sig_small, 0.0))
        dy_ref[lo:hi, 768:896] = dsmall.astype(LOW)
        yield
        dkey = beta * read_key + write_key
        dvalue = beta * dtarget

        def unit_back(grad, normed, scale):
            return scale * (grad - normed * jnp.sum(grad * normed, axis=1, keepdims=True))

        dact = jnp.concatenate(
            [
                unit_back(dquery, query, scale_q),
                unit_back(dkey[:SPAN], key0, scale_0),
                unit_back(dkey[SPAN:], key1, scale_1),
                dvalue[:SPAN],
                dvalue[SPAN:],
            ],
            axis=1,
        )
        dconv = dact * (sig * (1.0 + conv * (1.0 - sig)))
        yield
        here = pre_ref[lo:hi, :].astype(WIDE)
        if n:
            prior = pre_ref[lo - 16 : lo, :].astype(WIDE)
        else:
            prior = jnp.where(
                block == 0, edge_ref[...].astype(WIDE), prior_ref[...].astype(WIDE)
            )
        rows = stack(prior, here)
        dpre = taps_ref[0:1, :] * dconv
        dtaps_ref[0:1, :] += jnp.sum(dconv * here, axis=0, keepdims=True)
        for lag in range(1, 4):
            kept = jnp.where(pos >= lag, dconv, 0.0)
            shifted = rows[16 - lag : 16 - lag + SPAN]
            dtaps_ref[lag : lag + 1, :] += jnp.sum(kept * shifted, axis=0, keepdims=True)
            kept = kept * taps_ref[lag : lag + 1, :]
            dpre = dpre + stack(kept, next_ref[lag])[lag : lag + SPAN]
            next_ref[lag] = kept[0:8]
        dy_ref[lo:hi, 0:640] = dpre.astype(LOW)

    in_turns(local(n) for n in reversed(range(PER)))


def vmem_spec():
    return pl.BlockSpec(memory_space=pltpu.VMEM)


def smem_spec():
    return pl.BlockSpec(memory_space=pltpu.SMEM)


def fixed(shape):
    return pl.BlockSpec(shape, lambda *_: (0,) * len(shape))


def estimate(flops, mib):
    return pl.CostEstimate(flops=int(flops), bytes_accessed=int(mib * 2**20), transcendentals=0)


def run_forward(offs, rate, pre, gs, edge, taps, gain, state):
    tokens = pre.shape[0]
    spans = tokens // SPAN
    group = 8
    shape = jax.ShapeDtypeStruct
    outs = (
        (shape((tokens, 640), WIDE), pl.BlockSpec((group * SPAN, 640), lambda i: (i, 0))),
        (shape((spans, ROWS, ROWS), LOW), pl.BlockSpec((group, ROWS, ROWS), lambda i: (i, 0, 0))),
        (shape((spans, SPAN, ROWS), LOW), pl.BlockSpec((group, SPAN, ROWS), lambda i: (i, 0, 0))),
        (shape((spans, SPAN, HEAD), LOW), pl.BlockSpec((group, SPAN, HEAD), lambda i: (i, 0, 0))),
        (shape((spans, HEAD, HEAD), LOW), pl.BlockSpec((group, HEAD, HEAD), lambda i: (i, 0, 0))),
        (shape((spans, HEAD, HEAD), LOW), pl.BlockSpec((group, HEAD, HEAD), lambda i: (i, 0, 0))),
        (shape((tokens, HEAD), LOW), fixed((tokens, HEAD))),
        (shape((tokens, HEAD), WIDE), fixed((tokens, HEAD))),
        (shape((spans, ROWS, HEAD), LOW), fixed((spans, ROWS, HEAD))),
        (shape((spans, HEAD, HEAD), WIDE), fixed((spans, HEAD, HEAD))),
        (shape((HEAD, HEAD), WIDE), fixed((HEAD, HEAD))),
    )
    return pl.pallas_call(
        functools.partial(forward_kernel, spans, offs.shape[1] - 1, group),
        out_shape=[o for o, _ in outs],
        grid=(spans // group,),
        in_specs=[
            smem_spec(),
            smem_spec(),
            pl.BlockSpec((group * SPAN, 640), lambda i: (i, 0)),
            pl.BlockSpec((16, 640), lambda i: (jnp.maximum(i * (group * SPAN // 16) - 1, 0), 0)),
            pl.BlockSpec((group * SPAN, HEAD), lambda i: (i, 1)),
            fixed((tokens, HEAD)),
            fixed((16, 640)),
            fixed((8, 640)),
            fixed((1, HEAD)),
            fixed((HEAD, HEAD)),
        ],
        out_specs=[b for _, b in outs],
        scratch_shapes=[
            pltpu.VMEM((spans, ROWS, HEAD), LOW),
            pltpu.VMEM((spans, ROWS, HEAD), WIDE),
            pltpu.VMEM((spans, HEAD, HEAD), WIDE),
            pltpu.VMEM((spans, SPAN, HEAD), WIDE),
            pltpu.VMEM((spans, HEAD, HEAD), LOW),
            pltpu.VMEM((spans, HEAD, HEAD), LOW),
            pltpu.VMEM((spans, SPAN, HEAD), LOW),
        ],
        compiler_params=pltpu.CompilerParams(vmem_limit_bytes=VMEM_LIMIT),
        cost_estimate=estimate(70e9, 24),
        name="delta_forward",
    )(offs, rate, pre, pre, gs, gs, edge, taps, gain, state)


def run_gate_back(gs, gain, mixed, qh, high, rest, dgated, dend):
    tokens = mixed.shape[0]
    spans = tokens // SPAN
    shape = jax.ShapeDtypeStruct
    return pl.pallas_call(
        functools.partial(gate_back_kernel, spans),
        out_shape=(
            shape((spans, SPAN, HEAD), LOW),
            shape((spans, HEAD, HEAD), WIDE),
            shape((tokens, HEAD), LOW),
            shape((1, HEAD), WIDE),
            shape((HEAD, HEAD), WIDE),
        ),
        grid=(1,),
        in_specs=[
            fixed((tokens, HEAD)),
            fixed((1, HEAD)),
            fixed((tokens, HEAD)),
            fixed((spans, SPAN, HEAD)),
            fixed((spans, HEAD, HEAD)),
            fixed((spans, HEAD, HEAD)),
            fixed((tokens, HEAD)),
            fixed((HEAD, HEAD)),
        ],
        out_specs=(
            fixed((spans, SPAN, HEAD)),
            fixed((spans, HEAD, HEAD)),
            fixed((tokens, HEAD)),
            fixed((1, HEAD)),
            fixed((HEAD, HEAD)),
        ),
        scratch_shapes=[pltpu.VMEM((spans, HEAD, HEAD), WIDE)],
        compiler_params=pltpu.CompilerParams(vmem_limit_bytes=VMEM_LIMIT),
        cost_estimate=estimate(15e9, 8),
        name="delta_gate_back",
    )(gs, gain, mixed, qh, high, rest, dgated, dend)


def run_backward(last, steps, offs, rate, pre, gs, edge, taps, saved, carried, dy):
    conv, inverse, upd, scores, states, do, ds, dgate = saved
    tokens = pre.shape[0]

    def at(i):
        return last - i

    def rows(columns, lane=0):
        return pl.BlockSpec((PER * SPAN, columns), lambda i: (at(i), lane))

    def spans(a, b):
        return pl.BlockSpec((PER, a, b), lambda i: (at(i), 0, 0))

    shape = jax.ShapeDtypeStruct
    carried_specs = [fixed((4, 8, 640)), fixed((8, 640)), fixed((1, HEAD))]
    operands = [offs, rate, pre, pre, gs, edge, taps, conv, inverse, upd, scores, states, do, ds]
    operands += [dgate, *carried]
    in_specs = [
        smem_spec(),
        smem_spec(),
        rows(640),
        pl.BlockSpec((16, 640), lambda i: (jnp.maximum(at(i) * (PER * SPAN // 16) - 1, 0), 0)),
        rows(HEAD, 1),
        fixed((16, 640)),
        fixed((8, 640)),
        rows(640),
        spans(ROWS, ROWS),
        spans(ROWS, HEAD),
        spans(SPAN, ROWS),
        spans(HEAD, HEAD),
        spans(SPAN, HEAD),
        spans(HEAD, HEAD),
        rows(HEAD),
        *carried_specs,
    ]
    aliases = {}
    if dy is not None:
        aliases = {len(operands): 0}
        operands.append(dy)
        in_specs.append(pl.BlockSpec(memory_space=pl.ANY))
    dy, *carried = pl.pallas_call(
        functools.partial(backward_kernel, at, offs.shape[1] - 1),
        out_shape=(
            shape((tokens, 896), LOW),
            shape((4, 8, 640), WIDE),
            shape((8, 640), WIDE),
            shape((1, HEAD), WIDE),
        ),
        grid=(steps,),
        in_specs=in_specs,
        out_specs=(rows(896), *carried_specs),
        input_output_aliases=aliases,
        compiler_params=pltpu.CompilerParams(vmem_limit_bytes=VMEM_LIMIT),
        cost_estimate=estimate(4e9 * steps, 2.6 * steps),
        name="delta_backward",
    )(*operands)
    return dy, carried


def input_blocks_kernel(at_ref, dy_ref, out_ref, w_ref, send_ref, keep_ref):
    count = dy_ref.shape[0]
    block = contract(dy_ref[...], w_ref[...], 1, 1).astype(LOW)
    for n, to_ref in enumerate((send_ref, keep_ref)):

        @pl.when(pl.program_id(0) == n)
        def _():
            to_ref[:count, :] = block
            to_ref[count:, :] = out_ref[...]


def input_blocks(places, dy, grad_out, weights, count, out_rows):
    width = weights.shape[0]
    return pl.pallas_call(
        input_blocks_kernel,
        out_shape=[jax.ShapeDtypeStruct((count + out_rows, width), LOW)] * 2,
        grid_spec=pltpu.PrefetchScalarGridSpec(
            num_scalar_prefetch=1,
            grid=(2,),
            in_specs=[
                pl.BlockSpec((count, 896), lambda i, p: (p[i], 0)),
                pl.BlockSpec((out_rows, width), lambda i, p: (p[i], 0)),
                fixed(weights.shape),
            ],
            out_specs=[fixed((count + out_rows, width))] * 2,
        ),
        compiler_params=pltpu.CompilerParams(vmem_limit_bytes=VMEM_LIMIT),
        cost_estimate=estimate(4 * count * width * 896, 4),
        name="input_blocks",
    )(jnp.stack(places).astype(jnp.int32), dy, grad_out, weights)


def weight_grads_kernel(
    taps, at_ref, low_ref, dy_ref, w_ref, gain_ref, gff_ref, gh_ref, rate_ref, taps_ref, to_ref
):
    shard = w_ref.shape[0]
    grads = contract(low_ref[...], dy_ref[...], 0, 0)
    to_ref[:shard, :] = grads.astype(LOW)
    sums = jnp.sum(grads * w_ref[...].astype(WIDE), axis=1, keepdims=True)
    row = jnp.broadcast_to(sums, (shard, HEAD)).T[0:1] / gain_ref[...]

    def wide(value):
        return jnp.concatenate(
            [value, jnp.zeros((value.shape[0], 896 - value.shape[1]), WIDE)], axis=1
        )

    to_ref[shard:, :] = stack(
        wide(row),
        wide(gff_ref[...]),
        wide(gh_ref[0]),
        wide(rate_ref[...]),
        wide(taps_ref[:taps, :]),
        jnp.zeros((12 - taps, 896), WIDE),
    ).astype(LOW)


def weight_grads(order, low, dy, weights, gain, gain_ffn, gain_head, rate, taps_grad, taps):
    length, width = low.shape
    members = order.shape[0]
    shard = width // members
    gh = jnp.pad(gain_head.reshape(members, 1, -1), ((0, 0), (0, 0), (0, HEAD)))[:, :, :HEAD]
    return pl.pallas_call(
        functools.partial(weight_grads_kernel, taps),
        out_shape=jax.ShapeDtypeStruct((members * (shard + 16), 896), LOW),
        grid_spec=pltpu.PrefetchScalarGridSpec(
            num_scalar_prefetch=1,
            grid=(members,),
            in_specs=[
                pl.BlockSpec((length, shard), lambda i, p: (0, p[i])),
                fixed((length, 896)),
                pl.BlockSpec((shard, 896), lambda i, p: (p[i], 0)),
                pl.BlockSpec((1, shard), lambda i, p: (0, p[i])),
                pl.BlockSpec((1, shard), lambda i, p: (0, p[i])),
                pl.BlockSpec((1, 1, HEAD), lambda i, p: (p[i], 0, 0)),
                fixed((1, HEAD)),
                fixed((8, 640)),
            ],
            out_specs=pl.BlockSpec((shard + 16, 896), lambda i, p: (i, 0)),
        ),
        compiler_params=pltpu.CompilerParams(vmem_limit_bytes=VMEM_LIMIT),
        cost_estimate=estimate(2 * length * width * 896, 12),
        name="weight_grads",
    )(order, low, dy, weights, gain, gain_ffn, gh, rate, taps_grad)


def pack_kernel(
    heads, taps,
    place_ref, q_ref, k0_ref, k1_ref, v0_ref, v1_ref, g_ref, beta_ref, decay_ref, gin_ref,
    gff_ref, gh_ref, cq_ref, ck_ref, cv_ref, out_ref,
):
    h = place_ref[0]
    shard = q_ref.shape[0]
    for i, ref in enumerate((q_ref, k0_ref, k1_ref, v0_ref, v1_ref, g_ref)):
        out_ref[:shard, i * HEAD : (i + 1) * HEAD] = ref[...]
    beta, decay = beta_ref[...].astype(WIDE), decay_ref[...].astype(WIDE)

    def row_of(values, at):
        row = lax.broadcasted_iota(jnp.int32, values.shape, 0)
        return jnp.sum(jnp.where(row == at, values, 0.0), axis=0, keepdims=True)

    row = lax.broadcasted_iota(jnp.int32, (HEAD, shard), 0)
    small = jnp.where(row == 0, row_of(beta, h), 0.0)
    small = jnp.where(row == 1, row_of(beta, heads + h), small)
    small = jnp.where(row == 2, row_of(decay, h), small)
    out_ref[:shard, 6 * HEAD :] = small.T.astype(LOW)
    out_ref[shard:, :] = jnp.zeros((out_ref.shape[0] - shard, out_ref.shape[1]), LOW)
    vectors = stack(
        *[ref[...].astype(WIDE) for ref in (gin_ref, gff_ref, gh_ref, cq_ref)],
        *[
            ref[:, i * shard : (i + 1) * shard].astype(WIDE)
            for ref in (ck_ref, cv_ref)
            for i in range(2)
        ],
        jnp.zeros((32 - 3 - 5 * taps, shard), WIDE),
    )
    out_ref[shard:, :shard] = vectors.astype(LOW)


def pack_weights(
    head, w_query, w_key, w_value, w_outgate, w_beta, w_decay, gain_in, gain_ffn, gain_head,
    conv_query, conv_key, conv_value,
):
    shard, heads = w_decay.shape
    taps = conv_query.shape[0]

    def part(step):
        return pl.BlockSpec((shard, HEAD), lambda i, h: (0, step * heads + h[0]))

    small = (
        w_beta.T, w_decay.T, gain_in[None], gain_ffn[None],
        jnp.pad(gain_head, (0, shard - gain_head.shape[0]))[None],
        conv_query, conv_key, conv_value,
    )
    return pl.pallas_call(
        functools.partial(pack_kernel, heads, taps),
        out_shape=jax.ShapeDtypeStruct((shard + 32, 896), LOW),
        grid_spec=pltpu.PrefetchScalarGridSpec(
            num_scalar_prefetch=1,
            grid=(1,),
            in_specs=[part(0), part(0), part(1), part(0), part(1), part(0)]
            + [fixed(a.shape) for a in small],
            out_specs=fixed((shard + 32, 896)),
        ),
        compiler_params=pltpu.CompilerParams(vmem_limit_bytes=VMEM_LIMIT),
        cost_estimate=estimate(0, 2),
        name="pack_weights",
    )(head.reshape(1), w_query, w_key, w_key, w_value, w_value, w_outgate, *small)


def project_kernel(count, place_ref, gain_ref, w_ref, *refs):
    tok_refs, (low_ref, pre_ref, gs_ref) = refs[:count], refs[count:]
    for n in range(count):

        @pl.when(pl.program_id(0) == n)
        def _():
            values = tok_refs[n][...].astype(WIDE)
            scale = lax.rsqrt(jnp.mean(values * values, axis=1, keepdims=True) + EPSILON)
            low_ref[...] = (values * scale * gain_ref[...]).astype(LOW)

    normed = low_ref[...]
    pre_ref[...] = contract(normed, w_ref[:, :640], 1, 0).astype(LOW)
    gs_ref[...] = contract(normed, w_ref[:, 640:], 1, 0)


def project(found, gain, weights):
    blocks = [one for a, x, b, y in found for one in ((a, x), (b, y))]
    places = jnp.stack([place for place, _ in blocks]).astype(jnp.int32)
    count, (rows, width) = len(blocks), blocks[0][1].shape
    shape = jax.ShapeDtypeStruct
    return pl.pallas_call(
        functools.partial(project_kernel, count),
        out_shape=[
            shape((count * rows, n), t) for n, t in ((width, LOW), (640, LOW), (256, WIDE))
        ],
        grid_spec=pltpu.PrefetchScalarGridSpec(
            num_scalar_prefetch=1,
            grid=(count,),
            in_specs=[fixed(gain.shape), fixed(weights.shape)] + [fixed((rows, width))] * count,
            out_specs=[
                pl.BlockSpec((rows, n), lambda i, p: (p[i], 0)) for n in (width, 640, 256)
            ],
        ),
        compiler_params=pltpu.CompilerParams(vmem_limit_bytes=VMEM_LIMIT),
        cost_estimate=estimate(2 * count * rows * width * 896, 13),
        name="project",
    )(places, gain, weights, *(value for _, value in blocks))


def rms_parts(values):
    return values * lax.rsqrt(jnp.mean(values * values, axis=-1, keepdims=True) + EPSILON)


def rms_back(grad_scaled, values):
    scale = lax.rsqrt(jnp.mean(values * values, axis=-1, keepdims=True) + EPSILON)
    normed = values * scale
    return scale * (
        grad_scaled - normed * jnp.mean(grad_scaled * normed, axis=-1, keepdims=True)
    )


def dot_plain(left, right, kind=WIDE):
    return jnp.dot(left, right, preferred_element_type=kind)


def dot_left(left, right, kind=WIDE):
    return contract(left, right, 0, 0).astype(kind)


def dot_right(left, right):
    return contract(left, right, 1, 1)


def exchanged(value, axis, bit):
    size = lax.axis_size(axis)
    return lax.ppermute(value, axis, [(i, i ^ bit) for i in range(size)])


def near_order(size):
    order, bit = [0], size // 2
    while bit:
        order = order + [o ^ bit for o in order]
        bit //= 2
    return order


def near_gather(value, axis, first=None):
    bit = lax.axis_size(axis) // 2
    while bit:
        value = stack(value, exchanged(value, axis, bit) if first is None else first)
        first = None
        bit //= 2
    return value


def near_scatter(value, axis):
    size, bit = lax.axis_size(axis), 1
    while bit < size:
        half = value.shape[0] // 2
        came = exchanged(value[half:].astype(LOW), axis, bit).astype(WIDE)
        value = value[:half].astype(WIDE) + came
        bit *= 2
    return value


def near_scatter_stages(value, axis, ties):
    size, bit = lax.axis_size(axis), 1
    while bit < size:
        half = value.shape[0] // 2
        value = after(value, *ties)
        came = exchanged(value[half:].astype(LOW), axis, bit)
        yield [came]
        value = value[:half].astype(WIDE) + came.astype(WIDE)
        bit *= 2
    yield value


def near_blocks(value, axis):
    size, me = lax.axis_size(axis), lax.axis_index(axis)
    return stack(
        *[lax.dynamic_index_in_dim(value, me ^ o, 0, False) for o in near_order(size)]
    )


def ordered_step(value, other, axis, bit):
    mine_first = (lax.axis_index(axis) & bit) == 0
    pair = jnp.where(mine_first, jnp.stack([value, other], 1), jnp.stack([other, value], 1))
    return pair.reshape((pair.shape[0] * 2,) + value.shape[1:])


def ordered_gather(value, axis, first=None):
    bit = lax.axis_size(axis) // 2
    value = value[None]
    while bit:
        other = exchanged(value, axis, bit) if first is None else first[None]
        value = ordered_step(value, other, axis, bit)
        first = None
        bit //= 2
    return value


def far_exchange(value, axis):
    return exchanged(value, axis, lax.axis_size(axis) // 2)


def after(value, *done):
    return lax.optimization_barrier((value, *done))[0]


def team_step(value, team, move):
    size = lax.axis_size("seq")
    pairs = [(t + i, t + move(i)) for t in range(0, size, team) for i in range(team)]
    return lax.ppermute(value, "seq", pairs)


def turn(value, team, by):
    return team_step(value, team, lambda i: (i + 2 * by) % team)


def cross(value, team):
    return team_step(value, team, lambda i: i ^ 1)


def turns(team):
    half = team // 2
    return [0] + [k for n in range(1, half // 2 + 1) for k in dict.fromkeys((n, half - n))]


def gather_stages(value, team, ties=()):
    me = lax.axis_index("seq") % team
    half = team // 2
    turned, found, before = {0: value}, [], ()
    if half > 1:
        turned[1] = turn(value, team, 1)
    if half > 2:
        turned[half - 1] = turn(after(value, turned[1]), team, -1)
    for k in turns(team):
        across = cross(after(turned[k], *before, *ties), team)
        stage = [across]
        for n in (k + 1, k - 1):
            if 0 < n < half and n not in turned and k:
                turned[n] = turn(turned[k], team, 1 if n > k else -1)
                stage.append(turned[n])
        before = (across,)
        found.append(((me - 2 * k) % team, turned[k], ((me ^ 1) - 2 * k) % team, across))
        yield stage
    yield found


def last_of(stages):
    for stage in stages:
        pass
    return stage


def team_places(team):
    me = lax.axis_index("seq") % team
    return [
        (((me ^ 1) + 2 * k) % team, (me + 2 * k) % team) for k in reversed(turns(team))
    ]


def scatter_stages(blocks, team, ties=()):
    half = team // 2
    passing, leaving, before = {}, None, ()
    for (send, keep), k in zip(blocks, reversed(turns(team))):
        came = cross(after(send, *before, *ties), team)
        stage = [came]
        if leaving is not None:
            pair, n = leaving
            forward = 2 * n <= half
            to = n - 1 if forward else (n + 1) % half
            moved = turn(pair.astype(LOW), team, 1 if forward else -1)
            stage.append(moved)
            passing[to] = passing.get(to, []) + [moved]
        yield stage
        before = (came,)
        keep = keep(came) if callable(keep) else keep
        pair = keep.astype(WIDE) + came.astype(WIDE)
        for moved in passing.pop(k, []):
            pair = pair + moved.astype(WIDE)
        leaving = (pair, k)
    yield pair


def mixer_outputs_kernel(heads, taps, fsdp, place_ref, *refs):
    got_refs, out_refs, refs = refs[:heads], refs[heads : 2 * heads], refs[2 * heads :]
    (q_ref, k_ref, v_ref, g_ref, b_ref, d_ref, gin_ref, gff_ref, gh_ref, rate_ref, cq_ref,
     ck_ref, cv_ref, out_ref) = refs
    member = place_ref[0, heads]
    shard = q_ref.shape[0]
    gains = gh_ref.shape[1]
    width = heads * HEAD
    lane_r = lax.broadcasted_iota(jnp.int32, (1, heads), 1)
    rates = jnp.zeros((1, heads), WIDE)
    vectors = jnp.zeros((8, shard), WIDE)
    for n in range(heads):
        got_ref = got_refs[n]
        h = place_ref[0, n]

        def columns(step):
            return pl.ds(pl.multiple_of(step * width + h * HEAD, HEAD), HEAD)

        q_ref[:, columns(0)] = got_ref[:shard, 0:128].astype(WIDE)
        for i in range(2):
            k_ref[:, columns(i)] = got_ref[:shard, 128 + i * 128 : 256 + i * 128].astype(WIDE)
            v_ref[:, columns(i)] = got_ref[:shard, 384 + i * 128 : 512 + i * 128].astype(WIDE)
        g_ref[:, columns(0)] = got_ref[:shard, 640:768].astype(WIDE)
        last = got_ref[:shard, 768:896].astype(WIDE).T
        b_ref[pl.ds(h, 1), :] = last[0:1]
        b_ref[pl.ds(heads + h, 1), :] = last[1:2]
        d_ref[pl.ds(h, 1), :] = last[2:3]
        extra = got_ref[shard:, :].astype(WIDE)
        vectors = vectors + extra[0:8, :shard]
        rates = jnp.where(lane_r == h, extra[3:4, 2:3], rates)
        rows = out_refs[n].shape[0]
        out_ref[pl.ds(pl.multiple_of(h * rows, rows), rows), :] = out_refs[n][...].astype(WIDE)
        for ref, at, steps in ((cq_ref, 0, 1), (ck_ref, 128, 2), (cv_ref, 384, 2)):
            per = ref.shape[1] // HEAD
            for i in range(steps):
                slot = i * heads + h - member * per

                @pl.when((slot >= 0) & (slot < per))
                def _():
                    to = pl.ds(pl.multiple_of(slot * HEAD, HEAD), HEAD)
                    ref[:, to] = extra[4 : 4 + taps, at + i * HEAD : at + (i + 1) * HEAD]

    rate_ref[...] = rates
    gin_ref[...] = vectors[0:1]
    gff_ref[...] = vectors[1:2]
    gh_ref[...] = vectors[2:3, :gains]


def mixer_outputs(found, found_out, shard, gains, taps, fsdp, member):
    found, found_out = (
        [one for a, x, b, y in pairs for one in ((a, x), (b, y))] for pairs in (found, found_out)
    )
    heads = len(found)
    places = jnp.stack([place for place, _ in found] + [member])[None].astype(jnp.int32)
    width = heads * HEAD
    shape = jax.ShapeDtypeStruct
    outs = (
        shape((shard, width), WIDE),
        shape((shard, 2 * width), WIDE),
        shape((shard, 2 * width), WIDE),
        shape((shard, width), WIDE),
        shape((2 * heads, shard), WIDE),
        shape((heads, shard), WIDE),
        shape((1, shard), WIDE),
        shape((1, shard), WIDE),
        shape((1, gains), WIDE),
        shape((1, heads), WIDE),
        shape((taps, shard), WIDE),
        shape((taps, 2 * shard), WIDE),
        shape((taps, 2 * shard), WIDE),
        shape((shard, width), WIDE),
    )
    return pl.pallas_call(
        functools.partial(mixer_outputs_kernel, heads, taps, fsdp),
        out_shape=outs,
        in_specs=[smem_spec()] + [vmem_spec()] * (2 * heads),
        out_specs=[vmem_spec()] * len(outs),
        compiler_params=pltpu.CompilerParams(vmem_limit_bytes=VMEM_LIMIT),
        cost_estimate=estimate(0, 12),
        name="mixer_outputs",
    )(places, *(value for _, value in found), *(value for _, value in found_out))


def ff_outputs_kernel(count, slab, shard, place_ref, *refs):
    got_refs, (gate_ref, up_ref, down_ref), held = refs[:count], refs[count : count + 3], refs[-1]
    own = count * slab
    for n, got_ref in enumerate(got_refs):
        at = place_ref[n] * slab
        piece = got_ref[...].astype(WIDE)
        for m in range(2):
            for k in range(2):
                to = pl.multiple_of(k * own + at, 8)
                held[m, pl.ds(to, slab), :] = piece[
                    m * slab : (m + 1) * slab, k * shard : (k + 1) * shard
                ]
        down_ref[pl.ds(pl.multiple_of(at, 8), slab), :] = piece[2 * slab :]
    gate_ref[...] = held[0].T
    up_ref[...] = held[1].T


def ff_outputs(found, slab, shard, fsdp):
    found = [one for a, x, b, y in found for one in ((a, x), (b, y))]
    count, (rows, width) = len(found), found[0][1].shape
    own = count * slab
    shape = jax.ShapeDtypeStruct
    return pl.pallas_call(
        functools.partial(ff_outputs_kernel, count, slab, shard),
        out_shape=(
            shape((shard, fsdp * own), WIDE),
            shape((shard, fsdp * own), WIDE),
            shape((own, width), WIDE),
        ),
        grid_spec=pltpu.PrefetchScalarGridSpec(
            num_scalar_prefetch=1,
            grid=(fsdp // 2,),
            in_specs=[pl.BlockSpec((rows, 2 * shard), lambda i, p: (0, i))] * count,
            out_specs=(
                pl.BlockSpec((shard, 2 * own), lambda i, p: (0, i)),
                pl.BlockSpec((shard, 2 * own), lambda i, p: (0, i)),
                pl.BlockSpec((own, 2 * shard), lambda i, p: (0, i)),
            ),
            scratch_shapes=[pltpu.VMEM((2, 2 * own, shard), WIDE)],
        ),
        compiler_params=pltpu.CompilerParams(vmem_limit_bytes=VMEM_LIMIT),
        cost_estimate=estimate(0, 15),
        name="ff_outputs",
    )(jnp.stack([p for p, _ in found]).astype(jnp.int32), *(x for _, x in found))


def ff_outputs_plain(got, slab, shard, fsdp):
    seq, rows, width = got.shape
    own = seq * slab
    wide = got.astype(WIDE)

    def turned(at):
        part = wide[:, at : at + slab].reshape(seq, slab, fsdp, shard)
        return jnp.transpose(part, (3, 2, 0, 1)).reshape(shard, fsdp * own)

    return turned(0), turned(slab), wide[:, 2 * slab :].reshape(own, width)


def per_device(
    tokens, cotangent, offsets, gain_in, w_query, w_key, w_value, w_beta, w_decay, w_outgate,
    conv_query, conv_key, conv_value, decay_scale, gain_head, w_out, gain_ffn, w_gate, w_up,
    w_down,
):
    seq, fsdp = lax.axis_size("seq"), lax.axis_size("fsdp")
    heads = decay_scale.shape[0]
    taps = conv_query.shape[0]
    own_rows = tokens.shape[1]
    shard = w_query.shape[0]
    width = shard * fsdp
    teams = seq // heads
    assert teams * heads == seq and width == heads * HEAD
    place = lax.axis_index("seq")
    head, team = place % heads, place // heads
    member = lax.axis_index("fsdp")
    if teams == 1:
        team_groups, head_groups = None, None
    else:
        team_groups = [[t * heads + h for h in range(heads)] for t in range(teams)]
        head_groups = [[t * heads + h for t in range(teams)] for h in range(heads)]

    def gather_rows(value):
        return lax.all_gather(value, "fsdp", axis=0, tiled=True)

    start_ties = []
    spread = gather_stages(tokens[0], heads, start_ties)
    came = next(spread)[:1]
    length = heads * own_rows

    def column_blocks(value):
        return jnp.transpose(value.reshape(shard, fsdp, value.shape[1] // fsdp), (1, 0, 2))

    packed = pack_weights(
        head, after(w_query, came[0]), w_key, w_value, w_outgate, w_beta, w_decay, gain_in,
        gain_ffn, gain_head, conv_query, conv_key, conv_value,
    )
    far_packed = far_exchange(packed, "fsdp")
    start_ties[:] = [packed]
    came += next(spread)[:1]
    columns = jnp.stack(
        [column_blocks(after(w_gate, came[1])), column_blocks(after(w_up, came[1]))], axis=1
    )
    others = near_order(fsdp)[1:]
    column_sends = [lax.dynamic_index_in_dim(columns, member ^ o, 0, False) for o in others]
    start_ties[:] = [far_packed]
    came += next(spread)[:1]
    far_out = far_exchange(after(w_out, far_packed), "fsdp")
    got = ordered_gather(packed, "fsdp", far_packed)
    start_ties[:] = [got, far_out, *column_sends]
    for stage in spread:
        found = stage
        came += stage[:1]
    came = [one for one in came if not isinstance(one, tuple)]
    came += [came[-1]] * 3
    full_packed = got[:, :shard].reshape(width, 896)
    vectors = got[:, shard:, :shard]
    full_gain_in = vectors[:, 0].reshape(width).astype(WIDE)
    full_gain_ffn = vectors[:, 1].reshape(width).astype(WIDE)
    full_gain_head = vectors[:, 2, : gain_head.shape[0]].reshape(1, HEAD).astype(WIDE)

    def head_taps_of(row, pieces, step):
        column = step * width + head * HEAD
        inside = column % (pieces * shard)
        at = (column // (pieces * shard), row + inside // shard * taps, inside % shard)
        return lax.dynamic_slice(vectors, at, (1, taps, HEAD))[0]

    head_taps = jnp.concatenate(
        [head_taps_of(3, 1, 0)]
        + [head_taps_of(3 + taps, 2, i) for i in range(2)]
        + [head_taps_of(3 + 3 * taps, 2, i) for i in range(2)],
        axis=1,
    ).astype(WIDE)
    head_taps = jnp.pad(head_taps, ((0, 8 - taps), (0, 0)))
    def column_blocks(value):
        return jnp.transpose(value.reshape(shard, fsdp, value.shape[1] // fsdp), (1, 0, 2))

    cot = after(cotangent[0], came[2])
    far_cot = far_exchange(cot, "fsdp")
    column_got = [
        exchanged(after(send, came[2]), "fsdp", o) for o, send in zip(others, column_sends)
    ]
    normed_low, pre, gate_small = project(found, full_gain_in[None], full_packed)
    offs = jnp.concatenate(
        [offsets, jnp.broadcast_to(team * length, (1, 1)).astype(jnp.int32)], axis=1
    )
    rate = lax.dynamic_slice_in_dim(decay_scale, head, 1).reshape(1, 1)
    zero_state = jnp.zeros((HEAD, HEAD), WIDE)
    if teams == 1:
        edge = jnp.zeros((16, 640), LOW)
    else:
        forth = [(i, i + heads) for i in range(seq - heads)]
        back = [(i + heads, i) for i in range(seq - heads)]
        edge = lax.ppermute(pre[-16:], "seq", forth)

    def forward_from(state):
        return run_forward(
            offs, rate, pre, gate_small, edge, head_taps, full_gain_head, state
        )

    state_in = zero_state
    if teams > 1:
        trial = forward_from(zero_state)
        steps, end = trial[4].astype(WIDE) + trial[5].astype(WIDE), trial[10]

        def along(c, total):
            return jnp.dot(total, steps[c].T, precision=lax.Precision.HIGHEST)

        whole_map = lax.fori_loop(0, steps.shape[0], along, jnp.eye(HEAD, dtype=WIDE))
        for _ in range(teams - 1):
            out = jnp.dot(state_in, whole_map, precision=lax.Precision.HIGHEST) + end
            state_in = lax.ppermute(out.astype(LOW), "seq", forth).astype(WIDE)
    conv, inverse, scores, reach, high, rest, gated, mixed, upd, states, _ = forward_from(state_in)
    gated, far_out, far_cot, *column_got = lax.optimization_barrier(
        (gated, far_out, far_cot, *column_got)
    )
    own_columns = lax.dynamic_index_in_dim(columns, member, 0, False)
    full_out = ordered_gather(w_out, "fsdp", far_out).reshape(width, width)
    group_cot = near_gather(cot, "fsdp", far_cot)

    def ordered_columns(which):
        value = jnp.zeros((width, own_columns.shape[2]), LOW)
        for o, rows in zip([0, *others], [own_columns, *column_got]):
            value = lax.dynamic_update_slice(value, rows[which], ((member ^ o) * shard, 0))
        return value

    cols_gate, cols_up = ordered_columns(0), ordered_columns(1)

    gated_own = lax.all_to_all(
        gated, "seq", 0, 1, tiled=True, axis_index_groups=team_groups
    )
    inputs = tokens[0].astype(WIDE)
    mixer_res = inputs + dot_plain(gated_own, full_out)

    mid_normed = rms_parts(mixer_res)
    mid_low = (mid_normed * full_gain_ffn).astype(LOW)
    group_mid = near_gather(mid_low, "fsdp")
    gate_pre = dot_plain(group_mid, cols_gate)
    up_pre = dot_plain(group_mid, cols_up)
    sig = jax.nn.sigmoid(gate_pre)
    act = gate_pre * sig
    hidden = (act * up_pre).astype(LOW)
    grad_hidden = dot_right(group_cot, w_down)
    grad_gate_pre = (grad_hidden * up_pre * (sig * (1.0 + gate_pre * (1.0 - sig)))).astype(LOW)
    grad_up_pre = (grad_hidden * act).astype(LOW)
    grad_mid = dot_right(grad_gate_pre, cols_gate) + dot_right(grad_up_pre, cols_up)
    grad_gate_pre, grad_up_pre, grad_mid = lax.optimization_barrier(
        (grad_gate_pre, grad_up_pre, grad_mid)
    )
    grad_mid = near_scatter(grad_mid, "fsdp")

    grad_res = cotangent[0].astype(WIDE) + rms_back(grad_mid * full_gain_ffn, mixer_res)
    grad_gain_ffn = jnp.sum(grad_mid * mid_normed, axis=0)
    res_low = grad_res.astype(LOW)
    grad_gated = dot_right(res_low, full_out).astype(LOW)
    own_ff = w_down.shape[0]
    slab = own_ff // seq
    slabs = jnp.concatenate(
        [
            dot_left(grad_gate_pre, group_mid, LOW).reshape(seq, slab, width),
            dot_left(grad_up_pre, group_mid, LOW).reshape(seq, slab, width),
            dot_left(hidden, group_cot, LOW).reshape(seq, slab, width),
        ],
        axis=1,
    )
    permuted = teams == 1 and slab % 8 == 0 and own_ff * 2 % HEAD == 0 and fsdp % 2 == 0

    def turned_columns(summed):
        turned = lax.all_to_all(summed[: 2 * slab], "fsdp", 1, 1, tiled=True)
        return stack(turned, summed[2 * slab :])

    def feed_forward_sums():
        if not permuted:
            summed = lax.psum_scatter(
                slabs.reshape(seq * 3 * slab, width), "seq", scatter_dimension=0, tiled=True
            )
            yield [summed]
            slabs_done = lax.all_gather(turned_columns(summed), "seq", axis=0)
            yield ff_outputs_plain(slabs_done, slab, shard, fsdp)
            return
        def kept(at):
            return lambda came: lax.dynamic_index_in_dim(after(slabs, came), at, 0, False)

        blocks = [
            (lax.dynamic_index_in_dim(slabs, send, 0, False), kept(keep))
            for send, keep in team_places(heads)
        ]
        for stage in scatter_stages(blocks, heads, ties):
            if isinstance(stage, list):
                yield stage
        mine = turned_columns(after(stage.astype(LOW), *ties))
        yield [mine]
        for stage in gather_stages(mine, heads, ties):
            if isinstance(stage[0], tuple):
                break
            yield stage
        yield ff_outputs(stage, slab, shard, fsdp)

    ties, sums = [], feed_forward_sums()
    brought = [next(sums)]

    def beside(value):
        if not isinstance(brought[-1], tuple):
            ties[:] = [value]
            brought.append(next(sums))

    def settled(value):
        stage = brought[-1]
        return value if isinstance(stage, tuple) else after(value, *stage)

    dgated = lax.all_to_all(
        grad_gated, "seq", 1, 0, tiled=True, axis_index_groups=team_groups
    )
    grad_out = dot_left(after(gated_own, grad_gated), res_low, LOW).reshape(fsdp, shard, width)
    late = near_blocks(grad_out, "fsdp")
    dgated, late = lax.optimization_barrier((dgated, late))
    beside(dgated)
    late_ties = []
    late = near_scatter_stages(late, "fsdp", late_ties)
    late_stage = []

    def gate_back_from(dend):
        return run_gate_back(
            gate_small, full_gain_head, mixed, reach, high, rest, dgated, dend
        )

    dend = zero_state
    if teams > 1:
        begin = gate_back_from(zero_state)[4]
        for _ in range(teams - 1):
            out = lax.dot_general(
                dend, whole_map, (((1,), (1,)), ((), ())), precision=lax.Precision.HIGHEST
            )
            dend = lax.ppermute((out + begin).astype(LOW), "seq", back).astype(WIDE)
    do, ds, dgate, dgain, _ = gate_back_from(dend)
    carried = [
        jnp.zeros((4, 8, 640), WIDE), jnp.zeros((8, 640), WIDE), jnp.zeros((1, HEAD), WIDE)
    ]
    dy, calls = None, 2
    left = length // (PER * SPAN)
    for call in range(calls, 0, -1):
        steps_here = -(-left // call)
        if dy is None:
            carried[0] = after(carried[0], do)
        carried[0] = settled(after(carried[0], *late_stage))
        beside(carried[0])
        late_ties[:] = [carried[0]]
        late_stage = next(late)
        late_stage = late_stage if isinstance(late_stage, list) else [late_stage]
        dy, carried = run_backward(
            left - 1, steps_here, offs, rate, pre, gate_small, edge, head_taps,
            (conv, inverse, upd, scores, states, do, ds, dgate), carried, dy,
        )
        carried = list(carried)
        left -= steps_here
    dy = settled(dy)
    late_stage = late_stage[0]
    for stage in late:
        late_stage = stage
    grad_out = late_stage.astype(LOW)
    following, dtaps, drate = carried
    if teams > 1:
        none = jnp.zeros((16, 640), WIDE)
        dedge = sum(stack(none, following[lag])[lag : lag + 16] for lag in range(1, 4))
        from_next = lax.ppermute(dedge.astype(LOW), "seq", back).astype(WIDE)
        tail = (dy[-16:, :640].astype(WIDE) + from_next).astype(LOW)
        dy = lax.dynamic_update_slice(dy, tail, (length - 16, 0))

    out_rows = shard // heads

    blocks = [
        list(input_blocks(places, dy, grad_out, full_packed, own_rows, out_rows))
        for places in team_places(heads)
    ]
    turned_stage = []
    if not isinstance(brought[-1], tuple):
        beside(blocks[0][0])
        turned_stage = brought[-1] if isinstance(brought[-1], list) else []
    order = jnp.stack([member ^ o for o in near_order(fsdp)]).astype(jnp.int32)
    combined = weight_grads(
        order, normed_low, after(dy, blocks[0][0], *turned_stage), full_packed, full_gain_in[None],
        grad_gain_ffn[None], dgain, drate, dtaps, taps,
    )
    blocks = [
        (send if n == 0 else after(send, combined), keep)
        for n, (send, keep) in enumerate(blocks)
    ]
    near = near_scatter_stages(combined, "fsdp", [])
    near_stage = next(near)
    tail_ties = []
    sent = scatter_stages(blocks, heads, tail_ties)
    queue = [next(sent)[0]]
    joined = None
    while joined is None or not isinstance(brought[-1], tuple):
        if not isinstance(brought[-1], tuple):
            beside(queue[-1])
            if isinstance(brought[-1], list):
                queue.append(brought[-1][0])
        if joined is None:
            tail_ties[:] = [queue[-1]]
            if len(queue) == 2 and isinstance(near_stage, list):
                tail_ties += near_stage
            stage = next(sent)
            if isinstance(stage, list):
                queue.append(stage[0])
            else:
                joined = stage
    for near_stage in near:
        pass
    combined = after(near_stage.astype(LOW), queue[-1])
    out_gate, out_up, out_down = brought[-1]
    down_part = near_scatter(dot_plain(after(hidden, queue[1]), w_down).astype(LOW), "fsdp")
    layer_out = (mixer_res + down_part).astype(LOW)
    grad_normed, own_out = joined[:own_rows], joined[own_rows:].astype(LOW)
    input_grad = (grad_res + rms_back(grad_normed * full_gain_in, inputs)).astype(LOW)
    if teams > 1:
        own_out = lax.psum(own_out, "seq", axis_index_groups=head_groups)
    found_out = last_of(gather_stages(own_out, heads))

    if teams > 1:
        combined = lax.psum(combined, "seq", axis_index_groups=head_groups)
    (out_query, out_key, out_value, out_gatew, out_beta, out_decay, out_gain_in, out_gain_ffn,
     out_gain_head, out_rate, out_cq, out_ck, out_cv, out_out) = mixer_outputs(
        last_of(gather_stages(combined, heads)), found_out, shard, gain_head.shape[0], taps, fsdp, member
    )

    return (
        layer_out[None],
        input_grad[None],
        out_gain_in[0],
        out_query,
        out_key,
        out_value,
        out_beta.T,
        out_decay.T,
        out_gatew,
        out_cq,
        out_ck,
        out_cv,
        out_rate[0],
        out_gain_head[0],
        out_out,
        out_gain_ffn[0],
        out_gate,
        out_up,
        out_down,
    )


def solution(mesh):
    rows, lanes = P("fsdp", None), P(None, "fsdp")
    block = P("fsdp", "seq", None)
    return jax.shard_map(
        per_device,
        mesh=mesh,
        in_specs=(
            block, block, rows, P("fsdp"), rows, rows, rows, rows, rows, rows,
            lanes, lanes, lanes, P(), P("fsdp"), rows, P("fsdp"), rows, rows, rows,
        ),
        out_specs=(
            block, block, P("fsdp"), rows, rows, rows, rows, rows, rows,
            lanes, lanes, lanes, P(), P("fsdp"), rows, P("fsdp"), rows, rows, rows,
        ),
        check_vma=False,
    )
```

```python
import functools

import jax
import jax.numpy as jnp
from jax import lax
from jax.experimental import pallas as pl
from jax.experimental.pallas import tpu as pltpu
from jax.sharding import PartitionSpec as P

SPAN = 64
PER = 4
ROWS = 128
HEAD = 128
EPSILON = 1e-06
LOW = jnp.bfloat16
WIDE = jnp.float32
VMEM_LIMIT = 56 * 1024 * 1024


def contract(left, right, left_dim, right_dim):
    return lax.dot_general(
        left, right, (((left_dim,), (right_dim,)), ((), ())), preferred_element_type=WIDE
    )


def halves(value):
    high = value.astype(LOW)
    return high, (value - high.astype(WIDE)).astype(LOW)


def mm(left, right, left_dim=1, right_dim=0):
    return contract(left.astype(LOW), right.astype(LOW), left_dim, right_dim)


def stack(*parts):
    return jnp.concatenate(parts, axis=0)


def row_maps():
    row = lax.broadcasted_iota(jnp.int32, (ROWS, ROWS), 0)
    col = lax.broadcasted_iota(jnp.int32, (ROWS, ROWS), 1)
    tok, step = row & (SPAN - 1), row >> 6
    tok_c, step_c = col & (SPAN - 1), col >> 6
    return tok, step, tok_c, step_c


def span_tokens(offs_ref, doc_count, first):
    place = first + lax.broadcasted_iota(jnp.int32, (SPAN, 1), 0)
    begin = jnp.zeros((SPAN, 1), jnp.int32)
    for j in range(doc_count):
        start = offs_ref[0, j]
        begin = jnp.where(place >= start, start, begin)
    return place - begin


def softplus(value):
    return jnp.maximum(value, 0.0) + jnp.log1p(jnp.exp(-jnp.abs(value)))


def decay_sums(small, rate):
    logs = -rate * softplus(small)
    tok = lax.broadcasted_iota(jnp.int32, (SPAN, SPAN), 0)
    tok_c = lax.broadcasted_iota(jnp.int32, (SPAN, SPAN), 1)
    lower = jnp.where(tok >= tok_c, 1.0, 0.0).astype(LOW)
    tok_w = lax.broadcasted_iota(jnp.int32, (SPAN, ROWS), 0)
    tok_wc = lax.broadcasted_iota(jnp.int32, (SPAN, ROWS), 1) & (SPAN - 1)
    upper = jnp.where(tok_w <= tok_wc, 1.0, 0.0).astype(LOW)
    high, rest = halves(logs)
    cols = contract(lower, high, 1, 0) + contract(lower, rest, 1, 0)
    rows = contract(high, upper, 0, 0) + contract(rest, upper, 0, 0)
    return cols[:, 2:3], rows[2:3, :]


def unit(values):
    scale = lax.rsqrt(jnp.sum(values * values, axis=1, keepdims=True) + EPSILON)
    return values * scale, scale


def span_factors(small, rate, pos):
    sig = jax.nn.sigmoid(small)
    cum, cum_row = decay_sums(small, rate)
    beta = stack(sig[:, 0:1], sig[:, 1:2])
    cum2, pos2 = stack(cum, cum), stack(pos, pos)
    tok, step, tok_c, step_c = row_maps()
    before = tok > tok_c
    here = tok == tok_c
    reach = (before | (here & (step >= step_c))) & (tok - tok_c <= pos2)
    decay = jnp.where(reach, jnp.exp(jnp.where(reach, cum2 - cum_row, 0.0)), 0.0)
    strict = before | (here & (step > step_c))
    tok1 = tok[:, 0:1]
    carry = jnp.where(pos2 > tok1, jnp.exp(cum2), 0.0)
    end, end_pos = cum[SPAN - 1 : SPAN], pos[SPAN - 1 : SPAN]
    leave = jnp.where(SPAN - 1 - tok1 <= end_pos, jnp.exp(end - cum2), 0.0)
    carry_all = jnp.where(end_pos >= SPAN, jnp.exp(end), 0.0)
    return beta, decay, strict, carry, leave, carry_all, tok ^ tok_c


def in_turns(bodies):
    bodies = list(bodies)
    while bodies:
        bodies = [body for body in bodies if next(body, "end") != "end"]


def unit_lower_inverse(strict_part, apart):
    row = lax.broadcasted_iota(jnp.int32, (ROWS, ROWS), 0)
    col = lax.broadcasted_iota(jnp.int32, (ROWS, ROWS), 1)
    inverse = jnp.where(row == col, 1.0, 0.0) - jnp.where(apart == 0, strict_part, 0.0)
    for level in range(6):
        block = jnp.where((apart >> level) == 1, strict_part, 0.0)
        low = inverse.astype(LOW)
        half = contract(low, block.astype(LOW), 1, 0).astype(LOW)
        yield
        inverse = inverse - contract(half, low, 1, 0)
        yield
    return inverse


def conv_rows(prior, here):
    return stack(prior.astype(WIDE), here.astype(WIDE))


def forward_kernel(
    span_count, doc_count, group,
    offs_ref, rate_ref, pre_ref, prior_ref, small_ref, gate_ref, edge_ref, taps_ref, gain_ref,
    state_ref,
    conv_ref, t_ref, sc_ref, qh_ref, ah_ref, al_ref, gated_ref, mixed_ref, u_ref, s_ref, end_ref,
    w_scr, u0_scr, b_scr, o0_scr, ah_scr, al_scr, qh_scr,
):
    step = pl.program_id(0)
    base = offs_ref[0, doc_count]
    rate = rate_ref[0, 0]
    prior = jnp.where(step == 0, edge_ref[...].astype(WIDE), prior_ref[...].astype(WIDE))

    def local(u):
        c = step * group + u
        here = pre_ref[u * SPAN : (u + 1) * SPAN, :].astype(WIDE)
        if u:
            before = pre_ref[u * SPAN - 16 : u * SPAN, :].astype(WIDE)
        else:
            before = prior
        rows = stack(before, here)
        pos = span_tokens(offs_ref, doc_count, base + c * SPAN)
        conv = taps_ref[0:1, :] * here
        for lag in range(1, 4):
            shifted = rows[16 - lag : 16 - lag + SPAN]
            conv = conv + jnp.where(pos >= lag, taps_ref[lag : lag + 1, :] * shifted, 0.0)
        conv_ref[u * SPAN : (u + 1) * SPAN, :] = conv
        yield
        act = conv * jax.nn.sigmoid(conv)
        query, _ = unit(act[:, 0:128])
        key0, _ = unit(act[:, 128:256])
        key1, _ = unit(act[:, 256:384])
        keys = stack(key0, key1)
        values = stack(act[:, 384:512], act[:, 512:640])
        small = small_ref[u * SPAN : (u + 1) * SPAN, :]
        beta, decay, strict, carry, leave, carry_all, apart = span_factors(small, rate, pos)
        yield
        inner = mm(keys, keys, 1, 1)
        yield
        inverse = yield from unit_lower_inverse(
            jnp.where(strict, beta * decay * inner, 0.0), apart
        )
        t_ref[u] = inverse.astype(LOW)
        both = mm(inverse, jnp.concatenate([(beta * carry) * keys, beta * values], axis=1))
        yield
        weight, fresh = both[:, :HEAD], both[:, HEAD:]
        w_scr[c] = weight.astype(LOW)
        u0_scr[c] = fresh
        leaving = (keys * leave).astype(LOW)
        row = lax.broadcasted_iota(jnp.int32, (HEAD, HEAD), 0)
        col = lax.broadcasted_iota(jnp.int32, (HEAD, HEAD), 1)
        step_map = jnp.where(row == col, carry_all, 0.0) - mm(leaving, weight, 0, 0)
        map_high, map_rest = halves(step_map)
        ah_ref[u], al_ref[u] = map_high, map_rest
        ah_scr[c], al_scr[c] = map_high, map_rest
        yield
        b_scr[c] = mm(fresh, leaving, 0, 0)
        yield
        scores = mm(query, keys, 1, 1) * decay[SPAN:, :]
        yield
        sc_ref[u] = scores.astype(LOW)
        mixed_both = mm(scores, both)
        yield
        reach = (carry[SPAN:] * query - mixed_both[:, :HEAD]).astype(LOW)
        qh_ref[u] = reach
        qh_scr[c] = reach
        o0_scr[c] = mixed_both[:, HEAD:]

    in_turns(local(u) for u in range(group))

    def chain(i, state):
        for u in range(4):
            c = i * 4 + u
            s_ref[c] = state
            high, rest = halves(state)
            state = (
                contract(high, ah_scr[c], 1, 1)
                + contract(high, al_scr[c], 1, 1)
                + contract(rest, ah_scr[c], 1, 1)
                + b_scr[c]
            )
        return state

    def mixing(c):
        low = s_ref[c].astype(LOW)
        u_ref[c] = (u0_scr[c] - contract(w_scr[c], low, 1, 1)).astype(LOW)
        yield
        mixed = o0_scr[c] + contract(qh_scr[c], low, 1, 1)
        yield
        lo = pl.multiple_of(c * SPAN, SPAN)
        mixed_ref[pl.ds(lo, SPAN), :] = mixed
        scale = lax.rsqrt(jnp.mean(mixed * mixed, axis=1, keepdims=True) + EPSILON)
        yield
        gate = gate_ref[pl.ds(lo, SPAN), :]
        gated_ref[pl.ds(lo, SPAN), :] = (
            mixed * scale * gain_ref[...] * (gate * jax.nn.sigmoid(gate))
        ).astype(LOW)
        yield

    def mixing_step(i, none):
        in_turns(mixing(i * 8 + u) for u in range(8))
        return none

    @pl.when(step == pl.num_programs(0) - 1)
    def _():
        end_ref[...] = lax.fori_loop(0, span_count // 4, chain, state_ref[...])
        lax.fori_loop(0, span_count // 8, mixing_step, 0)


def gate_back_kernel(
    span_count,
    gate_ref, gain_ref, mixed_ref, qh_ref, ah_ref, al_ref, dgated_ref, dend_ref,
    do_ref, ds_ref, dgate_ref, dgain_ref, dbegin_ref,
    f_scr,
):
    dgain_ref[...] = jnp.zeros_like(dgain_ref)

    def gate_back(c):
        lo = pl.multiple_of(c * SPAN, SPAN)
        mixed = mixed_ref[pl.ds(lo, SPAN), :]
        gate = gate_ref[pl.ds(lo, SPAN), :]
        scale = lax.rsqrt(jnp.mean(mixed * mixed, axis=1, keepdims=True) + EPSILON)
        normed = mixed * scale
        yield
        sig = jax.nn.sigmoid(gate)
        grad = dgated_ref[pl.ds(lo, SPAN), :].astype(WIDE)
        by_gain = grad * normed
        dgate_ref[pl.ds(lo, SPAN), :] = (
            by_gain * gain_ref[...] * (sig * (1.0 + gate * (1.0 - sig)))
        ).astype(LOW)
        dgain_ref[...] += jnp.sum(by_gain * (gate * sig), axis=0, keepdims=True)
        yield
        dn = grad * (gate * sig) * gain_ref[...]
        dmixed = scale * (dn - normed * jnp.mean(dn * normed, axis=1, keepdims=True))
        do_low = dmixed.astype(LOW)
        do_ref[c] = do_low
        yield
        f_scr[c] = contract(do_low, qh_ref[c], 0, 0)

    def gate_step(i, none):
        in_turns(gate_back(i * 8 + u) for u in range(8))
        return none

    lax.fori_loop(0, span_count // 8, gate_step, 0)

    def chain_step(i, grad):
        for u in range(4):
            c = span_count - 1 - (i * 4 + u)
            ds_ref[c] = grad
            high, rest = halves(grad)
            grad = (
                contract(high, ah_ref[c], 1, 0)
                + contract(high, al_ref[c], 1, 0)
                + contract(rest, ah_ref[c], 1, 0)
                + f_scr[c]
            )
        return grad

    dbegin_ref[...] = lax.fori_loop(0, span_count // 4, chain_step, dend_ref[...])


def backward_kernel(
    at_block, doc_count,
    offs_ref, rate_ref, pre_ref, prior_ref, small_ref, edge_ref, taps_ref,
    conv_ref, t_ref, u_ref, sc_ref, s_ref, do_ref, ds_ref, dgate_ref,
    next_in, dtaps_in, drate_in, *refs,
):
    dy_ref, next_ref, dtaps_ref, drate_ref = refs[-4:]
    block = at_block(pl.program_id(0))
    base = offs_ref[0, doc_count]
    rate = rate_ref[0, 0]

    @pl.when(pl.program_id(0) == 0)
    def _():
        next_ref[...] = next_in[...]
        dtaps_ref[...] = dtaps_in[...]
        drate_ref[...] = drate_in[...]

    dy_ref[:, 640:768] = dgate_ref[...]

    def local(n):
        lo, hi = n * SPAN, (n + 1) * SPAN
        pos = span_tokens(offs_ref, doc_count, base + block * PER * SPAN + lo)
        conv = conv_ref[lo:hi, :]
        sig = jax.nn.sigmoid(conv)
        act = conv * sig
        query, scale_q = unit(act[:, 0:128])
        key0, scale_0 = unit(act[:, 128:256])
        key1, scale_1 = unit(act[:, 256:384])
        yield
        keys = stack(key0, key1)
        values = stack(act[:, 384:512], act[:, 512:640])
        small = small_ref[lo:hi, :]
        beta, decay, strict, carry, leave, carry_all, _ = span_factors(small, rate, pos)
        yield
        state, dstate = s_ref[n], ds_ref[n]
        state_l, dstate_l = state.astype(LOW), dstate.astype(LOW)
        upd, out_grad, keys_l = u_ref[n], do_ref[n], keys.astype(LOW)
        dupd = contract(sc_ref[n], out_grad, 0, 0) + mm(keys * leave, dstate_l, 1, 1)
        yield
        dtarget = mm(t_ref[n], dupd, 0, 0)
        yield
        pair = stack(dtarget.astype(LOW), out_grad)
        by_upd = contract(pair, upd, 1, 1)
        by_state = contract(pair, state_l, 1, 0)
        yield
        dinner = jnp.where(strict, -by_upd[:ROWS] * decay, 0.0)
        dscore = by_upd[ROWS:] * decay[SPAN:, :]
        both = stack(dinner, dscore).astype(LOW)
        reading = contract(both, keys_l, 1, 0)
        yield
        read_key = reading[:ROWS] - carry * by_state[:ROWS]
        dquery = reading[ROWS:] + carry[SPAN:] * by_state[ROWS:]
        dleave = leave * contract(upd, dstate_l, 1, 0)
        write_key = contract(both, stack(beta * keys, query).astype(LOW), 0, 0) + dleave
        yield
        key_read = jnp.sum(keys * read_key, axis=1, keepdims=True)
        dbeta = jnp.sum(dtarget * values, axis=1, keepdims=True) + key_read
        dcum = beta * key_read - jnp.sum(keys * write_key, axis=1, keepdims=True)
        dcum = dcum[:SPAN] + dcum[SPAN:] + jnp.sum(query * dquery, axis=1, keepdims=True)
        through = jnp.sum(keys * dleave, axis=0, keepdims=True) + carry_all * jnp.sum(
            dstate * state, axis=0, keepdims=True
        )
        through = jnp.sum(through, axis=1, keepdims=True)
        tok1 = lax.broadcasted_iota(jnp.int32, (SPAN, 1), 0)
        dcum = dcum + jnp.where(tok1 == SPAN - 1, through, 0.0)
        tok = lax.broadcasted_iota(jnp.int32, (SPAN, SPAN), 0)
        tok_c = lax.broadcasted_iota(jnp.int32, (SPAN, SPAN), 1)
        upper = jnp.where(tok <= tok_c, 1.0, 0.0).astype(LOW)
        high, rest = halves(jnp.broadcast_to(dcum, (SPAN, 128)))
        dlog = contract(upper, high, 1, 0) + contract(upper, rest, 1, 0)
        yield
        soft = softplus(small)
        sig_small = jax.nn.sigmoid(small)
        lane = lax.broadcasted_iota(jnp.int32, (SPAN, 128), 1)
        drate_ref[...] += jnp.sum(jnp.where(lane == 2, -dlog * soft, 0.0), axis=0, keepdims=True)
        dsig = jnp.where(lane == 0, dbeta[:SPAN], dbeta[SPAN:]) * sig_small * (1.0 - sig_small)
        dsmall = jnp.where(lane < 2, dsig, jnp.where(lane == 2, -rate * dlog * sig_small, 0.0))
        dy_ref[lo:hi, 768:896] = dsmall.astype(LOW)
        yield
        dkey = beta * read_key + write_key
        dvalue = beta * dtarget

        def unit_back(grad, normed, scale):
            return scale * (grad - normed * jnp.sum(grad * normed, axis=1, keepdims=True))

        dact = jnp.concatenate(
            [
                unit_back(dquery, query, scale_q),
                unit_back(dkey[:SPAN], key0, scale_0),
                unit_back(dkey[SPAN:], key1, scale_1),
                dvalue[:SPAN],
                dvalue[SPAN:],
            ],
            axis=1,
        )
        dconv = dact * (sig * (1.0 + conv * (1.0 - sig)))
        yield
        here = pre_ref[lo:hi, :].astype(WIDE)
        if n:
            prior = pre_ref[lo - 16 : lo, :].astype(WIDE)
        else:
            prior = jnp.where(
                block == 0, edge_ref[...].astype(WIDE), prior_ref[...].astype(WIDE)
            )
        rows = stack(prior, here)
        dpre = taps_ref[0:1, :] * dconv
        dtaps_ref[0:1, :] += jnp.sum(dconv * here, axis=0, keepdims=True)
        for lag in range(1, 4):
            kept = jnp.where(pos >= lag, dconv, 0.0)
            shifted = rows[16 - lag : 16 - lag + SPAN]
            dtaps_ref[lag : lag + 1, :] += jnp.sum(kept * shifted, axis=0, keepdims=True)
            kept = kept * taps_ref[lag : lag + 1, :]
            dpre = dpre + stack(kept, next_ref[lag])[lag : lag + SPAN]
            next_ref[lag] = kept[0:8]
        dy_ref[lo:hi, 0:640] = dpre.astype(LOW)

    in_turns(local(n) for n in reversed(range(PER)))


def vmem_spec():
    return pl.BlockSpec(memory_space=pltpu.VMEM)


def smem_spec():
    return pl.BlockSpec(memory_space=pltpu.SMEM)


def fixed(shape):
    return pl.BlockSpec(shape, lambda *_: (0,) * len(shape))


def estimate(flops, mib):
    return pl.CostEstimate(flops=int(flops), bytes_accessed=int(mib * 2**20), transcendentals=0)


def run_forward(offs, rate, pre, gs, edge, taps, gain, state):
    tokens = pre.shape[0]
    spans = tokens // SPAN
    group = 8
    shape = jax.ShapeDtypeStruct
    outs = (
        (shape((tokens, 640), WIDE), pl.BlockSpec((group * SPAN, 640), lambda i: (i, 0))),
        (shape((spans, ROWS, ROWS), LOW), pl.BlockSpec((group, ROWS, ROWS), lambda i: (i, 0, 0))),
        (shape((spans, SPAN, ROWS), LOW), pl.BlockSpec((group, SPAN, ROWS), lambda i: (i, 0, 0))),
        (shape((spans, SPAN, HEAD), LOW), pl.BlockSpec((group, SPAN, HEAD), lambda i: (i, 0, 0))),
        (shape((spans, HEAD, HEAD), LOW), pl.BlockSpec((group, HEAD, HEAD), lambda i: (i, 0, 0))),
        (shape((spans, HEAD, HEAD), LOW), pl.BlockSpec((group, HEAD, HEAD), lambda i: (i, 0, 0))),
        (shape((tokens, HEAD), LOW), fixed((tokens, HEAD))),
        (shape((tokens, HEAD), WIDE), fixed((tokens, HEAD))),
        (shape((spans, ROWS, HEAD), LOW), fixed((spans, ROWS, HEAD))),
        (shape((spans, HEAD, HEAD), WIDE), fixed((spans, HEAD, HEAD))),
        (shape((HEAD, HEAD), WIDE), fixed((HEAD, HEAD))),
    )
    return pl.pallas_call(
        functools.partial(forward_kernel, spans, offs.shape[1] - 1, group),
        out_shape=[o for o, _ in outs],
        grid=(spans // group,),
        in_specs=[
            smem_spec(),
            smem_spec(),
            pl.BlockSpec((group * SPAN, 640), lambda i: (i, 0)),
            pl.BlockSpec((16, 640), lambda i: (jnp.maximum(i * (group * SPAN // 16) - 1, 0), 0)),
            pl.BlockSpec((group * SPAN, HEAD), lambda i: (i, 1)),
            fixed((tokens, HEAD)),
            fixed((16, 640)),
            fixed((8, 640)),
            fixed((1, HEAD)),
            fixed((HEAD, HEAD)),
        ],
        out_specs=[b for _, b in outs],
        scratch_shapes=[
            pltpu.VMEM((spans, ROWS, HEAD), LOW),
            pltpu.VMEM((spans, ROWS, HEAD), WIDE),
            pltpu.VMEM((spans, HEAD, HEAD), WIDE),
            pltpu.VMEM((spans, SPAN, HEAD), WIDE),
            pltpu.VMEM((spans, HEAD, HEAD), LOW),
            pltpu.VMEM((spans, HEAD, HEAD), LOW),
            pltpu.VMEM((spans, SPAN, HEAD), LOW),
        ],
        compiler_params=pltpu.CompilerParams(vmem_limit_bytes=VMEM_LIMIT),
        cost_estimate=estimate(70e9, 24),
        name="delta_forward",
    )(offs, rate, pre, pre, gs, gs, edge, taps, gain, state)


def run_gate_back(gs, gain, mixed, qh, high, rest, dgated, dend):
    tokens = mixed.shape[0]
    spans = tokens // SPAN
    shape = jax.ShapeDtypeStruct
    return pl.pallas_call(
        functools.partial(gate_back_kernel, spans),
        out_shape=(
            shape((spans, SPAN, HEAD), LOW),
            shape((spans, HEAD, HEAD), WIDE),
            shape((tokens, HEAD), LOW),
            shape((1, HEAD), WIDE),
            shape((HEAD, HEAD), WIDE),
        ),
        grid=(1,),
        in_specs=[
            fixed((tokens, HEAD)),
            fixed((1, HEAD)),
            fixed((tokens, HEAD)),
            fixed((spans, SPAN, HEAD)),
            fixed((spans, HEAD, HEAD)),
            fixed((spans, HEAD, HEAD)),
            fixed((tokens, HEAD)),
            fixed((HEAD, HEAD)),
        ],
        out_specs=(
            fixed((spans, SPAN, HEAD)),
            fixed((spans, HEAD, HEAD)),
            fixed((tokens, HEAD)),
            fixed((1, HEAD)),
            fixed((HEAD, HEAD)),
        ),
        scratch_shapes=[pltpu.VMEM((spans, HEAD, HEAD), WIDE)],
        compiler_params=pltpu.CompilerParams(vmem_limit_bytes=VMEM_LIMIT),
        cost_estimate=estimate(15e9, 8),
        name="delta_gate_back",
    )(gs, gain, mixed, qh, high, rest, dgated, dend)


def run_backward(last, steps, offs, rate, pre, gs, edge, taps, saved, carried, dy):
    conv, inverse, upd, scores, states, do, ds, dgate = saved
    tokens = pre.shape[0]

    def at(i):
        return last - i

    def rows(columns, lane=0):
        return pl.BlockSpec((PER * SPAN, columns), lambda i: (at(i), lane))

    def spans(a, b):
        return pl.BlockSpec((PER, a, b), lambda i: (at(i), 0, 0))

    shape = jax.ShapeDtypeStruct
    carried_specs = [fixed((4, 8, 640)), fixed((8, 640)), fixed((1, HEAD))]
    operands = [offs, rate, pre, pre, gs, edge, taps, conv, inverse, upd, scores, states, do, ds]
    operands += [dgate, *carried]
    in_specs = [
        smem_spec(),
        smem_spec(),
        rows(640),
        pl.BlockSpec((16, 640), lambda i: (jnp.maximum(at(i) * (PER * SPAN // 16) - 1, 0), 0)),
        rows(HEAD, 1),
        fixed((16, 640)),
        fixed((8, 640)),
        rows(640),
        spans(ROWS, ROWS),
        spans(ROWS, HEAD),
        spans(SPAN, ROWS),
        spans(HEAD, HEAD),
        spans(SPAN, HEAD),
        spans(HEAD, HEAD),
        rows(HEAD),
        *carried_specs,
    ]
    aliases = {}
    if dy is not None:
        aliases = {len(operands): 0}
        operands.append(dy)
        in_specs.append(pl.BlockSpec(memory_space=pl.ANY))
    dy, *carried = pl.pallas_call(
        functools.partial(backward_kernel, at, offs.shape[1] - 1),
        out_shape=(
            shape((tokens, 896), LOW),
            shape((4, 8, 640), WIDE),
            shape((8, 640), WIDE),
            shape((1, HEAD), WIDE),
        ),
        grid=(steps,),
        in_specs=in_specs,
        out_specs=(rows(896), *carried_specs),
        input_output_aliases=aliases,
        compiler_params=pltpu.CompilerParams(vmem_limit_bytes=VMEM_LIMIT),
        cost_estimate=estimate(4e9 * steps, 2.6 * steps),
        name="delta_backward",
    )(*operands)
    return dy, carried


def input_blocks_kernel(at_ref, dy_ref, out_ref, w_ref, send_ref, keep_ref):
    count = dy_ref.shape[0]
    block = contract(dy_ref[...], w_ref[...], 1, 1).astype(LOW)
    for n, to_ref in enumerate((send_ref, keep_ref)):

        @pl.when(pl.program_id(0) == n)
        def _():
            to_ref[:count, :] = block
            to_ref[count:, :] = out_ref[...]


def input_blocks(places, dy, grad_out, weights, count, out_rows):
    width = weights.shape[0]
    return pl.pallas_call(
        input_blocks_kernel,
        out_shape=[jax.ShapeDtypeStruct((count + out_rows, width), LOW)] * 2,
        grid_spec=pltpu.PrefetchScalarGridSpec(
            num_scalar_prefetch=1,
            grid=(2,),
            in_specs=[
                pl.BlockSpec((count, 896), lambda i, p: (p[i], 0)),
                pl.BlockSpec((out_rows, width), lambda i, p: (p[i], 0)),
                fixed(weights.shape),
            ],
            out_specs=[fixed((count + out_rows, width))] * 2,
        ),
        compiler_params=pltpu.CompilerParams(vmem_limit_bytes=VMEM_LIMIT),
        cost_estimate=estimate(4 * count * width * 896, 4),
        name="input_blocks",
    )(jnp.stack(places).astype(jnp.int32), dy, grad_out, weights)


def weight_grads_kernel(
    taps, at_ref, low_ref, dy_ref, w_ref, gain_ref, gff_ref, gh_ref, rate_ref, taps_ref, to_ref
):
    shard = w_ref.shape[0]
    grads = contract(low_ref[...], dy_ref[...], 0, 0)
    to_ref[:shard, :] = grads.astype(LOW)
    sums = jnp.sum(grads * w_ref[...].astype(WIDE), axis=1, keepdims=True)
    row = jnp.broadcast_to(sums, (shard, HEAD)).T[0:1] / gain_ref[...]

    def wide(value):
        return jnp.concatenate(
            [value, jnp.zeros((value.shape[0], 896 - value.shape[1]), WIDE)], axis=1
        )

    to_ref[shard:, :] = stack(
        wide(row),
        wide(gff_ref[...]),
        wide(gh_ref[0]),
        wide(rate_ref[...]),
        wide(taps_ref[:taps, :]),
        jnp.zeros((12 - taps, 896), WIDE),
    ).astype(LOW)


def weight_grads(order, low, dy, weights, gain, gain_ffn, gain_head, rate, taps_grad, taps):
    length, width = low.shape
    members = order.shape[0]
    shard = width // members
    gh = jnp.pad(gain_head.reshape(members, 1, -1), ((0, 0), (0, 0), (0, HEAD)))[:, :, :HEAD]
    return pl.pallas_call(
        functools.partial(weight_grads_kernel, taps),
        out_shape=jax.ShapeDtypeStruct((members * (shard + 16), 896), LOW),
        grid_spec=pltpu.PrefetchScalarGridSpec(
            num_scalar_prefetch=1,
            grid=(members,),
            in_specs=[
                pl.BlockSpec((length, shard), lambda i, p: (0, p[i])),
                fixed((length, 896)),
                pl.BlockSpec((shard, 896), lambda i, p: (p[i], 0)),
                pl.BlockSpec((1, shard), lambda i, p: (0, p[i])),
                pl.BlockSpec((1, shard), lambda i, p: (0, p[i])),
                pl.BlockSpec((1, 1, HEAD), lambda i, p: (p[i], 0, 0)),
                fixed((1, HEAD)),
                fixed((8, 640)),
            ],
            out_specs=pl.BlockSpec((shard + 16, 896), lambda i, p: (i, 0)),
        ),
        compiler_params=pltpu.CompilerParams(vmem_limit_bytes=VMEM_LIMIT),
        cost_estimate=estimate(2 * length * width * 896, 12),
        name="weight_grads",
    )(order, low, dy, weights, gain, gain_ffn, gh, rate, taps_grad)


def pack_kernel(
    heads, taps,
    place_ref, q_ref, k0_ref, k1_ref, v0_ref, v1_ref, g_ref, beta_ref, decay_ref, gin_ref,
    gff_ref, gh_ref, cq_ref, ck_ref, cv_ref, out_ref,
):
    h = place_ref[0]
    shard = q_ref.shape[0]
    for i, ref in enumerate((q_ref, k0_ref, k1_ref, v0_ref, v1_ref, g_ref)):
        out_ref[:shard, i * HEAD : (i + 1) * HEAD] = ref[...]
    beta, decay = beta_ref[...].astype(WIDE), decay_ref[...].astype(WIDE)

    def row_of(values, at):
        row = lax.broadcasted_iota(jnp.int32, values.shape, 0)
        return jnp.sum(jnp.where(row == at, values, 0.0), axis=0, keepdims=True)

    row = lax.broadcasted_iota(jnp.int32, (HEAD, shard), 0)
    small = jnp.where(row == 0, row_of(beta, h), 0.0)
    small = jnp.where(row == 1, row_of(beta, heads + h), small)
    small = jnp.where(row == 2, row_of(decay, h), small)
    out_ref[:shard, 6 * HEAD :] = small.T.astype(LOW)
    out_ref[shard:, :] = jnp.zeros((out_ref.shape[0] - shard, out_ref.shape[1]), LOW)
    vectors = stack(
        *[ref[...].astype(WIDE) for ref in (gin_ref, gff_ref, gh_ref, cq_ref)],
        *[
            ref[:, i * shard : (i + 1) * shard].astype(WIDE)
            for ref in (ck_ref, cv_ref)
            for i in range(2)
        ],
        jnp.zeros((32 - 3 - 5 * taps, shard), WIDE),
    )
    out_ref[shard:, :shard] = vectors.astype(LOW)


def pack_weights(
    head, w_query, w_key, w_value, w_outgate, w_beta, w_decay, gain_in, gain_ffn, gain_head,
    conv_query, conv_key, conv_value,
):
    shard, heads = w_decay.shape
    taps = conv_query.shape[0]

    def part(step):
        return pl.BlockSpec((shard, HEAD), lambda i, h: (0, step * heads + h[0]))

    small = (
        w_beta.T, w_decay.T, gain_in[None], gain_ffn[None],
        jnp.pad(gain_head, (0, shard - gain_head.shape[0]))[None],
        conv_query, conv_key, conv_value,
    )
    return pl.pallas_call(
        functools.partial(pack_kernel, heads, taps),
        out_shape=jax.ShapeDtypeStruct((shard + 32, 896), LOW),
        grid_spec=pltpu.PrefetchScalarGridSpec(
            num_scalar_prefetch=1,
            grid=(1,),
            in_specs=[part(0), part(0), part(1), part(0), part(1), part(0)]
            + [fixed(a.shape) for a in small],
            out_specs=fixed((shard + 32, 896)),
        ),
        compiler_params=pltpu.CompilerParams(vmem_limit_bytes=VMEM_LIMIT),
        cost_estimate=estimate(0, 2),
        name="pack_weights",
    )(head.reshape(1), w_query, w_key, w_key, w_value, w_value, w_outgate, *small)


def project_kernel(count, place_ref, gain_ref, w_ref, *refs):
    tok_refs, (low_ref, pre_ref, gs_ref) = refs[:count], refs[count:]
    for n in range(count):

        @pl.when(pl.program_id(0) == n)
        def _():
            values = tok_refs[n][...].astype(WIDE)
            scale = lax.rsqrt(jnp.mean(values * values, axis=1, keepdims=True) + EPSILON)
            low_ref[...] = (values * scale * gain_ref[...]).astype(LOW)

    normed = low_ref[...]
    pre_ref[...] = contract(normed, w_ref[:, :640], 1, 0).astype(LOW)
    gs_ref[...] = contract(normed, w_ref[:, 640:], 1, 0)


def project(found, gain, weights):
    blocks = [one for a, x, b, y in found for one in ((a, x), (b, y))]
    places = jnp.stack([place for place, _ in blocks]).astype(jnp.int32)
    count, (rows, width) = len(blocks), blocks[0][1].shape
    shape = jax.ShapeDtypeStruct
    return pl.pallas_call(
        functools.partial(project_kernel, count),
        out_shape=[
            shape((count * rows, n), t) for n, t in ((width, LOW), (640, LOW), (256, WIDE))
        ],
        grid_spec=pltpu.PrefetchScalarGridSpec(
            num_scalar_prefetch=1,
            grid=(count,),
            in_specs=[fixed(gain.shape), fixed(weights.shape)] + [fixed((rows, width))] * count,
            out_specs=[
                pl.BlockSpec((rows, n), lambda i, p: (p[i], 0)) for n in (width, 640, 256)
            ],
        ),
        compiler_params=pltpu.CompilerParams(vmem_limit_bytes=VMEM_LIMIT),
        cost_estimate=estimate(2 * count * rows * width * 896, 13),
        name="project",
    )(places, gain, weights, *(value for _, value in blocks))


def rms_parts(values):
    return values * lax.rsqrt(jnp.mean(values * values, axis=-1, keepdims=True) + EPSILON)


def rms_back(grad_scaled, values):
    scale = lax.rsqrt(jnp.mean(values * values, axis=-1, keepdims=True) + EPSILON)
    normed = values * scale
    return scale * (
        grad_scaled - normed * jnp.mean(grad_scaled * normed, axis=-1, keepdims=True)
    )


def dot_plain(left, right, kind=WIDE):
    return jnp.dot(left, right, preferred_element_type=kind)


def dot_left(left, right, kind=WIDE):
    return contract(left, right, 0, 0).astype(kind)


def dot_right(left, right):
    return contract(left, right, 1, 1)


def exchanged(value, axis, bit):
    size = lax.axis_size(axis)
    return lax.ppermute(value, axis, [(i, i ^ bit) for i in range(size)])


def near_order(size):
    order, bit = [0], size // 2
    while bit:
        order = order + [o ^ bit for o in order]
        bit //= 2
    return order


def near_gather(value, axis, first=None):
    bit = lax.axis_size(axis) // 2
    while bit:
        value = stack(value, exchanged(value, axis, bit) if first is None else first)
        first = None
        bit //= 2
    return value


def near_scatter(value, axis):
    size, bit = lax.axis_size(axis), 1
    while bit < size:
        half = value.shape[0] // 2
        came = exchanged(value[half:].astype(LOW), axis, bit).astype(WIDE)
        value = value[:half].astype(WIDE) + came
        bit *= 2
    return value


def near_scatter_stages(value, axis, ties):
    size, bit = lax.axis_size(axis), 1
    while bit < size:
        half = value.shape[0] // 2
        value = after(value, *ties)
        came = exchanged(value[half:].astype(LOW), axis, bit)
        yield [came]
        value = value[:half].astype(WIDE) + came.astype(WIDE)
        bit *= 2
    yield value


def near_blocks(value, axis):
    size, me = lax.axis_size(axis), lax.axis_index(axis)
    return stack(
        *[lax.dynamic_index_in_dim(value, me ^ o, 0, False) for o in near_order(size)]
    )


def ordered_step(value, other, axis, bit):
    mine_first = (lax.axis_index(axis) & bit) == 0
    pair = jnp.where(mine_first, jnp.stack([value, other], 1), jnp.stack([other, value], 1))
    return pair.reshape((pair.shape[0] * 2,) + value.shape[1:])


def ordered_gather(value, axis, first=None):
    bit = lax.axis_size(axis) // 2
    value = value[None]
    while bit:
        other = exchanged(value, axis, bit) if first is None else first[None]
        value = ordered_step(value, other, axis, bit)
        first = None
        bit //= 2
    return value


def far_exchange(value, axis):
    return exchanged(value, axis, lax.axis_size(axis) // 2)


def after(value, *done):
    return lax.optimization_barrier((value, *done))[0]


def team_step(value, team, move):
    size = lax.axis_size("seq")
    pairs = [(t + i, t + move(i)) for t in range(0, size, team) for i in range(team)]
    return lax.ppermute(value, "seq", pairs)


def turn(value, team, by):
    return team_step(value, team, lambda i: (i + 2 * by) % team)


def cross(value, team):
    return team_step(value, team, lambda i: i ^ 1)


def rolled(value, by, axis):
    twice = jnp.concatenate([value, value], axis=axis)
    return lax.dynamic_slice_in_dim(twice, by, value.shape[axis], axis)


def swapped(blocks, team):
    return [blocks[0]] + [
        team_step(blocks[k], team, lambda i: (i - k) % team) for k in range(1, team)
    ]


def turns(team):
    half = team // 2
    return [0] + [k for n in range(1, half // 2 + 1) for k in dict.fromkeys((n, half - n))]


def gather_stages(value, team, ties=(), lag=1):
    me = lax.axis_index("seq") % team
    half = team // 2
    turned, found, brought = {0: value}, [], []
    if half > 1:
        turned[1] = turn(value, team, 1)
    if half > 2:
        turned[half - 1] = turn(after(value, turned[1]), team, -1)
    for k in turns(team):
        across = cross(after(turned[k], *brought[-lag:][: len(brought) - lag + 1], *ties), team)
        stage = [across]
        for n in (k + 1, k - 1):
            if 0 < n < half and n not in turned and k:
                turned[n] = turn(turned[k], team, 1 if n > k else -1)
                stage.append(turned[n])
        brought.append(across)
        found.append(((me - 2 * k) % team, turned[k], ((me ^ 1) - 2 * k) % team, across))
        yield stage
    yield found


def last_of(stages):
    for stage in stages:
        pass
    return stage


def team_places(team):
    me = lax.axis_index("seq") % team
    return [
        (((me ^ 1) + 2 * k) % team, (me + 2 * k) % team) for k in reversed(turns(team))
    ]


def scatter_stages(blocks, team, ties=()):
    half = team // 2
    passing, leaving, before = {}, None, ()
    for (send, keep), k in zip(blocks, reversed(turns(team))):
        came = cross(after(send, *before, *ties), team)
        stage = [came]
        if leaving is not None:
            pair, n = leaving
            forward = 2 * n <= half
            to = n - 1 if forward else (n + 1) % half
            moved = turn(pair.astype(LOW), team, 1 if forward else -1)
            stage.append(moved)
            passing[to] = passing.get(to, []) + [moved]
        yield stage
        before = (came,)
        keep = keep(came) if callable(keep) else keep
        pair = keep.astype(WIDE) + came.astype(WIDE)
        for moved in passing.pop(k, []):
            pair = pair + moved.astype(WIDE)
        leaving = (pair, k)
    yield pair


def mixer_outputs_kernel(heads, taps, fsdp, place_ref, *refs):
    got_refs, out_refs, refs = refs[:heads], refs[heads : 2 * heads], refs[2 * heads :]
    (q_ref, k_ref, v_ref, g_ref, b_ref, d_ref, gin_ref, gff_ref, gh_ref, rate_ref, cq_ref,
     ck_ref, cv_ref, out_ref) = refs
    member = place_ref[0, heads]
    shard = q_ref.shape[0]
    gains = gh_ref.shape[1]
    width = heads * HEAD
    lane_r = lax.broadcasted_iota(jnp.int32, (1, heads), 1)
    rates = jnp.zeros((1, heads), WIDE)
    vectors = jnp.zeros((8, shard), WIDE)
    for n in range(heads):
        got_ref = got_refs[n]
        h = place_ref[0, n]

        def columns(step):
            return pl.ds(pl.multiple_of(step * width + h * HEAD, HEAD), HEAD)

        q_ref[:, columns(0)] = got_ref[:shard, 0:128].astype(WIDE)
        for i in range(2):
            k_ref[:, columns(i)] = got_ref[:shard, 128 + i * 128 : 256 + i * 128].astype(WIDE)
            v_ref[:, columns(i)] = got_ref[:shard, 384 + i * 128 : 512 + i * 128].astype(WIDE)
        g_ref[:, columns(0)] = got_ref[:shard, 640:768].astype(WIDE)
        last = got_ref[:shard, 768:896].astype(WIDE).T
        b_ref[pl.ds(h, 1), :] = last[0:1]
        b_ref[pl.ds(heads + h, 1), :] = last[1:2]
        d_ref[pl.ds(h, 1), :] = last[2:3]
        extra = got_ref[shard:, :].astype(WIDE)
        vectors = vectors + extra[0:8, :shard]
        rates = jnp.where(lane_r == h, extra[3:4, 2:3], rates)
        rows = out_refs[n].shape[0]
        out_ref[pl.ds(pl.multiple_of(h * rows, rows), rows), :] = out_refs[n][...].astype(WIDE)
        for ref, at, steps in ((cq_ref, 0, 1), (ck_ref, 128, 2), (cv_ref, 384, 2)):
            per = ref.shape[1] // HEAD
            for i in range(steps):
                slot = i * heads + h - member * per

                @pl.when((slot >= 0) & (slot < per))
                def _():
                    to = pl.ds(pl.multiple_of(slot * HEAD, HEAD), HEAD)
                    ref[:, to] = extra[4 : 4 + taps, at + i * HEAD : at + (i + 1) * HEAD]

    rate_ref[...] = rates
    gin_ref[...] = vectors[0:1]
    gff_ref[...] = vectors[1:2]
    gh_ref[...] = vectors[2:3, :gains]


def mixer_outputs(found, found_out, shard, gains, taps, fsdp, member):
    found, found_out = (
        [one for a, x, b, y in pairs for one in ((a, x), (b, y))] for pairs in (found, found_out)
    )
    heads = len(found)
    places = jnp.stack([place for place, _ in found] + [member])[None].astype(jnp.int32)
    width = heads * HEAD
    shape = jax.ShapeDtypeStruct
    outs = (
        shape((shard, width), WIDE),
        shape((shard, 2 * width), WIDE),
        shape((shard, 2 * width), WIDE),
        shape((shard, width), WIDE),
        shape((2 * heads, shard), WIDE),
        shape((heads, shard), WIDE),
        shape((1, shard), WIDE),
        shape((1, shard), WIDE),
        shape((1, gains), WIDE),
        shape((1, heads), WIDE),
        shape((taps, shard), WIDE),
        shape((taps, 2 * shard), WIDE),
        shape((taps, 2 * shard), WIDE),
        shape((shard, width), WIDE),
    )
    return pl.pallas_call(
        functools.partial(mixer_outputs_kernel, heads, taps, fsdp),
        out_shape=outs,
        in_specs=[smem_spec()] + [vmem_spec()] * (2 * heads),
        out_specs=[vmem_spec()] * len(outs),
        compiler_params=pltpu.CompilerParams(vmem_limit_bytes=VMEM_LIMIT),
        cost_estimate=estimate(0, 12),
        name="mixer_outputs",
    )(places, *(value for _, value in found), *(value for _, value in found_out))


def ff_outputs_kernel(count, slab, shard, place_ref, *refs):
    got_refs, (gate_ref, up_ref, down_ref), held = refs[:count], refs[count : count + 3], refs[-1]
    own = count * slab
    for n, got_ref in enumerate(got_refs):
        at = place_ref[n] * slab
        piece = got_ref[...].astype(WIDE)
        for m in range(2):
            for k in range(2):
                to = pl.multiple_of(k * own + at, 8)
                held[m, pl.ds(to, slab), :] = piece[
                    m * slab : (m + 1) * slab, k * shard : (k + 1) * shard
                ]
        down_ref[pl.ds(pl.multiple_of(at, 8), slab), :] = piece[2 * slab :]
    gate_ref[...] = held[0].T
    up_ref[...] = held[1].T


def ff_outputs(found, slab, shard, fsdp):
    found = [one for a, x, b, y in found for one in ((a, x), (b, y))]
    count, (rows, width) = len(found), found[0][1].shape
    own = count * slab
    shape = jax.ShapeDtypeStruct
    return pl.pallas_call(
        functools.partial(ff_outputs_kernel, count, slab, shard),
        out_shape=(
            shape((shard, fsdp * own), WIDE),
            shape((shard, fsdp * own), WIDE),
            shape((own, width), WIDE),
        ),
        grid_spec=pltpu.PrefetchScalarGridSpec(
            num_scalar_prefetch=1,
            grid=(fsdp // 2,),
            in_specs=[pl.BlockSpec((rows, 2 * shard), lambda i, p: (0, i))] * count,
            out_specs=(
                pl.BlockSpec((shard, 2 * own), lambda i, p: (0, i)),
                pl.BlockSpec((shard, 2 * own), lambda i, p: (0, i)),
                pl.BlockSpec((own, 2 * shard), lambda i, p: (0, i)),
            ),
            scratch_shapes=[pltpu.VMEM((2, 2 * own, shard), WIDE)],
        ),
        compiler_params=pltpu.CompilerParams(vmem_limit_bytes=VMEM_LIMIT),
        cost_estimate=estimate(0, 15),
        name="ff_outputs",
    )(jnp.stack([p for p, _ in found]).astype(jnp.int32), *(x for _, x in found))


def ff_outputs_plain(got, slab, shard, fsdp):
    seq, rows, width = got.shape
    own = seq * slab
    wide = got.astype(WIDE)

    def turned(at):
        part = wide[:, at : at + slab].reshape(seq, slab, fsdp, shard)
        return jnp.transpose(part, (3, 2, 0, 1)).reshape(shard, fsdp * own)

    return turned(0), turned(slab), wide[:, 2 * slab :].reshape(own, width)


def per_device(
    tokens, cotangent, offsets, gain_in, w_query, w_key, w_value, w_beta, w_decay, w_outgate,
    conv_query, conv_key, conv_value, decay_scale, gain_head, w_out, gain_ffn, w_gate, w_up,
    w_down,
):
    seq, fsdp = lax.axis_size("seq"), lax.axis_size("fsdp")
    heads = decay_scale.shape[0]
    taps = conv_query.shape[0]
    own_rows = tokens.shape[1]
    shard = w_query.shape[0]
    width = shard * fsdp
    teams = seq // heads
    assert teams * heads == seq and width == heads * HEAD
    place = lax.axis_index("seq")
    head, team = place % heads, place // heads
    member = lax.axis_index("fsdp")
    if teams == 1:
        team_groups, head_groups = None, None
    else:
        team_groups = [[t * heads + h for h in range(heads)] for t in range(teams)]
        head_groups = [[t * heads + h for t in range(teams)] for h in range(heads)]

    def gather_rows(value):
        return lax.all_gather(value, "fsdp", axis=0, tiled=True)

    start_ties = []
    spread = gather_stages(tokens[0], heads, start_ties)
    came = next(spread)[:1]
    length = heads * own_rows

    def column_blocks(value):
        return jnp.transpose(value.reshape(shard, fsdp, value.shape[1] // fsdp), (1, 0, 2))

    packed = pack_weights(
        head, after(w_query, came[0]), w_key, w_value, w_outgate, w_beta, w_decay, gain_in,
        gain_ffn, gain_head, conv_query, conv_key, conv_value,
    )
    far_packed = far_exchange(packed, "fsdp")
    start_ties[:] = [packed]
    came += next(spread)[:1]
    columns = jnp.stack(
        [column_blocks(after(w_gate, came[1])), column_blocks(after(w_up, came[1]))], axis=1
    )
    others = near_order(fsdp)[1:]
    column_sends = [lax.dynamic_index_in_dim(columns, member ^ o, 0, False) for o in others]
    start_ties[:] = [far_packed]
    came += next(spread)[:1]
    far_out = far_exchange(after(w_out, far_packed), "fsdp")
    got = ordered_gather(packed, "fsdp", far_packed)
    start_ties[:] = [got, far_out, *column_sends]
    for stage in spread:
        found = stage
        came += stage[:1]
    came = [one for one in came if not isinstance(one, tuple)]
    came += [came[-1]] * 3
    full_packed = got[:, :shard].reshape(width, 896)
    vectors = got[:, shard:, :shard]
    full_gain_in = vectors[:, 0].reshape(width).astype(WIDE)
    full_gain_ffn = vectors[:, 1].reshape(width).astype(WIDE)
    full_gain_head = vectors[:, 2, : gain_head.shape[0]].reshape(1, HEAD).astype(WIDE)

    def head_taps_of(row, pieces, step):
        column = step * width + head * HEAD
        inside = column % (pieces * shard)
        at = (column // (pieces * shard), row + inside // shard * taps, inside % shard)
        return lax.dynamic_slice(vectors, at, (1, taps, HEAD))[0]

    head_taps = jnp.concatenate(
        [head_taps_of(3, 1, 0)]
        + [head_taps_of(3 + taps, 2, i) for i in range(2)]
        + [head_taps_of(3 + 3 * taps, 2, i) for i in range(2)],
        axis=1,
    ).astype(WIDE)
    head_taps = jnp.pad(head_taps, ((0, 8 - taps), (0, 0)))
    def column_blocks(value):
        return jnp.transpose(value.reshape(shard, fsdp, value.shape[1] // fsdp), (1, 0, 2))

    cot = after(cotangent[0], came[2])
    far_cot = far_exchange(cot, "fsdp")
    column_got = [
        exchanged(after(send, came[2]), "fsdp", o) for o, send in zip(others, column_sends)
    ]
    normed_low, pre, gate_small = project(found, full_gain_in[None], full_packed)
    offs = jnp.concatenate(
        [offsets, jnp.broadcast_to(team * length, (1, 1)).astype(jnp.int32)], axis=1
    )
    rate = lax.dynamic_slice_in_dim(decay_scale, head, 1).reshape(1, 1)
    zero_state = jnp.zeros((HEAD, HEAD), WIDE)
    if teams == 1:
        edge = jnp.zeros((16, 640), LOW)
    else:
        forth = [(i, i + heads) for i in range(seq - heads)]
        back = [(i + heads, i) for i in range(seq - heads)]
        edge = lax.ppermute(pre[-16:], "seq", forth)

    def forward_from(state):
        return run_forward(
            offs, rate, pre, gate_small, edge, head_taps, full_gain_head, state
        )

    state_in = zero_state
    if teams > 1:
        trial = forward_from(zero_state)
        steps, end = trial[4].astype(WIDE) + trial[5].astype(WIDE), trial[10]

        def along(c, total):
            return jnp.dot(total, steps[c].T, precision=lax.Precision.HIGHEST)

        whole_map = lax.fori_loop(0, steps.shape[0], along, jnp.eye(HEAD, dtype=WIDE))
        for _ in range(teams - 1):
            out = jnp.dot(state_in, whole_map, precision=lax.Precision.HIGHEST) + end
            state_in = lax.ppermute(out.astype(LOW), "seq", forth).astype(WIDE)
    conv, inverse, scores, reach, high, rest, gated, mixed, upd, states, _ = forward_from(state_in)
    gated, far_out, far_cot, *column_got = lax.optimization_barrier(
        (gated, far_out, far_cot, *column_got)
    )
    own_columns = lax.dynamic_index_in_dim(columns, member, 0, False)
    full_out = ordered_gather(w_out, "fsdp", far_out).reshape(width, width)
    group_cot = near_gather(cot, "fsdp", far_cot)

    def ordered_columns(which):
        value = jnp.zeros((width, own_columns.shape[2]), LOW)
        for o, rows in zip([0, *others], [own_columns, *column_got]):
            value = lax.dynamic_update_slice(value, rows[which], ((member ^ o) * shard, 0))
        return value

    cols_gate, cols_up = ordered_columns(0), ordered_columns(1)

    pieces = [
        lax.dynamic_slice_in_dim(gated, (head - k) % heads * own_rows, own_rows, 0)
        for k in range(heads)
    ]
    gated_own = rolled(
        jnp.concatenate(swapped(pieces, heads), axis=1), (heads - head) % heads * HEAD, 1
    )
    inputs = tokens[0].astype(WIDE)
    mixer_res = inputs + dot_plain(gated_own, full_out)

    mid_normed = rms_parts(mixer_res)
    mid_low = (mid_normed * full_gain_ffn).astype(LOW)
    group_mid = near_gather(mid_low, "fsdp")
    gate_pre = dot_plain(group_mid, cols_gate)
    up_pre = dot_plain(group_mid, cols_up)
    sig = jax.nn.sigmoid(gate_pre)
    act = gate_pre * sig
    hidden = (act * up_pre).astype(LOW)
    grad_hidden = dot_right(group_cot, w_down)
    grad_gate_pre = (grad_hidden * up_pre * (sig * (1.0 + gate_pre * (1.0 - sig)))).astype(LOW)
    grad_up_pre = (grad_hidden * act).astype(LOW)
    grad_mid = dot_right(grad_gate_pre, cols_gate) + dot_right(grad_up_pre, cols_up)
    grad_gate_pre, grad_up_pre, grad_mid = lax.optimization_barrier(
        (grad_gate_pre, grad_up_pre, grad_mid)
    )
    grad_mid = near_scatter(grad_mid, "fsdp")

    grad_res = cotangent[0].astype(WIDE) + rms_back(grad_mid * full_gain_ffn, mixer_res)
    grad_gain_ffn = jnp.sum(grad_mid * mid_normed, axis=0)
    res_low = grad_res.astype(LOW)
    grad_gated = dot_right(res_low, full_out).astype(LOW)
    own_ff = w_down.shape[0]
    slab = own_ff // seq
    slabs = jnp.concatenate(
        [
            dot_left(grad_gate_pre, group_mid, LOW).reshape(seq, slab, width),
            dot_left(grad_up_pre, group_mid, LOW).reshape(seq, slab, width),
            dot_left(hidden, group_cot, LOW).reshape(seq, slab, width),
        ],
        axis=1,
    )
    permuted = teams == 1 and slab % 8 == 0 and own_ff * 2 % HEAD == 0 and fsdp % 2 == 0

    def turned_columns(summed):
        turned = lax.all_to_all(summed[: 2 * slab], "fsdp", 1, 1, tiled=True)
        return stack(turned, summed[2 * slab :])

    def feed_forward_sums():
        if not permuted:
            summed = lax.psum_scatter(
                slabs.reshape(seq * 3 * slab, width), "seq", scatter_dimension=0, tiled=True
            )
            yield [summed]
            slabs_done = lax.all_gather(turned_columns(summed), "seq", axis=0)
            yield ff_outputs_plain(slabs_done, slab, shard, fsdp)
            return
        def kept(at):
            return lambda came: lax.dynamic_index_in_dim(after(slabs, came), at, 0, False)

        blocks = [
            (lax.dynamic_index_in_dim(slabs, send, 0, False), kept(keep))
            for send, keep in team_places(heads)
        ]
        for stage in scatter_stages(blocks, heads, ties):
            if isinstance(stage, list):
                yield stage
        mine = turned_columns(after(stage.astype(LOW), *ties))
        yield [mine]
        for stage in gather_stages(mine, heads, ties):
            if isinstance(stage[0], tuple):
                break
            yield stage
        yield ff_outputs(stage, slab, shard, fsdp)

    ties, sums = [], feed_forward_sums()
    brought = [next(sums)]

    def beside(value):
        if not isinstance(brought[-1], tuple):
            ties[:] = [value]
            brought.append(next(sums))

    def settled(value):
        stage = brought[-1]
        return value if isinstance(stage, tuple) else after(value, *stage)

    pieces = [
        lax.dynamic_slice_in_dim(grad_gated, (head - k) % heads * HEAD, HEAD, 1)
        for k in range(heads)
    ]
    dgated = rolled(
        jnp.concatenate(swapped(pieces, heads), axis=0), (heads - head) % heads * own_rows, 0
    )
    grad_out = dot_left(after(gated_own, grad_gated), res_low, LOW).reshape(fsdp, shard, width)
    late = near_blocks(grad_out, "fsdp")
    dgated, late = lax.optimization_barrier((dgated, late))
    beside(dgated)
    late_ties = []
    late = near_scatter_stages(late, "fsdp", late_ties)
    late_stage = []

    def gate_back_from(dend):
        return run_gate_back(
            gate_small, full_gain_head, mixed, reach, high, rest, dgated, dend
        )

    dend = zero_state
    if teams > 1:
        begin = gate_back_from(zero_state)[4]
        for _ in range(teams - 1):
            out = lax.dot_general(
                dend, whole_map, (((1,), (1,)), ((), ())), precision=lax.Precision.HIGHEST
            )
            dend = lax.ppermute((out + begin).astype(LOW), "seq", back).astype(WIDE)
    do, ds, dgate, dgain, _ = gate_back_from(dend)
    carried = [
        jnp.zeros((4, 8, 640), WIDE), jnp.zeros((8, 640), WIDE), jnp.zeros((1, HEAD), WIDE)
    ]
    dy, calls = None, 2
    left = length // (PER * SPAN)
    for call in range(calls, 0, -1):
        steps_here = -(-left // call)
        if dy is None:
            carried[0] = after(carried[0], do)
        carried[0] = settled(after(carried[0], *late_stage))
        beside(carried[0])
        late_ties[:] = [carried[0]]
        late_stage = next(late)
        late_stage = late_stage if isinstance(late_stage, list) else [late_stage]
        dy, carried = run_backward(
            left - 1, steps_here, offs, rate, pre, gate_small, edge, head_taps,
            (conv, inverse, upd, scores, states, do, ds, dgate), carried, dy,
        )
        carried = list(carried)
        left -= steps_here
    dy = settled(dy)
    late_stage = late_stage[0]
    for stage in late:
        late_stage = stage
    grad_out = late_stage.astype(LOW)
    following, dtaps, drate = carried
    if teams > 1:
        none = jnp.zeros((16, 640), WIDE)
        dedge = sum(stack(none, following[lag])[lag : lag + 16] for lag in range(1, 4))
        from_next = lax.ppermute(dedge.astype(LOW), "seq", back).astype(WIDE)
        tail = (dy[-16:, :640].astype(WIDE) + from_next).astype(LOW)
        dy = lax.dynamic_update_slice(dy, tail, (length - 16, 0))

    out_rows = shard // heads

    blocks = [
        list(input_blocks(places, dy, grad_out, full_packed, own_rows, out_rows))
        for places in team_places(heads)
    ]
    turned_stage = []
    if not isinstance(brought[-1], tuple):
        beside(blocks[0][0])
        turned_stage = brought[-1] if isinstance(brought[-1], list) else []
    order = jnp.stack([member ^ o for o in near_order(fsdp)]).astype(jnp.int32)
    combined = weight_grads(
        order, normed_low, after(dy, blocks[0][0], *turned_stage), full_packed, full_gain_in[None],
        grad_gain_ffn[None], dgain, drate, dtaps, taps,
    )
    combined = near_scatter(combined, "fsdp").astype(LOW)
    *queue, joined = scatter_stages(blocks, heads)
    while not isinstance(brought[-1], tuple):
        beside(blocks[0][0])
    out_gate, out_up, out_down = brought[-1]
    down_part = near_scatter(dot_plain(after(hidden, queue[1][0]), w_down).astype(LOW), "fsdp")
    layer_out = (mixer_res + down_part).astype(LOW)
    grad_normed, own_out = joined[:own_rows], joined[own_rows:].astype(LOW)
    input_grad = (grad_res + rms_back(grad_normed * full_gain_in, inputs)).astype(LOW)
    if teams > 1:
        own_out = lax.psum(own_out, "seq", axis_index_groups=head_groups)
    found_out = last_of(gather_stages(own_out, heads))

    if teams > 1:
        combined = lax.psum(combined, "seq", axis_index_groups=head_groups)
    (out_query, out_key, out_value, out_gatew, out_beta, out_decay, out_gain_in, out_gain_ffn,
     out_gain_head, out_rate, out_cq, out_ck, out_cv, out_out) = mixer_outputs(
        last_of(gather_stages(combined, heads, lag=1)), found_out, shard, gain_head.shape[0], taps, fsdp, member
    )

    return (
        layer_out[None],
        input_grad[None],
        out_gain_in[0],
        out_query,
        out_key,
        out_value,
        out_beta.T,
        out_decay.T,
        out_gatew,
        out_cq,
        out_ck,
        out_cv,
        out_rate[0],
        out_gain_head[0],
        out_out,
        out_gain_ffn[0],
        out_gate,
        out_up,
        out_down,
    )


def solution(mesh):
    rows, lanes = P("fsdp", None), P(None, "fsdp")
    block = P("fsdp", "seq", None)
    return jax.shard_map(
        per_device,
        mesh=mesh,
        in_specs=(
            block, block, rows, P("fsdp"), rows, rows, rows, rows, rows, rows,
            lanes, lanes, lanes, P(), P("fsdp"), rows, P("fsdp"), rows, rows, rows,
        ),
        out_specs=(
            block, block, P("fsdp"), rows, rows, rows, rows, rows, rows,
            lanes, lanes, lanes, P(), P("fsdp"), rows, P("fsdp"), rows, rows, rows,
        ),
        check_vma=False,
    )
```

```python
import functools

import jax
import jax.numpy as jnp
from jax import lax
from jax.experimental import pallas as pl
from jax.experimental.pallas import tpu as pltpu
from jax.sharding import PartitionSpec as P

SPAN = 64
PER = 4
ROWS = 128
HEAD = 128
EPSILON = 1e-06
LOW = jnp.bfloat16
WIDE = jnp.float32
VMEM_LIMIT = 56 * 1024 * 1024


def contract(left, right, left_dim, right_dim):
    return lax.dot_general(
        left, right, (((left_dim,), (right_dim,)), ((), ())), preferred_element_type=WIDE
    )


def halves(value):
    high = value.astype(LOW)
    return high, (value - high.astype(WIDE)).astype(LOW)


def mm(left, right, left_dim=1, right_dim=0):
    return contract(left.astype(LOW), right.astype(LOW), left_dim, right_dim)


def stack(*parts):
    return jnp.concatenate(parts, axis=0)


def row_maps():
    row = lax.broadcasted_iota(jnp.int32, (ROWS, ROWS), 0)
    col = lax.broadcasted_iota(jnp.int32, (ROWS, ROWS), 1)
    tok, step = row & (SPAN - 1), row >> 6
    tok_c, step_c = col & (SPAN - 1), col >> 6
    return tok, step, tok_c, step_c


def span_tokens(offs_ref, doc_count, first):
    place = first + lax.broadcasted_iota(jnp.int32, (SPAN, 1), 0)
    begin = jnp.zeros((SPAN, 1), jnp.int32)
    for j in range(doc_count):
        start = offs_ref[0, j]
        begin = jnp.where(place >= start, start, begin)
    return place - begin


def softplus(value):
    return jnp.maximum(value, 0.0) + jnp.log1p(jnp.exp(-jnp.abs(value)))


def decay_sums(small, rate):
    logs = -rate * softplus(small)
    tok = lax.broadcasted_iota(jnp.int32, (SPAN, SPAN), 0)
    tok_c = lax.broadcasted_iota(jnp.int32, (SPAN, SPAN), 1)
    lower = jnp.where(tok >= tok_c, 1.0, 0.0).astype(LOW)
    tok_w = lax.broadcasted_iota(jnp.int32, (SPAN, ROWS), 0)
    tok_wc = lax.broadcasted_iota(jnp.int32, (SPAN, ROWS), 1) & (SPAN - 1)
    upper = jnp.where(tok_w <= tok_wc, 1.0, 0.0).astype(LOW)
    high, rest = halves(logs)
    cols = contract(lower, high, 1, 0) + contract(lower, rest, 1, 0)
    rows = contract(high, upper, 0, 0) + contract(rest, upper, 0, 0)
    return cols[:, 2:3], rows[2:3, :]


def unit(values):
    scale = lax.rsqrt(jnp.sum(values * values, axis=1, keepdims=True) + EPSILON)
    return values * scale, scale


def span_factors(small, rate, pos):
    sig = jax.nn.sigmoid(small)
    cum, cum_row = decay_sums(small, rate)
    beta = stack(sig[:, 0:1], sig[:, 1:2])
    cum2, pos2 = stack(cum, cum), stack(pos, pos)
    tok, step, tok_c, step_c = row_maps()
    before = tok > tok_c
    here = tok == tok_c
    reach = (before | (here & (step >= step_c))) & (tok - tok_c <= pos2)
    decay = jnp.where(reach, jnp.exp(jnp.where(reach, cum2 - cum_row, 0.0)), 0.0)
    strict = before | (here & (step > step_c))
    tok1 = tok[:, 0:1]
    carry = jnp.where(pos2 > tok1, jnp.exp(cum2), 0.0)
    end, end_pos = cum[SPAN - 1 : SPAN], pos[SPAN - 1 : SPAN]
    leave = jnp.where(SPAN - 1 - tok1 <= end_pos, jnp.exp(end - cum2), 0.0)
    carry_all = jnp.where(end_pos >= SPAN, jnp.exp(end), 0.0)
    return beta, decay, strict, carry, leave, carry_all, tok ^ tok_c


def in_turns(bodies):
    bodies = list(bodies)
    while bodies:
        bodies = [body for body in bodies if next(body, "end") != "end"]


def unit_lower_inverse(strict_part, apart):
    row = lax.broadcasted_iota(jnp.int32, (ROWS, ROWS), 0)
    col = lax.broadcasted_iota(jnp.int32, (ROWS, ROWS), 1)
    inverse = jnp.where(row == col, 1.0, 0.0) - jnp.where(apart == 0, strict_part, 0.0)
    for level in range(6):
        block = jnp.where((apart >> level) == 1, strict_part, 0.0)
        low = inverse.astype(LOW)
        half = contract(low, block.astype(LOW), 1, 0).astype(LOW)
        yield
        inverse = inverse - contract(half, low, 1, 0)
        yield
    return inverse


def conv_rows(prior, here):
    return stack(prior.astype(WIDE), here.astype(WIDE))


def forward_kernel(
    span_count, doc_count, group,
    offs_ref, rate_ref, pre_ref, prior_ref, small_ref, gate_ref, edge_ref, taps_ref, gain_ref,
    state_ref,
    conv_ref, t_ref, sc_ref, qh_ref, ah_ref, al_ref, gated_ref, mixed_ref, u_ref, s_ref, end_ref,
    w_scr, u0_scr, b_scr, o0_scr, ah_scr, al_scr, qh_scr,
):
    step = pl.program_id(0)
    base = offs_ref[0, doc_count]
    rate = rate_ref[0, 0]
    prior = jnp.where(step == 0, edge_ref[...].astype(WIDE), prior_ref[...].astype(WIDE))

    def local(u):
        c = step * group + u
        here = pre_ref[u * SPAN : (u + 1) * SPAN, :].astype(WIDE)
        if u:
            before = pre_ref[u * SPAN - 16 : u * SPAN, :].astype(WIDE)
        else:
            before = prior
        rows = stack(before, here)
        pos = span_tokens(offs_ref, doc_count, base + c * SPAN)
        conv = taps_ref[0:1, :] * here
        for lag in range(1, 4):
            shifted = rows[16 - lag : 16 - lag + SPAN]
            conv = conv + jnp.where(pos >= lag, taps_ref[lag : lag + 1, :] * shifted, 0.0)
        conv_ref[u * SPAN : (u + 1) * SPAN, :] = conv
        yield
        act = conv * jax.nn.sigmoid(conv)
        query, _ = unit(act[:, 0:128])
        key0, _ = unit(act[:, 128:256])
        key1, _ = unit(act[:, 256:384])
        keys = stack(key0, key1)
        values = stack(act[:, 384:512], act[:, 512:640])
        small = small_ref[u * SPAN : (u + 1) * SPAN, :]
        beta, decay, strict, carry, leave, carry_all, apart = span_factors(small, rate, pos)
        yield
        inner = mm(keys, keys, 1, 1)
        yield
        inverse = yield from unit_lower_inverse(
            jnp.where(strict, beta * decay * inner, 0.0), apart
        )
        t_ref[u] = inverse.astype(LOW)
        both = mm(inverse, jnp.concatenate([(beta * carry) * keys, beta * values], axis=1))
        yield
        weight, fresh = both[:, :HEAD], both[:, HEAD:]
        w_scr[c] = weight.astype(LOW)
        u0_scr[c] = fresh
        leaving = (keys * leave).astype(LOW)
        row = lax.broadcasted_iota(jnp.int32, (HEAD, HEAD), 0)
        col = lax.broadcasted_iota(jnp.int32, (HEAD, HEAD), 1)
        step_map = jnp.where(row == col, carry_all, 0.0) - mm(leaving, weight, 0, 0)
        map_high, map_rest = halves(step_map)
        ah_ref[u], al_ref[u] = map_high, map_rest
        ah_scr[c], al_scr[c] = map_high, map_rest
        yield
        b_scr[c] = mm(fresh, leaving, 0, 0)
        yield
        scores = mm(query, keys, 1, 1) * decay[SPAN:, :]
        yield
        sc_ref[u] = scores.astype(LOW)
        mixed_both = mm(scores, both)
        yield
        reach = (carry[SPAN:] * query - mixed_both[:, :HEAD]).astype(LOW)
        qh_ref[u] = reach
        qh_scr[c] = reach
        o0_scr[c] = mixed_both[:, HEAD:]

    in_turns(local(u) for u in range(group))

    def chain(i, state):
        for u in range(4):
            c = i * 4 + u
            s_ref[c] = state
            high, rest = halves(state)
            state = (
                contract(high, ah_scr[c], 1, 1)
                + contract(high, al_scr[c], 1, 1)
                + contract(rest, ah_scr[c], 1, 1)
                + b_scr[c]
            )
        return state

    def mixing(c):
        low = s_ref[c].astype(LOW)
        u_ref[c] = (u0_scr[c] - contract(w_scr[c], low, 1, 1)).astype(LOW)
        yield
        mixed = o0_scr[c] + contract(qh_scr[c], low, 1, 1)
        yield
        lo = pl.multiple_of(c * SPAN, SPAN)
        mixed_ref[pl.ds(lo, SPAN), :] = mixed
        scale = lax.rsqrt(jnp.mean(mixed * mixed, axis=1, keepdims=True) + EPSILON)
        yield
        gate = gate_ref[pl.ds(lo, SPAN), :]
        gated_ref[pl.ds(lo, SPAN), :] = (
            mixed * scale * gain_ref[...] * (gate * jax.nn.sigmoid(gate))
        ).astype(LOW)
        yield

    def mixing_step(i, none):
        in_turns(mixing(i * 8 + u) for u in range(8))
        return none

    @pl.when(step == pl.num_programs(0) - 1)
    def _():
        end_ref[...] = lax.fori_loop(0, span_count // 4, chain, state_ref[...])
        lax.fori_loop(0, span_count // 8, mixing_step, 0)


def gate_back_kernel(
    span_count,
    gate_ref, gain_ref, mixed_ref, qh_ref, ah_ref, al_ref, dgated_ref, dend_ref,
    do_ref, ds_ref, dgate_ref, dgain_ref, dbegin_ref,
    f_scr,
):
    dgain_ref[...] = jnp.zeros_like(dgain_ref)

    def gate_back(c):
        lo = pl.multiple_of(c * SPAN, SPAN)
        mixed = mixed_ref[pl.ds(lo, SPAN), :]
        gate = gate_ref[pl.ds(lo, SPAN), :]
        scale = lax.rsqrt(jnp.mean(mixed * mixed, axis=1, keepdims=True) + EPSILON)
        normed = mixed * scale
        yield
        sig = jax.nn.sigmoid(gate)
        grad = dgated_ref[pl.ds(lo, SPAN), :].astype(WIDE)
        by_gain = grad * normed
        dgate_ref[pl.ds(lo, SPAN), :] = (
            by_gain * gain_ref[...] * (sig * (1.0 + gate * (1.0 - sig)))
        ).astype(LOW)
        dgain_ref[...] += jnp.sum(by_gain * (gate * sig), axis=0, keepdims=True)
        yield
        dn = grad * (gate * sig) * gain_ref[...]
        dmixed = scale * (dn - normed * jnp.mean(dn * normed, axis=1, keepdims=True))
        do_low = dmixed.astype(LOW)
        do_ref[c] = do_low
        yield
        f_scr[c] = contract(do_low, qh_ref[c], 0, 0)

    def gate_step(i, none):
        in_turns(gate_back(i * 8 + u) for u in range(8))
        return none

    lax.fori_loop(0, span_count // 8, gate_step, 0)

    def chain_step(i, grad):
        for u in range(4):
            c = span_count - 1 - (i * 4 + u)
            ds_ref[c] = grad
            high, rest = halves(grad)
            grad = (
                contract(high, ah_ref[c], 1, 0)
                + contract(high, al_ref[c], 1, 0)
                + contract(rest, ah_ref[c], 1, 0)
                + f_scr[c]
            )
        return grad

    dbegin_ref[...] = lax.fori_loop(0, span_count // 4, chain_step, dend_ref[...])


def backward_kernel(
    at_block, doc_count,
    offs_ref, rate_ref, pre_ref, prior_ref, small_ref, edge_ref, taps_ref,
    conv_ref, t_ref, u_ref, sc_ref, s_ref, do_ref, ds_ref, dgate_ref,
    next_in, dtaps_in, drate_in, *refs,
):
    dy_ref, next_ref, dtaps_ref, drate_ref = refs[-4:]
    block = at_block(pl.program_id(0))
    base = offs_ref[0, doc_count]
    rate = rate_ref[0, 0]

    @pl.when(pl.program_id(0) == 0)
    def _():
        next_ref[...] = next_in[...]
        dtaps_ref[...] = dtaps_in[...]
        drate_ref[...] = drate_in[...]

    dy_ref[:, 640:768] = dgate_ref[...]

    def local(n):
        lo, hi = n * SPAN, (n + 1) * SPAN
        pos = span_tokens(offs_ref, doc_count, base + block * PER * SPAN + lo)
        conv = conv_ref[lo:hi, :]
        sig = jax.nn.sigmoid(conv)
        act = conv * sig
        query, scale_q = unit(act[:, 0:128])
        key0, scale_0 = unit(act[:, 128:256])
        key1, scale_1 = unit(act[:, 256:384])
        yield
        keys = stack(key0, key1)
        values = stack(act[:, 384:512], act[:, 512:640])
        small = small_ref[lo:hi, :]
        beta, decay, strict, carry, leave, carry_all, _ = span_factors(small, rate, pos)
        yield
        state, dstate = s_ref[n], ds_ref[n]
        state_l, dstate_l = state.astype(LOW), dstate.astype(LOW)
        upd, out_grad, keys_l = u_ref[n], do_ref[n], keys.astype(LOW)
        dupd = contract(sc_ref[n], out_grad, 0, 0) + mm(keys * leave, dstate_l, 1, 1)
        yield
        dtarget = mm(t_ref[n], dupd, 0, 0)
        yield
        pair = stack(dtarget.astype(LOW), out_grad)
        by_upd = contract(pair, upd, 1, 1)
        by_state = contract(pair, state_l, 1, 0)
        yield
        dinner = jnp.where(strict, -by_upd[:ROWS] * decay, 0.0)
        dscore = by_upd[ROWS:] * decay[SPAN:, :]
        both = stack(dinner, dscore).astype(LOW)
        reading = contract(both, keys_l, 1, 0)
        yield
        read_key = reading[:ROWS] - carry * by_state[:ROWS]
        dquery = reading[ROWS:] + carry[SPAN:] * by_state[ROWS:]
        dleave = leave * contract(upd, dstate_l, 1, 0)
        write_key = contract(both, stack(beta * keys, query).astype(LOW), 0, 0) + dleave
        yield
        key_read = jnp.sum(keys * read_key, axis=1, keepdims=True)
        dbeta = jnp.sum(dtarget * values, axis=1, keepdims=True) + key_read
        dcum = beta * key_read - jnp.sum(keys * write_key, axis=1, keepdims=True)
        dcum = dcum[:SPAN] + dcum[SPAN:] + jnp.sum(query * dquery, axis=1, keepdims=True)
        through = jnp.sum(keys * dleave, axis=0, keepdims=True) + carry_all * jnp.sum(
            dstate * state, axis=0, keepdims=True
        )
        through = jnp.sum(through, axis=1, keepdims=True)
        tok1 = lax.broadcasted_iota(jnp.int32, (SPAN, 1), 0)
        dcum = dcum + jnp.where(tok1 == SPAN - 1, through, 0.0)
        tok = lax.broadcasted_iota(jnp.int32, (SPAN, SPAN), 0)
        tok_c = lax.broadcasted_iota(jnp.int32, (SPAN, SPAN), 1)
        upper = jnp.where(tok <= tok_c, 1.0, 0.0).astype(LOW)
        high, rest = halves(jnp.broadcast_to(dcum, (SPAN, 128)))
        dlog = contract(upper, high, 1, 0) + contract(upper, rest, 1, 0)
        yield
        soft = softplus(small)
        sig_small = jax.nn.sigmoid(small)
        lane = lax.broadcasted_iota(jnp.int32, (SPAN, 128), 1)
        drate_ref[...] += jnp.sum(jnp.where(lane == 2, -dlog * soft, 0.0), axis=0, keepdims=True)
        dsig = jnp.where(lane == 0, dbeta[:SPAN], dbeta[SPAN:]) * sig_small * (1.0 - sig_small)
        dsmall = jnp.where(lane < 2, dsig, jnp.where(lane == 2, -rate * dlog * sig_small, 0.0))
        dy_ref[lo:hi, 768:896] = dsmall.astype(LOW)
        yield
        dkey = beta * read_key + write_key
        dvalue = beta * dtarget

        def unit_back(grad, normed, scale):
            return scale * (grad - normed * jnp.sum(grad * normed, axis=1, keepdims=True))

        dact = jnp.concatenate(
            [
                unit_back(dquery, query, scale_q),
                unit_back(dkey[:SPAN], key0, scale_0),
                unit_back(dkey[SPAN:], key1, scale_1),
                dvalue[:SPAN],
                dvalue[SPAN:],
            ],
            axis=1,
        )
        dconv = dact * (sig * (1.0 + conv * (1.0 - sig)))
        yield
        here = pre_ref[lo:hi, :].astype(WIDE)
        if n:
            prior = pre_ref[lo - 16 : lo, :].astype(WIDE)
        else:
            prior = jnp.where(
                block == 0, edge_ref[...].astype(WIDE), prior_ref[...].astype(WIDE)
            )
        rows = stack(prior, here)
        dpre = taps_ref[0:1, :] * dconv
        dtaps_ref[0:1, :] += jnp.sum(dconv * here, axis=0, keepdims=True)
        for lag in range(1, 4):
            kept = jnp.where(pos >= lag, dconv, 0.0)
            shifted = rows[16 - lag : 16 - lag + SPAN]
            dtaps_ref[lag : lag + 1, :] += jnp.sum(kept * shifted, axis=0, keepdims=True)
            kept = kept * taps_ref[lag : lag + 1, :]
            dpre = dpre + stack(kept, next_ref[lag])[lag : lag + SPAN]
            next_ref[lag] = kept[0:8]
        dy_ref[lo:hi, 0:640] = dpre.astype(LOW)

    in_turns(local(n) for n in reversed(range(PER)))


def vmem_spec():
    return pl.BlockSpec(memory_space=pltpu.VMEM)


def smem_spec():
    return pl.BlockSpec(memory_space=pltpu.SMEM)


def fixed(shape):
    return pl.BlockSpec(shape, lambda *_: (0,) * len(shape))


def estimate(flops, mib):
    return pl.CostEstimate(flops=int(flops), bytes_accessed=int(mib * 2**20), transcendentals=0)


def run_forward(offs, rate, pre, gs, edge, taps, gain, state):
    tokens = pre.shape[0]
    spans = tokens // SPAN
    group = 8
    shape = jax.ShapeDtypeStruct
    outs = (
        (shape((tokens, 640), WIDE), pl.BlockSpec((group * SPAN, 640), lambda i: (i, 0))),
        (shape((spans, ROWS, ROWS), LOW), pl.BlockSpec((group, ROWS, ROWS), lambda i: (i, 0, 0))),
        (shape((spans, SPAN, ROWS), LOW), pl.BlockSpec((group, SPAN, ROWS), lambda i: (i, 0, 0))),
        (shape((spans, SPAN, HEAD), LOW), pl.BlockSpec((group, SPAN, HEAD), lambda i: (i, 0, 0))),
        (shape((spans, HEAD, HEAD), LOW), pl.BlockSpec((group, HEAD, HEAD), lambda i: (i, 0, 0))),
        (shape((spans, HEAD, HEAD), LOW), pl.BlockSpec((group, HEAD, HEAD), lambda i: (i, 0, 0))),
        (shape((tokens, HEAD), LOW), fixed((tokens, HEAD))),
        (shape((tokens, HEAD), WIDE), fixed((tokens, HEAD))),
        (shape((spans, ROWS, HEAD), LOW), fixed((spans, ROWS, HEAD))),
        (shape((spans, HEAD, HEAD), WIDE), fixed((spans, HEAD, HEAD))),
        (shape((HEAD, HEAD), WIDE), fixed((HEAD, HEAD))),
    )
    return pl.pallas_call(
        functools.partial(forward_kernel, spans, offs.shape[1] - 1, group),
        out_shape=[o for o, _ in outs],
        grid=(spans // group,),
        in_specs=[
            smem_spec(),
            smem_spec(),
            pl.BlockSpec((group * SPAN, 640), lambda i: (i, 0)),
            pl.BlockSpec((16, 640), lambda i: (jnp.maximum(i * (group * SPAN // 16) - 1, 0), 0)),
            pl.BlockSpec((group * SPAN, HEAD), lambda i: (i, 1)),
            fixed((tokens, HEAD)),
            fixed((16, 640)),
            fixed((8, 640)),
            fixed((1, HEAD)),
            fixed((HEAD, HEAD)),
        ],
        out_specs=[b for _, b in outs],
        scratch_shapes=[
            pltpu.VMEM((spans, ROWS, HEAD), LOW),
            pltpu.VMEM((spans, ROWS, HEAD), WIDE),
            pltpu.VMEM((spans, HEAD, HEAD), WIDE),
            pltpu.VMEM((spans, SPAN, HEAD), WIDE),
            pltpu.VMEM((spans, HEAD, HEAD), LOW),
            pltpu.VMEM((spans, HEAD, HEAD), LOW),
            pltpu.VMEM((spans, SPAN, HEAD), LOW),
        ],
        compiler_params=pltpu.CompilerParams(vmem_limit_bytes=VMEM_LIMIT),
        cost_estimate=estimate(70e9, 24),
        name="delta_forward",
    )(offs, rate, pre, pre, gs, gs, edge, taps, gain, state)


def run_gate_back(gs, gain, mixed, qh, high, rest, dgated, dend):
    tokens = mixed.shape[0]
    spans = tokens // SPAN
    shape = jax.ShapeDtypeStruct
    return pl.pallas_call(
        functools.partial(gate_back_kernel, spans),
        out_shape=(
            shape((spans, SPAN, HEAD), LOW),
            shape((spans, HEAD, HEAD), WIDE),
            shape((tokens, HEAD), LOW),
            shape((1, HEAD), WIDE),
            shape((HEAD, HEAD), WIDE),
        ),
        grid=(1,),
        in_specs=[
            fixed((tokens, HEAD)),
            fixed((1, HEAD)),
            fixed((tokens, HEAD)),
            fixed((spans, SPAN, HEAD)),
            fixed((spans, HEAD, HEAD)),
            fixed((spans, HEAD, HEAD)),
            fixed((tokens, HEAD)),
            fixed((HEAD, HEAD)),
        ],
        out_specs=(
            fixed((spans, SPAN, HEAD)),
            fixed((spans, HEAD, HEAD)),
            fixed((tokens, HEAD)),
            fixed((1, HEAD)),
            fixed((HEAD, HEAD)),
        ),
        scratch_shapes=[pltpu.VMEM((spans, HEAD, HEAD), WIDE)],
        compiler_params=pltpu.CompilerParams(vmem_limit_bytes=VMEM_LIMIT),
        cost_estimate=estimate(15e9, 8),
        name="delta_gate_back",
    )(gs, gain, mixed, qh, high, rest, dgated, dend)


def run_backward(last, steps, offs, rate, pre, gs, edge, taps, saved, carried, dy):
    conv, inverse, upd, scores, states, do, ds, dgate = saved
    tokens = pre.shape[0]

    def at(i):
        return last - i

    def rows(columns, lane=0):
        return pl.BlockSpec((PER * SPAN, columns), lambda i: (at(i), lane))

    def spans(a, b):
        return pl.BlockSpec((PER, a, b), lambda i: (at(i), 0, 0))

    shape = jax.ShapeDtypeStruct
    carried_specs = [fixed((4, 8, 640)), fixed((8, 640)), fixed((1, HEAD))]
    operands = [offs, rate, pre, pre, gs, edge, taps, conv, inverse, upd, scores, states, do, ds]
    operands += [dgate, *carried]
    in_specs = [
        smem_spec(),
        smem_spec(),
        rows(640),
        pl.BlockSpec((16, 640), lambda i: (jnp.maximum(at(i) * (PER * SPAN // 16) - 1, 0), 0)),
        rows(HEAD, 1),
        fixed((16, 640)),
        fixed((8, 640)),
        rows(640),
        spans(ROWS, ROWS),
        spans(ROWS, HEAD),
        spans(SPAN, ROWS),
        spans(HEAD, HEAD),
        spans(SPAN, HEAD),
        spans(HEAD, HEAD),
        rows(HEAD),
        *carried_specs,
    ]
    aliases = {}
    if dy is not None:
        aliases = {len(operands): 0}
        operands.append(dy)
        in_specs.append(pl.BlockSpec(memory_space=pl.ANY))
    dy, *carried = pl.pallas_call(
        functools.partial(backward_kernel, at, offs.shape[1] - 1),
        out_shape=(
            shape((tokens, 896), LOW),
            shape((4, 8, 640), WIDE),
            shape((8, 640), WIDE),
            shape((1, HEAD), WIDE),
        ),
        grid=(steps,),
        in_specs=in_specs,
        out_specs=(rows(896), *carried_specs),
        input_output_aliases=aliases,
        compiler_params=pltpu.CompilerParams(vmem_limit_bytes=VMEM_LIMIT),
        cost_estimate=estimate(4e9 * steps, 2.6 * steps),
        name="delta_backward",
    )(*operands)
    return dy, carried


def input_blocks_kernel(at_ref, dy_ref, out_ref, w_ref, send_ref, keep_ref):
    count = dy_ref.shape[0]
    block = contract(dy_ref[...], w_ref[...], 1, 1).astype(LOW)
    for n, to_ref in enumerate((send_ref, keep_ref)):

        @pl.when(pl.program_id(0) == n)
        def _():
            to_ref[:count, :] = block
            to_ref[count:, :] = out_ref[...]


def input_blocks(places, dy, grad_out, weights, count, out_rows):
    width = weights.shape[0]
    return pl.pallas_call(
        input_blocks_kernel,
        out_shape=[jax.ShapeDtypeStruct((count + out_rows, width), LOW)] * 2,
        grid_spec=pltpu.PrefetchScalarGridSpec(
            num_scalar_prefetch=1,
            grid=(2,),
            in_specs=[
                pl.BlockSpec((count, 896), lambda i, p: (p[i], 0)),
                pl.BlockSpec((out_rows, width), lambda i, p: (p[i], 0)),
                fixed(weights.shape),
            ],
            out_specs=[fixed((count + out_rows, width))] * 2,
        ),
        compiler_params=pltpu.CompilerParams(vmem_limit_bytes=VMEM_LIMIT),
        cost_estimate=estimate(4 * count * width * 896, 4),
        name="input_blocks",
    )(jnp.stack(places).astype(jnp.int32), dy, grad_out, weights)


def weight_grads_kernel(
    taps, at_ref, low_ref, dy_ref, w_ref, gain_ref, gff_ref, gh_ref, rate_ref, taps_ref, to_ref
):
    shard = w_ref.shape[0]
    grads = contract(low_ref[...], dy_ref[...], 0, 0)
    to_ref[:shard, :] = grads.astype(LOW)
    sums = jnp.sum(grads * w_ref[...].astype(WIDE), axis=1, keepdims=True)
    row = jnp.broadcast_to(sums, (shard, HEAD)).T[0:1] / gain_ref[...]

    def wide(value):
        return jnp.concatenate(
            [value, jnp.zeros((value.shape[0], 896 - value.shape[1]), WIDE)], axis=1
        )

    to_ref[shard:, :] = stack(
        wide(row),
        wide(gff_ref[...]),
        wide(gh_ref[0]),
        wide(rate_ref[...]),
        wide(taps_ref[:taps, :]),
        jnp.zeros((12 - taps, 896), WIDE),
    ).astype(LOW)


def weight_grads(order, low, dy, weights, gain, gain_ffn, gain_head, rate, taps_grad, taps):
    length, width = low.shape
    members = order.shape[0]
    shard = width // members
    gh = jnp.pad(gain_head.reshape(members, 1, -1), ((0, 0), (0, 0), (0, HEAD)))[:, :, :HEAD]
    return pl.pallas_call(
        functools.partial(weight_grads_kernel, taps),
        out_shape=jax.ShapeDtypeStruct((members * (shard + 16), 896), LOW),
        grid_spec=pltpu.PrefetchScalarGridSpec(
            num_scalar_prefetch=1,
            grid=(members,),
            in_specs=[
                pl.BlockSpec((length, shard), lambda i, p: (0, p[i])),
                fixed((length, 896)),
                pl.BlockSpec((shard, 896), lambda i, p: (p[i], 0)),
                pl.BlockSpec((1, shard), lambda i, p: (0, p[i])),
                pl.BlockSpec((1, shard), lambda i, p: (0, p[i])),
                pl.BlockSpec((1, 1, HEAD), lambda i, p: (p[i], 0, 0)),
                fixed((1, HEAD)),
                fixed((8, 640)),
            ],
            out_specs=pl.BlockSpec((shard + 16, 896), lambda i, p: (i, 0)),
        ),
        compiler_params=pltpu.CompilerParams(vmem_limit_bytes=VMEM_LIMIT),
        cost_estimate=estimate(2 * length * width * 896, 12),
        name="weight_grads",
    )(order, low, dy, weights, gain, gain_ffn, gh, rate, taps_grad)


def pack_kernel(
    heads, taps,
    place_ref, q_ref, k0_ref, k1_ref, v0_ref, v1_ref, g_ref, beta_ref, decay_ref, gin_ref,
    gff_ref, gh_ref, cq_ref, ck_ref, cv_ref, out_ref,
):
    h = place_ref[0]
    shard = q_ref.shape[0]
    for i, ref in enumerate((q_ref, k0_ref, k1_ref, v0_ref, v1_ref, g_ref)):
        out_ref[:shard, i * HEAD : (i + 1) * HEAD] = ref[...]
    beta, decay = beta_ref[...].astype(WIDE), decay_ref[...].astype(WIDE)

    def row_of(values, at):
        row = lax.broadcasted_iota(jnp.int32, values.shape, 0)
        return jnp.sum(jnp.where(row == at, values, 0.0), axis=0, keepdims=True)

    row = lax.broadcasted_iota(jnp.int32, (HEAD, shard), 0)
    small = jnp.where(row == 0, row_of(beta, h), 0.0)
    small = jnp.where(row == 1, row_of(beta, heads + h), small)
    small = jnp.where(row == 2, row_of(decay, h), small)
    out_ref[:shard, 6 * HEAD :] = small.T.astype(LOW)
    out_ref[shard:, :] = jnp.zeros((out_ref.shape[0] - shard, out_ref.shape[1]), LOW)
    vectors = stack(
        *[ref[...].astype(WIDE) for ref in (gin_ref, gff_ref, gh_ref, cq_ref)],
        *[
            ref[:, i * shard : (i + 1) * shard].astype(WIDE)
            for ref in (ck_ref, cv_ref)
            for i in range(2)
        ],
        jnp.zeros((32 - 3 - 5 * taps, shard), WIDE),
    )
    out_ref[shard:, :shard] = vectors.astype(LOW)


def pack_weights(
    head, w_query, w_key, w_value, w_outgate, w_beta, w_decay, gain_in, gain_ffn, gain_head,
    conv_query, conv_key, conv_value,
):
    shard, heads = w_decay.shape
    taps = conv_query.shape[0]

    def part(step):
        return pl.BlockSpec((shard, HEAD), lambda i, h: (0, step * heads + h[0]))

    small = (
        w_beta.T, w_decay.T, gain_in[None], gain_ffn[None],
        jnp.pad(gain_head, (0, shard - gain_head.shape[0]))[None],
        conv_query, conv_key, conv_value,
    )
    return pl.pallas_call(
        functools.partial(pack_kernel, heads, taps),
        out_shape=jax.ShapeDtypeStruct((shard + 32, 896), LOW),
        grid_spec=pltpu.PrefetchScalarGridSpec(
            num_scalar_prefetch=1,
            grid=(1,),
            in_specs=[part(0), part(0), part(1), part(0), part(1), part(0)]
            + [fixed(a.shape) for a in small],
            out_specs=fixed((shard + 32, 896)),
        ),
        compiler_params=pltpu.CompilerParams(vmem_limit_bytes=VMEM_LIMIT),
        cost_estimate=estimate(0, 2),
        name="pack_weights",
    )(head.reshape(1), w_query, w_key, w_key, w_value, w_value, w_outgate, *small)


def project_kernel(count, place_ref, gain_ref, w_ref, *refs):
    tok_refs, (low_ref, pre_ref, gs_ref) = refs[:count], refs[count:]
    for n in range(count):

        @pl.when(pl.program_id(0) == n)
        def _():
            values = tok_refs[n][...].astype(WIDE)
            scale = lax.rsqrt(jnp.mean(values * values, axis=1, keepdims=True) + EPSILON)
            low_ref[...] = (values * scale * gain_ref[...]).astype(LOW)

    normed = low_ref[...]
    pre_ref[...] = contract(normed, w_ref[:, :640], 1, 0).astype(LOW)
    gs_ref[...] = contract(normed, w_ref[:, 640:], 1, 0)


def project(found, gain, weights):
    blocks = [one for a, x, b, y in found for one in ((a, x), (b, y))]
    places = jnp.stack([place for place, _ in blocks]).astype(jnp.int32)
    count, (rows, width) = len(blocks), blocks[0][1].shape
    shape = jax.ShapeDtypeStruct
    return pl.pallas_call(
        functools.partial(project_kernel, count),
        out_shape=[
            shape((count * rows, n), t) for n, t in ((width, LOW), (640, LOW), (256, WIDE))
        ],
        grid_spec=pltpu.PrefetchScalarGridSpec(
            num_scalar_prefetch=1,
            grid=(count,),
            in_specs=[fixed(gain.shape), fixed(weights.shape)] + [fixed((rows, width))] * count,
            out_specs=[
                pl.BlockSpec((rows, n), lambda i, p: (p[i], 0)) for n in (width, 640, 256)
            ],
        ),
        compiler_params=pltpu.CompilerParams(vmem_limit_bytes=VMEM_LIMIT),
        cost_estimate=estimate(2 * count * rows * width * 896, 13),
        name="project",
    )(places, gain, weights, *(value for _, value in blocks))


def rms_parts(values):
    return values * lax.rsqrt(jnp.mean(values * values, axis=-1, keepdims=True) + EPSILON)


def rms_back(grad_scaled, values):
    scale = lax.rsqrt(jnp.mean(values * values, axis=-1, keepdims=True) + EPSILON)
    normed = values * scale
    return scale * (
        grad_scaled - normed * jnp.mean(grad_scaled * normed, axis=-1, keepdims=True)
    )


def dot_plain(left, right, kind=WIDE):
    return jnp.dot(left, right, preferred_element_type=kind)


def dot_left(left, right, kind=WIDE):
    return contract(left, right, 0, 0).astype(kind)


def dot_right(left, right):
    return contract(left, right, 1, 1)


def exchanged(value, axis, bit):
    size = lax.axis_size(axis)
    return lax.ppermute(value, axis, [(i, i ^ bit) for i in range(size)])


def near_order(size):
    order, bit = [0], size // 2
    while bit:
        order = order + [o ^ bit for o in order]
        bit //= 2
    return order


def near_gather(value, axis, first=None):
    bit = lax.axis_size(axis) // 2
    while bit:
        value = stack(value, exchanged(value, axis, bit) if first is None else first)
        first = None
        bit //= 2
    return value


def near_scatter(value, axis):
    size, bit = lax.axis_size(axis), 1
    while bit < size:
        half = value.shape[0] // 2
        came = exchanged(value[half:].astype(LOW), axis, bit).astype(WIDE)
        value = value[:half].astype(WIDE) + came
        bit *= 2
    return value


def near_scatter_stages(value, axis, ties):
    size, bit = lax.axis_size(axis), 1
    while bit < size:
        half = value.shape[0] // 2
        value = after(value, *ties)
        came = exchanged(value[half:].astype(LOW), axis, bit)
        yield [came]
        value = value[:half].astype(WIDE) + came.astype(WIDE)
        bit *= 2
    yield value


def near_blocks(value, axis):
    size, me = lax.axis_size(axis), lax.axis_index(axis)
    return stack(
        *[lax.dynamic_index_in_dim(value, me ^ o, 0, False) for o in near_order(size)]
    )


def ordered_step(value, other, axis, bit):
    mine_first = (lax.axis_index(axis) & bit) == 0
    pair = jnp.where(mine_first, jnp.stack([value, other], 1), jnp.stack([other, value], 1))
    return pair.reshape((pair.shape[0] * 2,) + value.shape[1:])


def ordered_gather(value, axis, first=None):
    bit = lax.axis_size(axis) // 2
    value = value[None]
    while bit:
        other = exchanged(value, axis, bit) if first is None else first[None]
        value = ordered_step(value, other, axis, bit)
        first = None
        bit //= 2
    return value


def far_exchange(value, axis):
    return exchanged(value, axis, lax.axis_size(axis) // 2)


def after(value, *done):
    return lax.optimization_barrier((value, *done))[0]


def team_step(value, team, move):
    size = lax.axis_size("seq")
    pairs = [(t + i, t + move(i)) for t in range(0, size, team) for i in range(team)]
    return lax.ppermute(value, "seq", pairs)


def turn(value, team, by):
    return team_step(value, team, lambda i: (i + 2 * by) % team)


def cross(value, team):
    return team_step(value, team, lambda i: i ^ 1)


def rolled(value, by, axis):
    twice = jnp.concatenate([value, value], axis=axis)
    return lax.dynamic_slice_in_dim(twice, by, value.shape[axis], axis)


def swapped(blocks, team):
    return [blocks[0]] + [
        team_step(blocks[k], team, lambda i: (i - k) % team) for k in range(1, team)
    ]


def turns(team):
    half = team // 2
    return [0] + [k for n in range(1, half // 2 + 1) for k in dict.fromkeys((n, half - n))]


def gather_stages(value, team, ties=(), lag=1):
    me = lax.axis_index("seq") % team
    half = team // 2
    turned, found, brought = {0: value}, [], []
    if half > 1:
        turned[1] = turn(value, team, 1)
    if half > 2:
        turned[half - 1] = turn(after(value, turned[1]), team, -1)
    for k in turns(team):
        across = cross(after(turned[k], *brought[-lag:][: len(brought) - lag + 1], *ties), team)
        stage = [across]
        for n in (k + 1, k - 1):
            if 0 < n < half and n not in turned and k:
                turned[n] = turn(turned[k], team, 1 if n > k else -1)
                stage.append(turned[n])
        brought.append(across)
        found.append(((me - 2 * k) % team, turned[k], ((me ^ 1) - 2 * k) % team, across))
        yield stage
    yield found


def last_of(stages):
    for stage in stages:
        pass
    return stage


def team_places(team):
    me = lax.axis_index("seq") % team
    return [
        (((me ^ 1) + 2 * k) % team, (me + 2 * k) % team) for k in reversed(turns(team))
    ]


def scatter_stages(blocks, team, ties=()):
    half = team // 2
    passing, leaving, before = {}, None, ()
    for (send, keep), k in zip(blocks, reversed(turns(team))):
        came = cross(after(send, *before, *ties), team)
        stage = [came]
        if leaving is not None:
            pair, n = leaving
            forward = 2 * n <= half
            to = n - 1 if forward else (n + 1) % half
            moved = turn(pair.astype(LOW), team, 1 if forward else -1)
            stage.append(moved)
            passing[to] = passing.get(to, []) + [moved]
        yield stage
        before = (came,)
        keep = keep(came) if callable(keep) else keep
        pair = keep.astype(WIDE) + came.astype(WIDE)
        for moved in passing.pop(k, []):
            pair = pair + moved.astype(WIDE)
        leaving = (pair, k)
    yield pair


def mixer_outputs_kernel(heads, taps, fsdp, place_ref, *refs):
    got_refs, out_refs, refs = refs[:heads], refs[heads : 2 * heads], refs[2 * heads :]
    (q_ref, k_ref, v_ref, g_ref, b_ref, d_ref, gin_ref, gff_ref, gh_ref, rate_ref, cq_ref,
     ck_ref, cv_ref, out_ref) = refs
    member = place_ref[0, heads]
    shard = q_ref.shape[0]
    gains = gh_ref.shape[1]
    width = heads * HEAD
    lane_r = lax.broadcasted_iota(jnp.int32, (1, heads), 1)
    rates = jnp.zeros((1, heads), WIDE)
    vectors = jnp.zeros((8, shard), WIDE)
    for n in range(heads):
        got_ref = got_refs[n]
        h = place_ref[0, n]

        def columns(step):
            return pl.ds(pl.multiple_of(step * width + h * HEAD, HEAD), HEAD)

        q_ref[:, columns(0)] = got_ref[:shard, 0:128].astype(WIDE)
        for i in range(2):
            k_ref[:, columns(i)] = got_ref[:shard, 128 + i * 128 : 256 + i * 128].astype(WIDE)
            v_ref[:, columns(i)] = got_ref[:shard, 384 + i * 128 : 512 + i * 128].astype(WIDE)
        g_ref[:, columns(0)] = got_ref[:shard, 640:768].astype(WIDE)
        last = got_ref[:shard, 768:896].astype(WIDE).T
        b_ref[pl.ds(h, 1), :] = last[0:1]
        b_ref[pl.ds(heads + h, 1), :] = last[1:2]
        d_ref[pl.ds(h, 1), :] = last[2:3]
        extra = got_ref[shard:, :].astype(WIDE)
        vectors = vectors + extra[0:8, :shard]
        rates = jnp.where(lane_r == h, extra[3:4, 2:3], rates)
        rows = out_refs[n].shape[0]
        out_ref[pl.ds(pl.multiple_of(h * rows, rows), rows), :] = out_refs[n][...].astype(WIDE)
        for ref, at, steps in ((cq_ref, 0, 1), (ck_ref, 128, 2), (cv_ref, 384, 2)):
            per = ref.shape[1] // HEAD
            for i in range(steps):
                slot = i * heads + h - member * per

                @pl.when((slot >= 0) & (slot < per))
                def _():
                    to = pl.ds(pl.multiple_of(slot * HEAD, HEAD), HEAD)
                    ref[:, to] = extra[4 : 4 + taps, at + i * HEAD : at + (i + 1) * HEAD]

    rate_ref[...] = rates
    gin_ref[...] = vectors[0:1]
    gff_ref[...] = vectors[1:2]
    gh_ref[...] = vectors[2:3, :gains]


def mixer_outputs(found, found_out, shard, gains, taps, fsdp, member):
    found, found_out = (
        [one for a, x, b, y in pairs for one in ((a, x), (b, y))] for pairs in (found, found_out)
    )
    heads = len(found)
    places = jnp.stack([place for place, _ in found] + [member])[None].astype(jnp.int32)
    width = heads * HEAD
    shape = jax.ShapeDtypeStruct
    outs = (
        shape((shard, width), WIDE),
        shape((shard, 2 * width), WIDE),
        shape((shard, 2 * width), WIDE),
        shape((shard, width), WIDE),
        shape((2 * heads, shard), WIDE),
        shape((heads, shard), WIDE),
        shape((1, shard), WIDE),
        shape((1, shard), WIDE),
        shape((1, gains), WIDE),
        shape((1, heads), WIDE),
        shape((taps, shard), WIDE),
        shape((taps, 2 * shard), WIDE),
        shape((taps, 2 * shard), WIDE),
        shape((shard, width), WIDE),
    )
    return pl.pallas_call(
        functools.partial(mixer_outputs_kernel, heads, taps, fsdp),
        out_shape=outs,
        in_specs=[smem_spec()] + [vmem_spec()] * (2 * heads),
        out_specs=[vmem_spec()] * len(outs),
        compiler_params=pltpu.CompilerParams(vmem_limit_bytes=VMEM_LIMIT),
        cost_estimate=estimate(0, 12),
        name="mixer_outputs",
    )(places, *(value for _, value in found), *(value for _, value in found_out))


def ff_outputs_kernel(count, slab, shard, place_ref, *refs):
    got_refs, (gate_ref, up_ref, down_ref), held = refs[:count], refs[count : count + 3], refs[-1]
    own = count * slab
    for n, got_ref in enumerate(got_refs):
        at = place_ref[n] * slab
        piece = got_ref[...].astype(WIDE)
        for m in range(2):
            for k in range(2):
                to = pl.multiple_of(k * own + at, 8)
                held[m, pl.ds(to, slab), :] = piece[
                    m * slab : (m + 1) * slab, k * shard : (k + 1) * shard
                ]
        down_ref[pl.ds(pl.multiple_of(at, 8), slab), :] = piece[2 * slab :]
    gate_ref[...] = held[0].T
    up_ref[...] = held[1].T


def ff_outputs(found, slab, shard, fsdp):
    found = [one for a, x, b, y in found for one in ((a, x), (b, y))]
    count, (rows, width) = len(found), found[0][1].shape
    own = count * slab
    shape = jax.ShapeDtypeStruct
    return pl.pallas_call(
        functools.partial(ff_outputs_kernel, count, slab, shard),
        out_shape=(
            shape((shard, fsdp * own), WIDE),
            shape((shard, fsdp * own), WIDE),
            shape((own, width), WIDE),
        ),
        grid_spec=pltpu.PrefetchScalarGridSpec(
            num_scalar_prefetch=1,
            grid=(fsdp // 2,),
            in_specs=[pl.BlockSpec((rows, 2 * shard), lambda i, p: (0, i))] * count,
            out_specs=(
                pl.BlockSpec((shard, 2 * own), lambda i, p: (0, i)),
                pl.BlockSpec((shard, 2 * own), lambda i, p: (0, i)),
                pl.BlockSpec((own, 2 * shard), lambda i, p: (0, i)),
            ),
            scratch_shapes=[pltpu.VMEM((2, 2 * own, shard), WIDE)],
        ),
        compiler_params=pltpu.CompilerParams(vmem_limit_bytes=VMEM_LIMIT),
        cost_estimate=estimate(0, 15),
        name="ff_outputs",
    )(jnp.stack([p for p, _ in found]).astype(jnp.int32), *(x for _, x in found))


def ff_outputs_plain(got, slab, shard, fsdp):
    seq, rows, width = got.shape
    own = seq * slab
    wide = got.astype(WIDE)

    def turned(at):
        part = wide[:, at : at + slab].reshape(seq, slab, fsdp, shard)
        return jnp.transpose(part, (3, 2, 0, 1)).reshape(shard, fsdp * own)

    return turned(0), turned(slab), wide[:, 2 * slab :].reshape(own, width)


def per_device(
    tokens, cotangent, offsets, gain_in, w_query, w_key, w_value, w_beta, w_decay, w_outgate,
    conv_query, conv_key, conv_value, decay_scale, gain_head, w_out, gain_ffn, w_gate, w_up,
    w_down,
):
    seq, fsdp = lax.axis_size("seq"), lax.axis_size("fsdp")
    heads = decay_scale.shape[0]
    taps = conv_query.shape[0]
    own_rows = tokens.shape[1]
    shard = w_query.shape[0]
    width = shard * fsdp
    teams = seq // heads
    assert teams * heads == seq and width == heads * HEAD
    place = lax.axis_index("seq")
    head, team = place % heads, place // heads
    member = lax.axis_index("fsdp")
    if teams == 1:
        team_groups, head_groups = None, None
    else:
        team_groups = [[t * heads + h for h in range(heads)] for t in range(teams)]
        head_groups = [[t * heads + h for t in range(teams)] for h in range(heads)]

    def gather_rows(value):
        return lax.all_gather(value, "fsdp", axis=0, tiled=True)

    start_ties = []
    spread = gather_stages(tokens[0], heads, start_ties)
    came = next(spread)[:1]
    length = heads * own_rows

    def column_blocks(value):
        return jnp.transpose(value.reshape(shard, fsdp, value.shape[1] // fsdp), (1, 0, 2))

    packed = pack_weights(
        head, after(w_query, came[0]), w_key, w_value, w_outgate, w_beta, w_decay, gain_in,
        gain_ffn, gain_head, conv_query, conv_key, conv_value,
    )
    far_packed = far_exchange(packed, "fsdp")
    start_ties[:] = [packed]
    came += next(spread)[:1]
    columns = jnp.stack(
        [column_blocks(after(w_gate, came[1])), column_blocks(after(w_up, came[1]))], axis=1
    )
    others = near_order(fsdp)[1:]
    column_sends = [lax.dynamic_index_in_dim(columns, member ^ o, 0, False) for o in others]
    start_ties[:] = [far_packed]
    came += next(spread)[:1]
    far_out = far_exchange(after(w_out, far_packed), "fsdp")
    got = ordered_gather(packed, "fsdp", far_packed)
    start_ties[:] = [got, far_out, *column_sends]
    for stage in spread:
        found = stage
        came += stage[:1]
    came = [one for one in came if not isinstance(one, tuple)]
    came += [came[-1]] * 3
    full_packed = got[:, :shard].reshape(width, 896)
    vectors = got[:, shard:, :shard]
    full_gain_in = vectors[:, 0].reshape(width).astype(WIDE)
    full_gain_ffn = vectors[:, 1].reshape(width).astype(WIDE)
    full_gain_head = vectors[:, 2, : gain_head.shape[0]].reshape(1, HEAD).astype(WIDE)

    def head_taps_of(row, pieces, step):
        column = step * width + head * HEAD
        inside = column % (pieces * shard)
        at = (column // (pieces * shard), row + inside // shard * taps, inside % shard)
        return lax.dynamic_slice(vectors, at, (1, taps, HEAD))[0]

    head_taps = jnp.concatenate(
        [head_taps_of(3, 1, 0)]
        + [head_taps_of(3 + taps, 2, i) for i in range(2)]
        + [head_taps_of(3 + 3 * taps, 2, i) for i in range(2)],
        axis=1,
    ).astype(WIDE)
    head_taps = jnp.pad(head_taps, ((0, 8 - taps), (0, 0)))
    def column_blocks(value):
        return jnp.transpose(value.reshape(shard, fsdp, value.shape[1] // fsdp), (1, 0, 2))

    cot = after(cotangent[0], came[2])
    far_cot = far_exchange(cot, "fsdp")
    column_got = [
        exchanged(after(send, came[2]), "fsdp", o) for o, send in zip(others, column_sends)
    ]
    normed_low, pre, gate_small = project(found, full_gain_in[None], full_packed)
    offs = jnp.concatenate(
        [offsets, jnp.broadcast_to(team * length, (1, 1)).astype(jnp.int32)], axis=1
    )
    rate = lax.dynamic_slice_in_dim(decay_scale, head, 1).reshape(1, 1)
    zero_state = jnp.zeros((HEAD, HEAD), WIDE)
    if teams == 1:
        edge = jnp.zeros((16, 640), LOW)
    else:
        forth = [(i, i + heads) for i in range(seq - heads)]
        back = [(i + heads, i) for i in range(seq - heads)]
        edge = lax.ppermute(pre[-16:], "seq", forth)

    def forward_from(state):
        return run_forward(
            offs, rate, pre, gate_small, edge, head_taps, full_gain_head, state
        )

    state_in = zero_state
    if teams > 1:
        trial = forward_from(zero_state)
        steps, end = trial[4].astype(WIDE) + trial[5].astype(WIDE), trial[10]

        def along(c, total):
            return jnp.dot(total, steps[c].T, precision=lax.Precision.HIGHEST)

        whole_map = lax.fori_loop(0, steps.shape[0], along, jnp.eye(HEAD, dtype=WIDE))
        for _ in range(teams - 1):
            out = jnp.dot(state_in, whole_map, precision=lax.Precision.HIGHEST) + end
            state_in = lax.ppermute(out.astype(LOW), "seq", forth).astype(WIDE)
    conv, inverse, scores, reach, high, rest, gated, mixed, upd, states, _ = forward_from(state_in)
    gated, far_out, far_cot, *column_got = lax.optimization_barrier(
        (gated, far_out, far_cot, *column_got)
    )
    own_columns = lax.dynamic_index_in_dim(columns, member, 0, False)
    full_out = ordered_gather(w_out, "fsdp", far_out).reshape(width, width)
    group_cot = near_gather(cot, "fsdp", far_cot)

    def ordered_columns(which):
        value = jnp.zeros((width, own_columns.shape[2]), LOW)
        for o, rows in zip([0, *others], [own_columns, *column_got]):
            value = lax.dynamic_update_slice(value, rows[which], ((member ^ o) * shard, 0))
        return value

    cols_gate, cols_up = ordered_columns(0), ordered_columns(1)

    pieces = [
        lax.dynamic_slice_in_dim(gated, (head - k) % heads * own_rows, own_rows, 0)
        for k in range(heads)
    ]
    gated_own = rolled(
        jnp.concatenate(swapped(pieces, heads), axis=1), (heads - head) % heads * HEAD, 1
    )
    inputs = tokens[0].astype(WIDE)
    mixer_res = inputs + dot_plain(gated_own, full_out)

    mid_normed = rms_parts(mixer_res)
    mid_low = (mid_normed * full_gain_ffn).astype(LOW)
    group_mid = near_gather(mid_low, "fsdp")
    gate_pre = dot_plain(group_mid, cols_gate)
    up_pre = dot_plain(group_mid, cols_up)
    sig = jax.nn.sigmoid(gate_pre)
    act = gate_pre * sig
    hidden = (act * up_pre).astype(LOW)
    grad_hidden = dot_right(group_cot, w_down)
    grad_gate_pre = (grad_hidden * up_pre * (sig * (1.0 + gate_pre * (1.0 - sig)))).astype(LOW)
    grad_up_pre = (grad_hidden * act).astype(LOW)
    grad_mid = dot_right(grad_gate_pre, cols_gate) + dot_right(grad_up_pre, cols_up)
    grad_gate_pre, grad_up_pre, grad_mid = lax.optimization_barrier(
        (grad_gate_pre, grad_up_pre, grad_mid)
    )
    grad_mid = near_scatter(grad_mid, "fsdp")

    grad_res = cotangent[0].astype(WIDE) + rms_back(grad_mid * full_gain_ffn, mixer_res)
    grad_gain_ffn = jnp.sum(grad_mid * mid_normed, axis=0)
    res_low = grad_res.astype(LOW)
    grad_gated = dot_right(res_low, full_out).astype(LOW)
    own_ff = w_down.shape[0]
    slab = own_ff // seq
    slabs = jnp.concatenate(
        [
            dot_left(grad_gate_pre, group_mid, LOW).reshape(seq, slab, width),
            dot_left(grad_up_pre, group_mid, LOW).reshape(seq, slab, width),
            dot_left(hidden, group_cot, LOW).reshape(seq, slab, width),
        ],
        axis=1,
    )
    permuted = teams == 1 and slab % 8 == 0 and own_ff * 2 % HEAD == 0 and fsdp % 2 == 0

    def turned_columns(summed):
        turned = lax.all_to_all(summed[: 2 * slab], "fsdp", 1, 1, tiled=True)
        return stack(turned, summed[2 * slab :])

    def feed_forward_sums():
        if not permuted:
            summed = lax.psum_scatter(
                slabs.reshape(seq * 3 * slab, width), "seq", scatter_dimension=0, tiled=True
            )
            yield [summed]
            slabs_done = lax.all_gather(turned_columns(summed), "seq", axis=0)
            yield ff_outputs_plain(slabs_done, slab, shard, fsdp)
            return
        def kept(at):
            return lambda came: lax.dynamic_index_in_dim(after(slabs, came), at, 0, False)

        blocks = [
            (lax.dynamic_index_in_dim(slabs, send, 0, False), kept(keep))
            for send, keep in team_places(heads)
        ]
        for stage in scatter_stages(blocks, heads, ties):
            if isinstance(stage, list):
                yield stage
        mine = turned_columns(after(stage.astype(LOW), *ties))
        yield [mine]
        for stage in gather_stages(mine, heads, ties):
            if isinstance(stage[0], tuple):
                break
            yield stage
        yield ff_outputs(stage, slab, shard, fsdp)

    ties, sums = [], feed_forward_sums()
    brought = [next(sums)]

    def beside(value):
        if not isinstance(brought[-1], tuple):
            ties[:] = [value]
            brought.append(next(sums))

    def settled(value):
        stage = brought[-1]
        return value if isinstance(stage, tuple) else after(value, *stage)

    pieces = [
        lax.dynamic_slice_in_dim(grad_gated, (head - k) % heads * HEAD, HEAD, 1)
        for k in range(heads)
    ]
    dgated = rolled(
        jnp.concatenate(swapped(pieces, heads), axis=0), (heads - head) % heads * own_rows, 0
    )
    grad_out = dot_left(after(gated_own, grad_gated), res_low, LOW).reshape(fsdp, shard, width)
    late = near_blocks(grad_out, "fsdp")
    dgated, late = lax.optimization_barrier((dgated, late))
    beside(dgated)
    late_ties = []
    late = near_scatter_stages(late, "fsdp", late_ties)
    late_stage = []

    def gate_back_from(dend):
        return run_gate_back(
            gate_small, full_gain_head, mixed, reach, high, rest, dgated, dend
        )

    dend = zero_state
    if teams > 1:
        begin = gate_back_from(zero_state)[4]
        for _ in range(teams - 1):
            out = lax.dot_general(
                dend, whole_map, (((1,), (1,)), ((), ())), precision=lax.Precision.HIGHEST
            )
            dend = lax.ppermute((out + begin).astype(LOW), "seq", back).astype(WIDE)
    do, ds, dgate, dgain, _ = gate_back_from(dend)
    carried = [
        jnp.zeros((4, 8, 640), WIDE), jnp.zeros((8, 640), WIDE), jnp.zeros((1, HEAD), WIDE)
    ]
    dy, calls = None, 2
    left = length // (PER * SPAN)
    for call in range(calls, 0, -1):
        steps_here = -(-left // call)
        if dy is None:
            carried[0] = after(carried[0], do)
        carried[0] = settled(after(carried[0], *late_stage))
        beside(carried[0])
        late_ties[:] = [carried[0]]
        late_stage = next(late)
        late_stage = late_stage if isinstance(late_stage, list) else [late_stage]
        dy, carried = run_backward(
            left - 1, steps_here, offs, rate, pre, gate_small, edge, head_taps,
            (conv, inverse, upd, scores, states, do, ds, dgate), carried, dy,
        )
        carried = list(carried)
        left -= steps_here
    dy = settled(dy)
    late_stage = late_stage[0]
    for stage in late:
        late_stage = stage
    grad_out = late_stage.astype(LOW)
    following, dtaps, drate = carried
    if teams > 1:
        none = jnp.zeros((16, 640), WIDE)
        dedge = sum(stack(none, following[lag])[lag : lag + 16] for lag in range(1, 4))
        from_next = lax.ppermute(dedge.astype(LOW), "seq", back).astype(WIDE)
        tail = (dy[-16:, :640].astype(WIDE) + from_next).astype(LOW)
        dy = lax.dynamic_update_slice(dy, tail, (length - 16, 0))

    out_rows = shard // heads

    blocks = [
        list(input_blocks(places, dy, grad_out, full_packed, own_rows, out_rows))
        for places in team_places(heads)
    ]
    turned_stage = []
    if not isinstance(brought[-1], tuple):
        beside(blocks[0][0])
        turned_stage = brought[-1] if isinstance(brought[-1], list) else []
    order = jnp.stack([member ^ o for o in near_order(fsdp)]).astype(jnp.int32)
    combined = weight_grads(
        order, normed_low, after(dy, blocks[0][0], *turned_stage), full_packed, full_gain_in[None],
        grad_gain_ffn[None], dgain, drate, dtaps, taps,
    )
    sent = scatter_stages(blocks, heads)
    queue = [next(sent)]
    combined = near_scatter(after(combined, queue[0][0]), "fsdp").astype(LOW)
    *more, joined = sent
    queue += more
    while not isinstance(brought[-1], tuple):
        beside(blocks[0][0])
    out_gate, out_up, out_down = brought[-1]
    down_part = near_scatter(dot_plain(after(hidden, queue[1][0]), w_down).astype(LOW), "fsdp")
    layer_out = (mixer_res + down_part).astype(LOW)
    grad_normed, own_out = joined[:own_rows], joined[own_rows:].astype(LOW)
    input_grad = (grad_res + rms_back(grad_normed * full_gain_in, inputs)).astype(LOW)
    if teams > 1:
        own_out = lax.psum(own_out, "seq", axis_index_groups=head_groups)
    found_out = last_of(gather_stages(own_out, heads))

    if teams > 1:
        combined = lax.psum(combined, "seq", axis_index_groups=head_groups)
    (out_query, out_key, out_value, out_gatew, out_beta, out_decay, out_gain_in, out_gain_ffn,
     out_gain_head, out_rate, out_cq, out_ck, out_cv, out_out) = mixer_outputs(
        last_of(gather_stages(combined, heads, lag=1)), found_out, shard, gain_head.shape[0], taps, fsdp, member
    )

    return (
        layer_out[None],
        input_grad[None],
        out_gain_in[0],
        out_query,
        out_key,
        out_value,
        out_beta.T,
        out_decay.T,
        out_gatew,
        out_cq,
        out_ck,
        out_cv,
        out_rate[0],
        out_gain_head[0],
        out_out,
        out_gain_ffn[0],
        out_gate,
        out_up,
        out_down,
    )


def solution(mesh):
    rows, lanes = P("fsdp", None), P(None, "fsdp")
    block = P("fsdp", "seq", None)
    return jax.shard_map(
        per_device,
        mesh=mesh,
        in_specs=(
            block, block, rows, P("fsdp"), rows, rows, rows, rows, rows, rows,
            lanes, lanes, lanes, P(), P("fsdp"), rows, P("fsdp"), rows, rows, rows,
        ),
        out_specs=(
            block, block, P("fsdp"), rows, rows, rows, rows, rows, rows,
            lanes, lanes, lanes, P(), P("fsdp"), rows, P("fsdp"), rows, rows, rows,
        ),
        check_vma=False,
    )
```

```python
import functools

import jax
import jax.numpy as jnp
from jax import lax
from jax.experimental import pallas as pl
from jax.experimental.pallas import tpu as pltpu
from jax.sharding import PartitionSpec as P

SPAN = 64
PER = 4
ROWS = 128
HEAD = 128
EPSILON = 1e-06
LOW = jnp.bfloat16
WIDE = jnp.float32
VMEM_LIMIT = 56 * 1024 * 1024


def contract(left, right, left_dim, right_dim):
    return lax.dot_general(
        left, right, (((left_dim,), (right_dim,)), ((), ())), preferred_element_type=WIDE
    )


def halves(value):
    high = value.astype(LOW)
    return high, (value - high.astype(WIDE)).astype(LOW)


def mm(left, right, left_dim=1, right_dim=0):
    return contract(left.astype(LOW), right.astype(LOW), left_dim, right_dim)


def stack(*parts):
    return jnp.concatenate(parts, axis=0)


def row_maps():
    row = lax.broadcasted_iota(jnp.int32, (ROWS, ROWS), 0)
    col = lax.broadcasted_iota(jnp.int32, (ROWS, ROWS), 1)
    tok, step = row & (SPAN - 1), row >> 6
    tok_c, step_c = col & (SPAN - 1), col >> 6
    return tok, step, tok_c, step_c


def span_tokens(offs_ref, doc_count, first):
    place = first + lax.broadcasted_iota(jnp.int32, (SPAN, 1), 0)
    begin = jnp.zeros((SPAN, 1), jnp.int32)
    for j in range(doc_count):
        start = offs_ref[0, j]
        begin = jnp.where(place >= start, start, begin)
    return place - begin


def softplus(value):
    return jnp.maximum(value, 0.0) + jnp.log1p(jnp.exp(-jnp.abs(value)))


def decay_sums(small, rate):
    logs = -rate * softplus(small)
    tok = lax.broadcasted_iota(jnp.int32, (SPAN, SPAN), 0)
    tok_c = lax.broadcasted_iota(jnp.int32, (SPAN, SPAN), 1)
    lower = jnp.where(tok >= tok_c, 1.0, 0.0).astype(LOW)
    tok_w = lax.broadcasted_iota(jnp.int32, (SPAN, ROWS), 0)
    tok_wc = lax.broadcasted_iota(jnp.int32, (SPAN, ROWS), 1) & (SPAN - 1)
    upper = jnp.where(tok_w <= tok_wc, 1.0, 0.0).astype(LOW)
    high, rest = halves(logs)
    cols = contract(lower, high, 1, 0) + contract(lower, rest, 1, 0)
    rows = contract(high, upper, 0, 0) + contract(rest, upper, 0, 0)
    return cols[:, 2:3], rows[2:3, :]


def unit(values):
    scale = lax.rsqrt(jnp.sum(values * values, axis=1, keepdims=True) + EPSILON)
    return values * scale, scale


def span_factors(small, rate, pos):
    sig = jax.nn.sigmoid(small)
    cum, cum_row = decay_sums(small, rate)
    beta = stack(sig[:, 0:1], sig[:, 1:2])
    cum2, pos2 = stack(cum, cum), stack(pos, pos)
    tok, step, tok_c, step_c = row_maps()
    before = tok > tok_c
    here = tok == tok_c
    reach = (before | (here & (step >= step_c))) & (tok - tok_c <= pos2)
    decay = jnp.where(reach, jnp.exp(jnp.where(reach, cum2 - cum_row, 0.0)), 0.0)
    strict = before | (here & (step > step_c))
    tok1 = tok[:, 0:1]
    carry = jnp.where(pos2 > tok1, jnp.exp(cum2), 0.0)
    end, end_pos = cum[SPAN - 1 : SPAN], pos[SPAN - 1 : SPAN]
    leave = jnp.where(SPAN - 1 - tok1 <= end_pos, jnp.exp(end - cum2), 0.0)
    carry_all = jnp.where(end_pos >= SPAN, jnp.exp(end), 0.0)
    return beta, decay, strict, carry, leave, carry_all, tok ^ tok_c


def in_turns(bodies):
    bodies = list(bodies)
    while bodies:
        bodies = [body for body in bodies if next(body, "end") != "end"]


def unit_lower_inverse(strict_part, apart):
    row = lax.broadcasted_iota(jnp.int32, (ROWS, ROWS), 0)
    col = lax.broadcasted_iota(jnp.int32, (ROWS, ROWS), 1)
    inverse = jnp.where(row == col, 1.0, 0.0) - jnp.where(apart == 0, strict_part, 0.0)
    for level in range(6):
        block = jnp.where((apart >> level) == 1, strict_part, 0.0)
        low = inverse.astype(LOW)
        half = contract(low, block.astype(LOW), 1, 0).astype(LOW)
        yield
        inverse = inverse - contract(half, low, 1, 0)
        yield
    return inverse


def conv_rows(prior, here):
    return stack(prior.astype(WIDE), here.astype(WIDE))


def forward_kernel(
    span_count, doc_count, group,
    offs_ref, rate_ref, pre_ref, prior_ref, small_ref, gate_ref, edge_ref, taps_ref, gain_ref,
    state_ref,
    conv_ref, t_ref, sc_ref, qh_ref, ah_ref, al_ref, gated_ref, mixed_ref, u_ref, s_ref, end_ref,
    w_scr, u0_scr, b_scr, o0_scr, ah_scr, al_scr, qh_scr,
):
    step = pl.program_id(0)
    base = offs_ref[0, doc_count]
    rate = rate_ref[0, 0]
    prior = jnp.where(step == 0, edge_ref[...].astype(WIDE), prior_ref[...].astype(WIDE))

    def local(u):
        c = step * group + u
        here = pre_ref[u * SPAN : (u + 1) * SPAN, :].astype(WIDE)
        if u:
            before = pre_ref[u * SPAN - 16 : u * SPAN, :].astype(WIDE)
        else:
            before = prior
        rows = stack(before, here)
        pos = span_tokens(offs_ref, doc_count, base + c * SPAN)
        conv = taps_ref[0:1, :] * here
        for lag in range(1, 4):
            shifted = rows[16 - lag : 16 - lag + SPAN]
            conv = conv + jnp.where(pos >= lag, taps_ref[lag : lag + 1, :] * shifted, 0.0)
        conv_ref[u * SPAN : (u + 1) * SPAN, :] = conv
        yield
        act = conv * jax.nn.sigmoid(conv)
        query, _ = unit(act[:, 0:128])
        key0, _ = unit(act[:, 128:256])
        key1, _ = unit(act[:, 256:384])
        keys = stack(key0, key1)
        values = stack(act[:, 384:512], act[:, 512:640])
        small = small_ref[u * SPAN : (u + 1) * SPAN, :]
        beta, decay, strict, carry, leave, carry_all, apart = span_factors(small, rate, pos)
        yield
        inner = mm(keys, keys, 1, 1)
        yield
        inverse = yield from unit_lower_inverse(
            jnp.where(strict, beta * decay * inner, 0.0), apart
        )
        t_ref[u] = inverse.astype(LOW)
        both = mm(inverse, jnp.concatenate([(beta * carry) * keys, beta * values], axis=1))
        yield
        weight, fresh = both[:, :HEAD], both[:, HEAD:]
        w_scr[c] = weight.astype(LOW)
        u0_scr[c] = fresh
        leaving = (keys * leave).astype(LOW)
        row = lax.broadcasted_iota(jnp.int32, (HEAD, HEAD), 0)
        col = lax.broadcasted_iota(jnp.int32, (HEAD, HEAD), 1)
        step_map = jnp.where(row == col, carry_all, 0.0) - mm(leaving, weight, 0, 0)
        map_high, map_rest = halves(step_map)
        ah_ref[u], al_ref[u] = map_high, map_rest
        ah_scr[c], al_scr[c] = map_high, map_rest
        yield
        b_scr[c] = mm(fresh, leaving, 0, 0)
        yield
        scores = mm(query, keys, 1, 1) * decay[SPAN:, :]
        yield
        sc_ref[u] = scores.astype(LOW)
        mixed_both = mm(scores, both)
        yield
        reach = (carry[SPAN:] * query - mixed_both[:, :HEAD]).astype(LOW)
        qh_ref[u] = reach
        qh_scr[c] = reach
        o0_scr[c] = mixed_both[:, HEAD:]

    in_turns(local(u) for u in range(group))

    def chain(i, state):
        for u in range(4):
            c = i * 4 + u
            s_ref[c] = state
            high, rest = halves(state)
            state = (
                contract(high, ah_scr[c], 1, 1)
                + contract(high, al_scr[c], 1, 1)
                + contract(rest, ah_scr[c], 1, 1)
                + b_scr[c]
            )
        return state

    def mixing(c):
        low = s_ref[c].astype(LOW)
        u_ref[c] = (u0_scr[c] - contract(w_scr[c], low, 1, 1)).astype(LOW)
        yield
        mixed = o0_scr[c] + contract(qh_scr[c], low, 1, 1)
        yield
        lo = pl.multiple_of(c * SPAN, SPAN)
        mixed_ref[pl.ds(lo, SPAN), :] = mixed
        scale = lax.rsqrt(jnp.mean(mixed * mixed, axis=1, keepdims=True) + EPSILON)
        yield
        gate = gate_ref[pl.ds(lo, SPAN), :]
        gated_ref[pl.ds(lo, SPAN), :] = (
            mixed * scale * gain_ref[...] * (gate * jax.nn.sigmoid(gate))
        ).astype(LOW)
        yield

    def mixing_step(i, none):
        in_turns(mixing(i * 8 + u) for u in range(8))
        return none

    @pl.when(step == pl.num_programs(0) - 1)
    def _():
        end_ref[...] = lax.fori_loop(0, span_count // 4, chain, state_ref[...])
        lax.fori_loop(0, span_count // 8, mixing_step, 0)


def gate_back_kernel(
    span_count,
    gate_ref, gain_ref, mixed_ref, qh_ref, ah_ref, al_ref, dgated_ref, dend_ref,
    do_ref, ds_ref, dgate_ref, dgain_ref, dbegin_ref,
    f_scr,
):
    dgain_ref[...] = jnp.zeros_like(dgain_ref)

    def gate_back(c):
        lo = pl.multiple_of(c * SPAN, SPAN)
        mixed = mixed_ref[pl.ds(lo, SPAN), :]
        gate = gate_ref[pl.ds(lo, SPAN), :]
        scale = lax.rsqrt(jnp.mean(mixed * mixed, axis=1, keepdims=True) + EPSILON)
        normed = mixed * scale
        yield
        sig = jax.nn.sigmoid(gate)
        grad = dgated_ref[pl.ds(lo, SPAN), :].astype(WIDE)
        by_gain = grad * normed
        dgate_ref[pl.ds(lo, SPAN), :] = (
            by_gain * gain_ref[...] * (sig * (1.0 + gate * (1.0 - sig)))
        ).astype(LOW)
        dgain_ref[...] += jnp.sum(by_gain * (gate * sig), axis=0, keepdims=True)
        yield
        dn = grad * (gate * sig) * gain_ref[...]
        dmixed = scale * (dn - normed * jnp.mean(dn * normed, axis=1, keepdims=True))
        do_low = dmixed.astype(LOW)
        do_ref[c] = do_low
        yield
        f_scr[c] = contract(do_low, qh_ref[c], 0, 0)

    def gate_step(i, none):
        in_turns(gate_back(i * 8 + u) for u in range(8))
        return none

    lax.fori_loop(0, span_count // 8, gate_step, 0)

    def chain_step(i, grad):
        for u in range(4):
            c = span_count - 1 - (i * 4 + u)
            ds_ref[c] = grad
            high, rest = halves(grad)
            grad = (
                contract(high, ah_ref[c], 1, 0)
                + contract(high, al_ref[c], 1, 0)
                + contract(rest, ah_ref[c], 1, 0)
                + f_scr[c]
            )
        return grad

    dbegin_ref[...] = lax.fori_loop(0, span_count // 4, chain_step, dend_ref[...])


def backward_kernel(
    at_block, doc_count,
    offs_ref, rate_ref, pre_ref, prior_ref, small_ref, edge_ref, taps_ref,
    conv_ref, t_ref, u_ref, sc_ref, s_ref, do_ref, ds_ref, dgate_ref,
    next_in, dtaps_in, drate_in, *refs,
):
    dy_ref, next_ref, dtaps_ref, drate_ref = refs[-4:]
    block = at_block(pl.program_id(0))
    base = offs_ref[0, doc_count]
    rate = rate_ref[0, 0]

    @pl.when(pl.program_id(0) == 0)
    def _():
        next_ref[...] = next_in[...]
        dtaps_ref[...] = dtaps_in[...]
        drate_ref[...] = drate_in[...]

    dy_ref[:, 640:768] = dgate_ref[...]

    def local(n):
        lo, hi = n * SPAN, (n + 1) * SPAN
        pos = span_tokens(offs_ref, doc_count, base + block * PER * SPAN + lo)
        conv = conv_ref[lo:hi, :]
        sig = jax.nn.sigmoid(conv)
        act = conv * sig
        query, scale_q = unit(act[:, 0:128])
        key0, scale_0 = unit(act[:, 128:256])
        key1, scale_1 = unit(act[:, 256:384])
        yield
        keys = stack(key0, key1)
        values = stack(act[:, 384:512], act[:, 512:640])
        small = small_ref[lo:hi, :]
        beta, decay, strict, carry, leave, carry_all, _ = span_factors(small, rate, pos)
        yield
        state, dstate = s_ref[n], ds_ref[n]
        state_l, dstate_l = state.astype(LOW), dstate.astype(LOW)
        upd, out_grad, keys_l = u_ref[n], do_ref[n], keys.astype(LOW)
        dupd = contract(sc_ref[n], out_grad, 0, 0) + mm(keys * leave, dstate_l, 1, 1)
        yield
        dtarget = mm(t_ref[n], dupd, 0, 0)
        yield
        pair = stack(dtarget.astype(LOW), out_grad)
        by_upd = contract(pair, upd, 1, 1)
        by_state = contract(pair, state_l, 1, 0)
        yield
        dinner = jnp.where(strict, -by_upd[:ROWS] * decay, 0.0)
        dscore = by_upd[ROWS:] * decay[SPAN:, :]
        both = stack(dinner, dscore).astype(LOW)
        reading = contract(both, keys_l, 1, 0)
        yield
        read_key = reading[:ROWS] - carry * by_state[:ROWS]
        dquery = reading[ROWS:] + carry[SPAN:] * by_state[ROWS:]
        dleave = leave * contract(upd, dstate_l, 1, 0)
        write_key = contract(both, stack(beta * keys, query).astype(LOW), 0, 0) + dleave
        yield
        key_read = jnp.sum(keys * read_key, axis=1, keepdims=True)
        dbeta = jnp.sum(dtarget * values, axis=1, keepdims=True) + key_read
        dcum = beta * key_read - jnp.sum(keys * write_key, axis=1, keepdims=True)
        dcum = dcum[:SPAN] + dcum[SPAN:] + jnp.sum(query * dquery, axis=1, keepdims=True)
        through = jnp.sum(keys * dleave, axis=0, keepdims=True) + carry_all * jnp.sum(
            dstate * state, axis=0, keepdims=True
        )
        through = jnp.sum(through, axis=1, keepdims=True)
        tok1 = lax.broadcasted_iota(jnp.int32, (SPAN, 1), 0)
        dcum = dcum + jnp.where(tok1 == SPAN - 1, through, 0.0)
        tok = lax.broadcasted_iota(jnp.int32, (SPAN, SPAN), 0)
        tok_c = lax.broadcasted_iota(jnp.int32, (SPAN, SPAN), 1)
        upper = jnp.where(tok <= tok_c, 1.0, 0.0).astype(LOW)
        high, rest = halves(jnp.broadcast_to(dcum, (SPAN, 128)))
        dlog = contract(upper, high, 1, 0) + contract(upper, rest, 1, 0)
        yield
        soft = softplus(small)
        sig_small = jax.nn.sigmoid(small)
        lane = lax.broadcasted_iota(jnp.int32, (SPAN, 128), 1)
        drate_ref[...] += jnp.sum(jnp.where(lane == 2, -dlog * soft, 0.0), axis=0, keepdims=True)
        dsig = jnp.where(lane == 0, dbeta[:SPAN], dbeta[SPAN:]) * sig_small * (1.0 - sig_small)
        dsmall = jnp.where(lane < 2, dsig, jnp.where(lane == 2, -rate * dlog * sig_small, 0.0))
        dy_ref[lo:hi, 768:896] = dsmall.astype(LOW)
        yield
        dkey = beta * read_key + write_key
        dvalue = beta * dtarget

        def unit_back(grad, normed, scale):
            return scale * (grad - normed * jnp.sum(grad * normed, axis=1, keepdims=True))

        dact = jnp.concatenate(
            [
                unit_back(dquery, query, scale_q),
                unit_back(dkey[:SPAN], key0, scale_0),
                unit_back(dkey[SPAN:], key1, scale_1),
                dvalue[:SPAN],
                dvalue[SPAN:],
            ],
            axis=1,
        )
        dconv = dact * (sig * (1.0 + conv * (1.0 - sig)))
        yield
        here = pre_ref[lo:hi, :].astype(WIDE)
        if n:
            prior = pre_ref[lo - 16 : lo, :].astype(WIDE)
        else:
            prior = jnp.where(
                block == 0, edge_ref[...].astype(WIDE), prior_ref[...].astype(WIDE)
            )
        rows = stack(prior, here)
        dpre = taps_ref[0:1, :] * dconv
        dtaps_ref[0:1, :] += jnp.sum(dconv * here, axis=0, keepdims=True)
        for lag in range(1, 4):
            kept = jnp.where(pos >= lag, dconv, 0.0)
            shifted = rows[16 - lag : 16 - lag + SPAN]
            dtaps_ref[lag : lag + 1, :] += jnp.sum(kept * shifted, axis=0, keepdims=True)
            kept = kept * taps_ref[lag : lag + 1, :]
            dpre = dpre + stack(kept, next_ref[lag])[lag : lag + SPAN]
            next_ref[lag] = kept[0:8]
        dy_ref[lo:hi, 0:640] = dpre.astype(LOW)

    in_turns(local(n) for n in reversed(range(PER)))


def vmem_spec():
    return pl.BlockSpec(memory_space=pltpu.VMEM)


def smem_spec():
    return pl.BlockSpec(memory_space=pltpu.SMEM)


def fixed(shape):
    return pl.BlockSpec(shape, lambda *_: (0,) * len(shape))


def estimate(flops, mib):
    return pl.CostEstimate(flops=int(flops), bytes_accessed=int(mib * 2**20), transcendentals=0)


def run_forward(offs, rate, pre, gs, edge, taps, gain, state):
    tokens = pre.shape[0]
    spans = tokens // SPAN
    group = 8
    shape = jax.ShapeDtypeStruct
    outs = (
        (shape((tokens, 640), WIDE), pl.BlockSpec((group * SPAN, 640), lambda i: (i, 0))),
        (shape((spans, ROWS, ROWS), LOW), pl.BlockSpec((group, ROWS, ROWS), lambda i: (i, 0, 0))),
        (shape((spans, SPAN, ROWS), LOW), pl.BlockSpec((group, SPAN, ROWS), lambda i: (i, 0, 0))),
        (shape((spans, SPAN, HEAD), LOW), pl.BlockSpec((group, SPAN, HEAD), lambda i: (i, 0, 0))),
        (shape((spans, HEAD, HEAD), LOW), pl.BlockSpec((group, HEAD, HEAD), lambda i: (i, 0, 0))),
        (shape((spans, HEAD, HEAD), LOW), pl.BlockSpec((group, HEAD, HEAD), lambda i: (i, 0, 0))),
        (shape((tokens, HEAD), LOW), fixed((tokens, HEAD))),
        (shape((tokens, HEAD), WIDE), fixed((tokens, HEAD))),
        (shape((spans, ROWS, HEAD), LOW), fixed((spans, ROWS, HEAD))),
        (shape((spans, HEAD, HEAD), WIDE), fixed((spans, HEAD, HEAD))),
        (shape((HEAD, HEAD), WIDE), fixed((HEAD, HEAD))),
    )
    return pl.pallas_call(
        functools.partial(forward_kernel, spans, offs.shape[1] - 1, group),
        out_shape=[o for o, _ in outs],
        grid=(spans // group,),
        in_specs=[
            smem_spec(),
            smem_spec(),
            pl.BlockSpec((group * SPAN, 640), lambda i: (i, 0)),
            pl.BlockSpec((16, 640), lambda i: (jnp.maximum(i * (group * SPAN // 16) - 1, 0), 0)),
            pl.BlockSpec((group * SPAN, HEAD), lambda i: (i, 1)),
            fixed((tokens, HEAD)),
            fixed((16, 640)),
            fixed((8, 640)),
            fixed((1, HEAD)),
            fixed((HEAD, HEAD)),
        ],
        out_specs=[b for _, b in outs],
        scratch_shapes=[
            pltpu.VMEM((spans, ROWS, HEAD), LOW),
            pltpu.VMEM((spans, ROWS, HEAD), WIDE),
            pltpu.VMEM((spans, HEAD, HEAD), WIDE),
            pltpu.VMEM((spans, SPAN, HEAD), WIDE),
            pltpu.VMEM((spans, HEAD, HEAD), LOW),
            pltpu.VMEM((spans, HEAD, HEAD), LOW),
            pltpu.VMEM((spans, SPAN, HEAD), LOW),
        ],
        compiler_params=pltpu.CompilerParams(vmem_limit_bytes=VMEM_LIMIT),
        cost_estimate=estimate(70e9, 24),
        name="delta_forward",
    )(offs, rate, pre, pre, gs, gs, edge, taps, gain, state)


def run_gate_back(gs, gain, mixed, qh, high, rest, dgated, dend):
    tokens = mixed.shape[0]
    spans = tokens // SPAN
    shape = jax.ShapeDtypeStruct
    return pl.pallas_call(
        functools.partial(gate_back_kernel, spans),
        out_shape=(
            shape((spans, SPAN, HEAD), LOW),
            shape((spans, HEAD, HEAD), WIDE),
            shape((tokens, HEAD), LOW),
            shape((1, HEAD), WIDE),
            shape((HEAD, HEAD), WIDE),
        ),
        grid=(1,),
        in_specs=[
            fixed((tokens, HEAD)),
            fixed((1, HEAD)),
            fixed((tokens, HEAD)),
            fixed((spans, SPAN, HEAD)),
            fixed((spans, HEAD, HEAD)),
            fixed((spans, HEAD, HEAD)),
            fixed((tokens, HEAD)),
            fixed((HEAD, HEAD)),
        ],
        out_specs=(
            fixed((spans, SPAN, HEAD)),
            fixed((spans, HEAD, HEAD)),
            fixed((tokens, HEAD)),
            fixed((1, HEAD)),
            fixed((HEAD, HEAD)),
        ),
        scratch_shapes=[pltpu.VMEM((spans, HEAD, HEAD), WIDE)],
        compiler_params=pltpu.CompilerParams(vmem_limit_bytes=VMEM_LIMIT),
        cost_estimate=estimate(15e9, 8),
        name="delta_gate_back",
    )(gs, gain, mixed, qh, high, rest, dgated, dend)


def run_backward(last, steps, offs, rate, pre, gs, edge, taps, saved, carried, dy):
    conv, inverse, upd, scores, states, do, ds, dgate = saved
    tokens = pre.shape[0]

    def at(i):
        return last - i

    def rows(columns, lane=0):
        return pl.BlockSpec((PER * SPAN, columns), lambda i: (at(i), lane))

    def spans(a, b):
        return pl.BlockSpec((PER, a, b), lambda i: (at(i), 0, 0))

    shape = jax.ShapeDtypeStruct
    carried_specs = [fixed((4, 8, 640)), fixed((8, 640)), fixed((1, HEAD))]
    operands = [offs, rate, pre, pre, gs, edge, taps, conv, inverse, upd, scores, states, do, ds]
    operands += [dgate, *carried]
    in_specs = [
        smem_spec(),
        smem_spec(),
        rows(640),
        pl.BlockSpec((16, 640), lambda i: (jnp.maximum(at(i) * (PER * SPAN // 16) - 1, 0), 0)),
        rows(HEAD, 1),
        fixed((16, 640)),
        fixed((8, 640)),
        rows(640),
        spans(ROWS, ROWS),
        spans(ROWS, HEAD),
        spans(SPAN, ROWS),
        spans(HEAD, HEAD),
        spans(SPAN, HEAD),
        spans(HEAD, HEAD),
        rows(HEAD),
        *carried_specs,
    ]
    aliases = {}
    if dy is not None:
        aliases = {len(operands): 0}
        operands.append(dy)
        in_specs.append(pl.BlockSpec(memory_space=pl.ANY))
    dy, *carried = pl.pallas_call(
        functools.partial(backward_kernel, at, offs.shape[1] - 1),
        out_shape=(
            shape((tokens, 896), LOW),
            shape((4, 8, 640), WIDE),
            shape((8, 640), WIDE),
            shape((1, HEAD), WIDE),
        ),
        grid=(steps,),
        in_specs=in_specs,
        out_specs=(rows(896), *carried_specs),
        input_output_aliases=aliases,
        compiler_params=pltpu.CompilerParams(vmem_limit_bytes=VMEM_LIMIT),
        cost_estimate=estimate(4e9 * steps, 2.6 * steps),
        name="delta_backward",
    )(*operands)
    return dy, carried


def input_blocks_kernel(at_ref, dy_ref, out_ref, w_ref, send_ref, keep_ref):
    count = dy_ref.shape[0]
    block = contract(dy_ref[...], w_ref[...], 1, 1).astype(LOW)
    for n, to_ref in enumerate((send_ref, keep_ref)):

        @pl.when(pl.program_id(0) == n)
        def _():
            to_ref[:count, :] = block
            to_ref[count:, :] = out_ref[...]


def input_blocks(places, dy, grad_out, weights, count, out_rows):
    width = weights.shape[0]
    return pl.pallas_call(
        input_blocks_kernel,
        out_shape=[jax.ShapeDtypeStruct((count + out_rows, width), LOW)] * 2,
        grid_spec=pltpu.PrefetchScalarGridSpec(
            num_scalar_prefetch=1,
            grid=(2,),
            in_specs=[
                pl.BlockSpec((count, 896), lambda i, p: (p[i], 0)),
                pl.BlockSpec((out_rows, width), lambda i, p: (p[i], 0)),
                fixed(weights.shape),
            ],
            out_specs=[fixed((count + out_rows, width))] * 2,
        ),
        compiler_params=pltpu.CompilerParams(vmem_limit_bytes=VMEM_LIMIT),
        cost_estimate=estimate(4 * count * width * 896, 4),
        name="input_blocks",
    )(jnp.stack(places).astype(jnp.int32), dy, grad_out, weights)


def weight_grads_kernel(
    taps, at_ref, low_ref, dy_ref, w_ref, gain_ref, gff_ref, gh_ref, rate_ref, taps_ref, to_ref
):
    shard = w_ref.shape[0]
    grads = contract(low_ref[...], dy_ref[...], 0, 0)
    to_ref[:shard, :] = grads.astype(LOW)
    sums = jnp.sum(grads * w_ref[...].astype(WIDE), axis=1, keepdims=True)
    row = jnp.broadcast_to(sums, (shard, HEAD)).T[0:1] / gain_ref[...]

    def wide(value):
        return jnp.concatenate(
            [value, jnp.zeros((value.shape[0], 896 - value.shape[1]), WIDE)], axis=1
        )

    to_ref[shard:, :] = stack(
        wide(row),
        wide(gff_ref[...]),
        wide(gh_ref[0]),
        wide(rate_ref[...]),
        wide(taps_ref[:taps, :]),
        jnp.zeros((12 - taps, 896), WIDE),
    ).astype(LOW)


def weight_grads(order, low, dy, weights, gain, gain_ffn, gain_head, rate, taps_grad, taps):
    length, width = low.shape
    members = order.shape[0]
    shard = width // members
    gh = jnp.pad(gain_head.reshape(members, 1, -1), ((0, 0), (0, 0), (0, HEAD)))[:, :, :HEAD]
    return pl.pallas_call(
        functools.partial(weight_grads_kernel, taps),
        out_shape=jax.ShapeDtypeStruct((members * (shard + 16), 896), LOW),
        grid_spec=pltpu.PrefetchScalarGridSpec(
            num_scalar_prefetch=1,
            grid=(members,),
            in_specs=[
                pl.BlockSpec((length, shard), lambda i, p: (0, p[i])),
                fixed((length, 896)),
                pl.BlockSpec((shard, 896), lambda i, p: (p[i], 0)),
                pl.BlockSpec((1, shard), lambda i, p: (0, p[i])),
                pl.BlockSpec((1, shard), lambda i, p: (0, p[i])),
                pl.BlockSpec((1, 1, HEAD), lambda i, p: (p[i], 0, 0)),
                fixed((1, HEAD)),
                fixed((8, 640)),
            ],
            out_specs=pl.BlockSpec((shard + 16, 896), lambda i, p: (i, 0)),
        ),
        compiler_params=pltpu.CompilerParams(vmem_limit_bytes=VMEM_LIMIT),
        cost_estimate=estimate(2 * length * width * 896, 12),
        name="weight_grads",
    )(order, low, dy, weights, gain, gain_ffn, gh, rate, taps_grad)


def pack_kernel(
    heads, taps,
    place_ref, q_ref, k0_ref, k1_ref, v0_ref, v1_ref, g_ref, beta_ref, decay_ref, gin_ref,
    gff_ref, gh_ref, cq_ref, ck_ref, cv_ref, out_ref,
):
    h = place_ref[0]
    shard = q_ref.shape[0]
    for i, ref in enumerate((q_ref, k0_ref, k1_ref, v0_ref, v1_ref, g_ref)):
        out_ref[:shard, i * HEAD : (i + 1) * HEAD] = ref[...]
    beta, decay = beta_ref[...].astype(WIDE), decay_ref[...].astype(WIDE)

    def row_of(values, at):
        row = lax.broadcasted_iota(jnp.int32, values.shape, 0)
        return jnp.sum(jnp.where(row == at, values, 0.0), axis=0, keepdims=True)

    row = lax.broadcasted_iota(jnp.int32, (HEAD, shard), 0)
    small = jnp.where(row == 0, row_of(beta, h), 0.0)
    small = jnp.where(row == 1, row_of(beta, heads + h), small)
    small = jnp.where(row == 2, row_of(decay, h), small)
    out_ref[:shard, 6 * HEAD :] = small.T.astype(LOW)
    out_ref[shard:, :] = jnp.zeros((out_ref.shape[0] - shard, out_ref.shape[1]), LOW)
    vectors = stack(
        *[ref[...].astype(WIDE) for ref in (gin_ref, gff_ref, gh_ref, cq_ref)],
        *[
            ref[:, i * shard : (i + 1) * shard].astype(WIDE)
            for ref in (ck_ref, cv_ref)
            for i in range(2)
        ],
        jnp.zeros((32 - 3 - 5 * taps, shard), WIDE),
    )
    out_ref[shard:, :shard] = vectors.astype(LOW)


def pack_weights(
    head, w_query, w_key, w_value, w_outgate, w_beta, w_decay, gain_in, gain_ffn, gain_head,
    conv_query, conv_key, conv_value,
):
    shard, heads = w_decay.shape
    taps = conv_query.shape[0]

    def part(step):
        return pl.BlockSpec((shard, HEAD), lambda i, h: (0, step * heads + h[0]))

    small = (
        w_beta.T, w_decay.T, gain_in[None], gain_ffn[None],
        jnp.pad(gain_head, (0, shard - gain_head.shape[0]))[None],
        conv_query, conv_key, conv_value,
    )
    return pl.pallas_call(
        functools.partial(pack_kernel, heads, taps),
        out_shape=jax.ShapeDtypeStruct((shard + 32, 896), LOW),
        grid_spec=pltpu.PrefetchScalarGridSpec(
            num_scalar_prefetch=1,
            grid=(1,),
            in_specs=[part(0), part(0), part(1), part(0), part(1), part(0)]
            + [fixed(a.shape) for a in small],
            out_specs=fixed((shard + 32, 896)),
        ),
        compiler_params=pltpu.CompilerParams(vmem_limit_bytes=VMEM_LIMIT),
        cost_estimate=estimate(0, 2),
        name="pack_weights",
    )(head.reshape(1), w_query, w_key, w_key, w_value, w_value, w_outgate, *small)


def project_kernel(count, place_ref, gain_ref, w_ref, *refs):
    tok_refs, (low_ref, pre_ref, gs_ref) = refs[:count], refs[-3:]
    for n in range(count):

        @pl.when(pl.program_id(0) == n)
        def _():
            values = tok_refs[n][...].astype(WIDE)
            scale = lax.rsqrt(jnp.mean(values * values, axis=1, keepdims=True) + EPSILON)
            low_ref[...] = (values * scale * gain_ref[...]).astype(LOW)

    normed = low_ref[...]
    pre_ref[...] = contract(normed, w_ref[:, :640], 1, 0).astype(LOW)
    gs_ref[...] = contract(normed, w_ref[:, 640:], 1, 0)


def project(found, gain, weights, length, filled):
    blocks = [one for a, x, b, y in found for one in ((a, x), (b, y))]
    places = jnp.stack([place for place, _ in blocks]).astype(jnp.int32)
    count, (rows, width) = len(blocks), blocks[0][1].shape
    shape = jax.ShapeDtypeStruct
    aliases = {3 + count + i: i for i in range(len(filled))}
    return pl.pallas_call(
        functools.partial(project_kernel, count),
        out_shape=[
            shape((length, n), t) for n, t in ((width, LOW), (640, LOW), (256, WIDE))
        ],
        input_output_aliases=aliases,
        grid_spec=pltpu.PrefetchScalarGridSpec(
            num_scalar_prefetch=1,
            grid=(count,),
            in_specs=[fixed(gain.shape), fixed(weights.shape)]
            + [fixed((rows, width))] * count
            + [pl.BlockSpec(memory_space=pl.ANY)] * len(filled),
            out_specs=[
                pl.BlockSpec((rows, n), lambda i, p: (p[i], 0)) for n in (width, 640, 256)
            ],
        ),
        compiler_params=pltpu.CompilerParams(vmem_limit_bytes=VMEM_LIMIT),
        cost_estimate=estimate(2 * count * rows * width * 896, 13),
        name="project",
    )(places, gain, weights, *(value for _, value in blocks), *filled)


def rms_parts(values):
    return values * lax.rsqrt(jnp.mean(values * values, axis=-1, keepdims=True) + EPSILON)


def rms_back(grad_scaled, values):
    scale = lax.rsqrt(jnp.mean(values * values, axis=-1, keepdims=True) + EPSILON)
    normed = values * scale
    return scale * (
        grad_scaled - normed * jnp.mean(grad_scaled * normed, axis=-1, keepdims=True)
    )


def dot_plain(left, right, kind=WIDE):
    return jnp.dot(left, right, preferred_element_type=kind)


def dot_left(left, right, kind=WIDE):
    return contract(left, right, 0, 0).astype(kind)


def dot_right(left, right):
    return contract(left, right, 1, 1)


def exchanged(value, axis, bit):
    size = lax.axis_size(axis)
    return lax.ppermute(value, axis, [(i, i ^ bit) for i in range(size)])


def near_order(size):
    order, bit = [0], size // 2
    while bit:
        order = order + [o ^ bit for o in order]
        bit //= 2
    return order


def near_gather(value, axis, first=None):
    bit = lax.axis_size(axis) // 2
    while bit:
        value = stack(value, exchanged(value, axis, bit) if first is None else first)
        first = None
        bit //= 2
    return value


def near_scatter(value, axis):
    size, bit = lax.axis_size(axis), 1
    while bit < size:
        half = value.shape[0] // 2
        came = exchanged(value[half:].astype(LOW), axis, bit).astype(WIDE)
        value = value[:half].astype(WIDE) + came
        bit *= 2
    return value


def near_scatter_stages(value, axis, ties):
    size, bit = lax.axis_size(axis), 1
    while bit < size:
        half = value.shape[0] // 2
        value = after(value, *ties)
        came = exchanged(value[half:].astype(LOW), axis, bit)
        yield [came]
        value = value[:half].astype(WIDE) + came.astype(WIDE)
        bit *= 2
    yield value


def near_blocks(value, axis):
    size, me = lax.axis_size(axis), lax.axis_index(axis)
    return stack(
        *[lax.dynamic_index_in_dim(value, me ^ o, 0, False) for o in near_order(size)]
    )


def ordered_step(value, other, axis, bit):
    mine_first = (lax.axis_index(axis) & bit) == 0
    pair = jnp.where(mine_first, jnp.stack([value, other], 1), jnp.stack([other, value], 1))
    return pair.reshape((pair.shape[0] * 2,) + value.shape[1:])


def ordered_gather(value, axis, first=None):
    bit = lax.axis_size(axis) // 2
    value = value[None]
    while bit:
        other = exchanged(value, axis, bit) if first is None else first[None]
        value = ordered_step(value, other, axis, bit)
        first = None
        bit //= 2
    return value


def far_exchange(value, axis):
    return exchanged(value, axis, lax.axis_size(axis) // 2)


def after(value, *done):
    return lax.optimization_barrier((value, *done))[0]


def team_step(value, team, move):
    size = lax.axis_size("seq")
    pairs = [(t + i, t + move(i)) for t in range(0, size, team) for i in range(team)]
    return lax.ppermute(value, "seq", pairs)


def turn(value, team, by):
    return team_step(value, team, lambda i: (i + 2 * by) % team)


def cross(value, team):
    return team_step(value, team, lambda i: i ^ 1)


def rolled(value, by, axis):
    twice = jnp.concatenate([value, value], axis=axis)
    return lax.dynamic_slice_in_dim(twice, by, value.shape[axis], axis)


def swapped(blocks, team):
    return [blocks[0]] + [
        team_step(blocks[k], team, lambda i: (i - k) % team) for k in range(1, team)
    ]


def turns(team):
    half = team // 2
    return [0] + [k for n in range(1, half // 2 + 1) for k in dict.fromkeys((n, half - n))]


def gather_stages(value, team, ties=(), lag=1):
    me = lax.axis_index("seq") % team
    half = team // 2
    turned, found, brought = {0: value}, [], []
    if half > 1:
        turned[1] = turn(value, team, 1)
    if half > 2:
        turned[half - 1] = turn(after(value, turned[1]), team, -1)
    for k in turns(team):
        across = cross(after(turned[k], *brought[-lag:][: len(brought) - lag + 1], *ties), team)
        stage = [across]
        for n in (k + 1, k - 1):
            if 0 < n < half and n not in turned and k:
                turned[n] = turn(turned[k], team, 1 if n > k else -1)
                stage.append(turned[n])
        brought.append(across)
        found.append(((me - 2 * k) % team, turned[k], ((me ^ 1) - 2 * k) % team, across))
        yield stage
    yield found


def last_of(stages):
    for stage in stages:
        pass
    return stage


def team_places(team):
    me = lax.axis_index("seq") % team
    return [
        (((me ^ 1) + 2 * k) % team, (me + 2 * k) % team) for k in reversed(turns(team))
    ]


def scatter_stages(blocks, team, ties=()):
    half = team // 2
    passing, leaving, before = {}, None, ()
    for (send, keep), k in zip(blocks, reversed(turns(team))):
        came = cross(after(send, *before, *ties), team)
        stage = [came]
        if leaving is not None:
            pair, n = leaving
            forward = 2 * n <= half
            to = n - 1 if forward else (n + 1) % half
            moved = turn(pair.astype(LOW), team, 1 if forward else -1)
            stage.append(moved)
            passing[to] = passing.get(to, []) + [moved]
        yield stage
        before = (came,)
        keep = keep(came) if callable(keep) else keep
        pair = keep.astype(WIDE) + came.astype(WIDE)
        for moved in passing.pop(k, []):
            pair = pair + moved.astype(WIDE)
        leaving = (pair, k)
    yield pair


def mixer_outputs_kernel(heads, taps, fsdp, place_ref, *refs):
    got_refs, out_refs, refs = refs[:heads], refs[heads : 2 * heads], refs[2 * heads :]
    (q_ref, k_ref, v_ref, g_ref, b_ref, d_ref, gin_ref, gff_ref, gh_ref, rate_ref, cq_ref,
     ck_ref, cv_ref, out_ref) = refs
    member = place_ref[0, heads]
    shard = q_ref.shape[0]
    gains = gh_ref.shape[1]
    width = heads * HEAD
    lane_r = lax.broadcasted_iota(jnp.int32, (1, heads), 1)
    rates = jnp.zeros((1, heads), WIDE)
    vectors = jnp.zeros((8, shard), WIDE)
    for n in range(heads):
        got_ref = got_refs[n]
        h = place_ref[0, n]

        def columns(step):
            return pl.ds(pl.multiple_of(step * width + h * HEAD, HEAD), HEAD)

        q_ref[:, columns(0)] = got_ref[:shard, 0:128].astype(WIDE)
        for i in range(2):
            k_ref[:, columns(i)] = got_ref[:shard, 128 + i * 128 : 256 + i * 128].astype(WIDE)
            v_ref[:, columns(i)] = got_ref[:shard, 384 + i * 128 : 512 + i * 128].astype(WIDE)
        g_ref[:, columns(0)] = got_ref[:shard, 640:768].astype(WIDE)
        last = got_ref[:shard, 768:896].astype(WIDE).T
        b_ref[pl.ds(h, 1), :] = last[0:1]
        b_ref[pl.ds(heads + h, 1), :] = last[1:2]
        d_ref[pl.ds(h, 1), :] = last[2:3]
        extra = got_ref[shard:, :].astype(WIDE)
        vectors = vectors + extra[0:8, :shard]
        rates = jnp.where(lane_r == h, extra[3:4, 2:3], rates)
        rows = out_refs[n].shape[0]
        out_ref[pl.ds(pl.multiple_of(h * rows, rows), rows), :] = out_refs[n][...].astype(WIDE)
        for ref, at, steps in ((cq_ref, 0, 1), (ck_ref, 128, 2), (cv_ref, 384, 2)):
            per = ref.shape[1] // HEAD
            for i in range(steps):
                slot = i * heads + h - member * per

                @pl.when((slot >= 0) & (slot < per))
                def _():
                    to = pl.ds(pl.multiple_of(slot * HEAD, HEAD), HEAD)
                    ref[:, to] = extra[4 : 4 + taps, at + i * HEAD : at + (i + 1) * HEAD]

    rate_ref[...] = rates
    gin_ref[...] = vectors[0:1]
    gff_ref[...] = vectors[1:2]
    gh_ref[...] = vectors[2:3, :gains]


def mixer_outputs(found, found_out, shard, gains, taps, fsdp, member):
    found, found_out = (
        [one for a, x, b, y in pairs for one in ((a, x), (b, y))] for pairs in (found, found_out)
    )
    heads = len(found)
    places = jnp.stack([place for place, _ in found] + [member])[None].astype(jnp.int32)
    width = heads * HEAD
    shape = jax.ShapeDtypeStruct
    outs = (
        shape((shard, width), WIDE),
        shape((shard, 2 * width), WIDE),
        shape((shard, 2 * width), WIDE),
        shape((shard, width), WIDE),
        shape((2 * heads, shard), WIDE),
        shape((heads, shard), WIDE),
        shape((1, shard), WIDE),
        shape((1, shard), WIDE),
        shape((1, gains), WIDE),
        shape((1, heads), WIDE),
        shape((taps, shard), WIDE),
        shape((taps, 2 * shard), WIDE),
        shape((taps, 2 * shard), WIDE),
        shape((shard, width), WIDE),
    )
    return pl.pallas_call(
        functools.partial(mixer_outputs_kernel, heads, taps, fsdp),
        out_shape=outs,
        in_specs=[smem_spec()] + [vmem_spec()] * (2 * heads),
        out_specs=[vmem_spec()] * len(outs),
        compiler_params=pltpu.CompilerParams(vmem_limit_bytes=VMEM_LIMIT),
        cost_estimate=estimate(0, 12),
        name="mixer_outputs",
    )(places, *(value for _, value in found), *(value for _, value in found_out))


def ff_outputs_kernel(count, slab, shard, place_ref, *refs):
    got_refs, (gate_ref, up_ref, down_ref), held = refs[:count], refs[count : count + 3], refs[-1]
    own = count * slab
    for n, got_ref in enumerate(got_refs):
        at = place_ref[n] * slab
        piece = got_ref[...].astype(WIDE)
        for m in range(2):
            for k in range(2):
                to = pl.multiple_of(k * own + at, 8)
                held[m, pl.ds(to, slab), :] = piece[
                    m * slab : (m + 1) * slab, k * shard : (k + 1) * shard
                ]
        down_ref[pl.ds(pl.multiple_of(at, 8), slab), :] = piece[2 * slab :]
    gate_ref[...] = held[0].T
    up_ref[...] = held[1].T


def ff_outputs(found, slab, shard, fsdp):
    found = [one for a, x, b, y in found for one in ((a, x), (b, y))]
    count, (rows, width) = len(found), found[0][1].shape
    own = count * slab
    shape = jax.ShapeDtypeStruct
    return pl.pallas_call(
        functools.partial(ff_outputs_kernel, count, slab, shard),
        out_shape=(
            shape((shard, fsdp * own), WIDE),
            shape((shard, fsdp * own), WIDE),
            shape((own, width), WIDE),
        ),
        grid_spec=pltpu.PrefetchScalarGridSpec(
            num_scalar_prefetch=1,
            grid=(fsdp // 2,),
            in_specs=[pl.BlockSpec((rows, 2 * shard), lambda i, p: (0, i))] * count,
            out_specs=(
                pl.BlockSpec((shard, 2 * own), lambda i, p: (0, i)),
                pl.BlockSpec((shard, 2 * own), lambda i, p: (0, i)),
                pl.BlockSpec((own, 2 * shard), lambda i, p: (0, i)),
            ),
            scratch_shapes=[pltpu.VMEM((2, 2 * own, shard), WIDE)],
        ),
        compiler_params=pltpu.CompilerParams(vmem_limit_bytes=VMEM_LIMIT),
        cost_estimate=estimate(0, 15),
        name="ff_outputs",
    )(jnp.stack([p for p, _ in found]).astype(jnp.int32), *(x for _, x in found))


def ff_outputs_plain(got, slab, shard, fsdp):
    seq, rows, width = got.shape
    own = seq * slab
    wide = got.astype(WIDE)

    def turned(at):
        part = wide[:, at : at + slab].reshape(seq, slab, fsdp, shard)
        return jnp.transpose(part, (3, 2, 0, 1)).reshape(shard, fsdp * own)

    return turned(0), turned(slab), wide[:, 2 * slab :].reshape(own, width)


def per_device(
    tokens, cotangent, offsets, gain_in, w_query, w_key, w_value, w_beta, w_decay, w_outgate,
    conv_query, conv_key, conv_value, decay_scale, gain_head, w_out, gain_ffn, w_gate, w_up,
    w_down,
):
    seq, fsdp = lax.axis_size("seq"), lax.axis_size("fsdp")
    heads = decay_scale.shape[0]
    taps = conv_query.shape[0]
    own_rows = tokens.shape[1]
    shard = w_query.shape[0]
    width = shard * fsdp
    teams = seq // heads
    assert teams * heads == seq and width == heads * HEAD
    place = lax.axis_index("seq")
    head, team = place % heads, place // heads
    member = lax.axis_index("fsdp")
    if teams == 1:
        team_groups, head_groups = None, None
    else:
        team_groups = [[t * heads + h for h in range(heads)] for t in range(teams)]
        head_groups = [[t * heads + h for t in range(teams)] for h in range(heads)]

    def gather_rows(value):
        return lax.all_gather(value, "fsdp", axis=0, tiled=True)

    start_ties = []
    spread = gather_stages(tokens[0], heads, start_ties)
    came = next(spread)[:1]
    length = heads * own_rows

    def column_blocks(value):
        return jnp.transpose(value.reshape(shard, fsdp, value.shape[1] // fsdp), (1, 0, 2))

    packed = pack_weights(
        head, after(w_query, came[0]), w_key, w_value, w_outgate, w_beta, w_decay, gain_in,
        gain_ffn, gain_head, conv_query, conv_key, conv_value,
    )
    far_packed = far_exchange(packed, "fsdp")
    start_ties[:] = [packed]
    came += next(spread)[:1]
    columns = jnp.stack(
        [column_blocks(after(w_gate, came[1])), column_blocks(after(w_up, came[1]))], axis=1
    )
    others = near_order(fsdp)[1:]
    column_sends = [lax.dynamic_index_in_dim(columns, member ^ o, 0, False) for o in others]
    start_ties[:] = [far_packed]
    came += next(spread)[:1]
    far_out = far_exchange(after(w_out, far_packed), "fsdp")
    got = ordered_gather(packed, "fsdp", far_packed)
    start_ties[:] = [got, far_out, *column_sends]
    for stage in spread:
        found = stage
        came += stage[:1]
    came = [one for one in came if not isinstance(one, tuple)]
    came += [came[-1]] * 3
    full_packed = got[:, :shard].reshape(width, 896)
    vectors = got[:, shard:, :shard]
    full_gain_in = vectors[:, 0].reshape(width).astype(WIDE)
    full_gain_ffn = vectors[:, 1].reshape(width).astype(WIDE)
    full_gain_head = vectors[:, 2, : gain_head.shape[0]].reshape(1, HEAD).astype(WIDE)

    def head_taps_of(row, pieces, step):
        column = step * width + head * HEAD
        inside = column % (pieces * shard)
        at = (column // (pieces * shard), row + inside // shard * taps, inside % shard)
        return lax.dynamic_slice(vectors, at, (1, taps, HEAD))[0]

    head_taps = jnp.concatenate(
        [head_taps_of(3, 1, 0)]
        + [head_taps_of(3 + taps, 2, i) for i in range(2)]
        + [head_taps_of(3 + 3 * taps, 2, i) for i in range(2)],
        axis=1,
    ).astype(WIDE)
    head_taps = jnp.pad(head_taps, ((0, 8 - taps), (0, 0)))
    def column_blocks(value):
        return jnp.transpose(value.reshape(shard, fsdp, value.shape[1] // fsdp), (1, 0, 2))

    cot = after(cotangent[0], came[2])
    far_cot = far_exchange(cot, "fsdp")
    column_got = [
        exchanged(after(send, came[2]), "fsdp", o) for o, send in zip(others, column_sends)
    ]
    filled = project(found[:-1], full_gain_in[None], full_packed, length, []) if found[1:] else []
    normed_low, pre, gate_small = project(
        found[-1:], full_gain_in[None], full_packed, length, filled
    )
    offs = jnp.concatenate(
        [offsets, jnp.broadcast_to(team * length, (1, 1)).astype(jnp.int32)], axis=1
    )
    rate = lax.dynamic_slice_in_dim(decay_scale, head, 1).reshape(1, 1)
    zero_state = jnp.zeros((HEAD, HEAD), WIDE)
    if teams == 1:
        edge = jnp.zeros((16, 640), LOW)
    else:
        forth = [(i, i + heads) for i in range(seq - heads)]
        back = [(i + heads, i) for i in range(seq - heads)]
        edge = lax.ppermute(pre[-16:], "seq", forth)

    def forward_from(state):
        return run_forward(
            offs, rate, pre, gate_small, edge, head_taps, full_gain_head, state
        )

    state_in = zero_state
    if teams > 1:
        trial = forward_from(zero_state)
        steps, end = trial[4].astype(WIDE) + trial[5].astype(WIDE), trial[10]

        def along(c, total):
            return jnp.dot(total, steps[c].T, precision=lax.Precision.HIGHEST)

        whole_map = lax.fori_loop(0, steps.shape[0], along, jnp.eye(HEAD, dtype=WIDE))
        for _ in range(teams - 1):
            out = jnp.dot(state_in, whole_map, precision=lax.Precision.HIGHEST) + end
            state_in = lax.ppermute(out.astype(LOW), "seq", forth).astype(WIDE)
    conv, inverse, scores, reach, high, rest, gated, mixed, upd, states, _ = forward_from(state_in)
    gated, far_out, far_cot, *column_got = lax.optimization_barrier(
        (gated, far_out, far_cot, *column_got)
    )
    own_columns = lax.dynamic_index_in_dim(columns, member, 0, False)
    full_out = ordered_gather(w_out, "fsdp", far_out).reshape(width, width)
    group_cot = near_gather(cot, "fsdp", far_cot)

    def ordered_columns(which):
        value = jnp.zeros((width, own_columns.shape[2]), LOW)
        for o, rows in zip([0, *others], [own_columns, *column_got]):
            value = lax.dynamic_update_slice(value, rows[which], ((member ^ o) * shard, 0))
        return value

    cols_gate, cols_up = ordered_columns(0), ordered_columns(1)

    pieces = [
        lax.dynamic_slice_in_dim(gated, (head - k) % heads * own_rows, own_rows, 0)
        for k in range(heads)
    ]
    gated_own = rolled(
        jnp.concatenate(swapped(pieces, heads), axis=1), (heads - head) % heads * HEAD, 1
    )
    inputs = tokens[0].astype(WIDE)
    mixer_res = inputs + dot_plain(gated_own, full_out)

    mid_normed = rms_parts(mixer_res)
    mid_low = (mid_normed * full_gain_ffn).astype(LOW)
    group_mid = near_gather(mid_low, "fsdp")
    gate_pre = dot_plain(group_mid, cols_gate)
    up_pre = dot_plain(group_mid, cols_up)
    sig = jax.nn.sigmoid(gate_pre)
    act = gate_pre * sig
    hidden = (act * up_pre).astype(LOW)
    grad_hidden = dot_right(group_cot, w_down)
    grad_gate_pre = (grad_hidden * up_pre * (sig * (1.0 + gate_pre * (1.0 - sig)))).astype(LOW)
    grad_up_pre = (grad_hidden * act).astype(LOW)
    grad_mid = dot_right(grad_gate_pre, cols_gate) + dot_right(grad_up_pre, cols_up)
    grad_gate_pre, grad_up_pre, grad_mid = lax.optimization_barrier(
        (grad_gate_pre, grad_up_pre, grad_mid)
    )
    grad_mid = near_scatter(grad_mid, "fsdp")

    grad_res = cotangent[0].astype(WIDE) + rms_back(grad_mid * full_gain_ffn, mixer_res)
    grad_gain_ffn = jnp.sum(grad_mid * mid_normed, axis=0)
    res_low = grad_res.astype(LOW)
    grad_gated = dot_right(res_low, full_out).astype(LOW)
    own_ff = w_down.shape[0]
    slab = own_ff // seq
    slabs = jnp.concatenate(
        [
            dot_left(grad_gate_pre, group_mid, LOW).reshape(seq, slab, width),
            dot_left(grad_up_pre, group_mid, LOW).reshape(seq, slab, width),
            dot_left(hidden, group_cot, LOW).reshape(seq, slab, width),
        ],
        axis=1,
    )
    permuted = teams == 1 and slab % 8 == 0 and own_ff * 2 % HEAD == 0 and fsdp % 2 == 0

    def turned_columns(summed):
        turned = lax.all_to_all(summed[: 2 * slab], "fsdp", 1, 1, tiled=True)
        return stack(turned, summed[2 * slab :])

    def feed_forward_sums():
        if not permuted:
            summed = lax.psum_scatter(
                slabs.reshape(seq * 3 * slab, width), "seq", scatter_dimension=0, tiled=True
            )
            yield [summed]
            slabs_done = lax.all_gather(turned_columns(summed), "seq", axis=0)
            yield ff_outputs_plain(slabs_done, slab, shard, fsdp)
            return
        def kept(at):
            return lambda came: lax.dynamic_index_in_dim(after(slabs, came), at, 0, False)

        blocks = [
            (lax.dynamic_index_in_dim(slabs, send, 0, False), kept(keep))
            for send, keep in team_places(heads)
        ]
        for stage in scatter_stages(blocks, heads, ties):
            if isinstance(stage, list):
                yield stage
        mine = turned_columns(after(stage.astype(LOW), *ties))
        yield [mine]
        for stage in gather_stages(mine, heads, ties):
            if isinstance(stage[0], tuple):
                break
            yield stage
        yield ff_outputs(stage, slab, shard, fsdp)

    ties, sums = [], feed_forward_sums()
    brought = [next(sums)]

    def beside(value):
        if not isinstance(brought[-1], tuple):
            ties[:] = [value]
            brought.append(next(sums))

    def settled(value):
        stage = brought[-1]
        return value if isinstance(stage, tuple) else after(value, *stage)

    pieces = [
        lax.dynamic_slice_in_dim(grad_gated, (head - k) % heads * HEAD, HEAD, 1)
        for k in range(heads)
    ]
    dgated = rolled(
        jnp.concatenate(swapped(pieces, heads), axis=0), (heads - head) % heads * own_rows, 0
    )
    grad_out = dot_left(after(gated_own, grad_gated), res_low, LOW).reshape(fsdp, shard, width)
    late = near_blocks(grad_out, "fsdp")
    dgated, late = lax.optimization_barrier((dgated, late))
    beside(dgated)
    late_ties = []
    late = near_scatter_stages(late, "fsdp", late_ties)
    late_stage = []

    def gate_back_from(dend):
        return run_gate_back(
            gate_small, full_gain_head, mixed, reach, high, rest, dgated, dend
        )

    dend = zero_state
    if teams > 1:
        begin = gate_back_from(zero_state)[4]
        for _ in range(teams - 1):
            out = lax.dot_general(
                dend, whole_map, (((1,), (1,)), ((), ())), precision=lax.Precision.HIGHEST
            )
            dend = lax.ppermute((out + begin).astype(LOW), "seq", back).astype(WIDE)
    do, ds, dgate, dgain, _ = gate_back_from(dend)
    carried = [
        jnp.zeros((4, 8, 640), WIDE), jnp.zeros((8, 640), WIDE), jnp.zeros((1, HEAD), WIDE)
    ]
    dy, calls = None, 2
    left = length // (PER * SPAN)
    for call in range(calls, 0, -1):
        steps_here = -(-left // call)
        if dy is None:
            carried[0] = after(carried[0], do)
        carried[0] = settled(after(carried[0], *late_stage))
        beside(carried[0])
        late_ties[:] = [carried[0]]
        late_stage = next(late)
        late_stage = late_stage if isinstance(late_stage, list) else [late_stage]
        dy, carried = run_backward(
            left - 1, steps_here, offs, rate, pre, gate_small, edge, head_taps,
            (conv, inverse, upd, scores, states, do, ds, dgate), carried, dy,
        )
        carried = list(carried)
        left -= steps_here
    dy = settled(dy)
    late_stage = late_stage[0]
    for stage in late:
        late_stage = stage
    grad_out = late_stage.astype(LOW)
    following, dtaps, drate = carried
    if teams > 1:
        none = jnp.zeros((16, 640), WIDE)
        dedge = sum(stack(none, following[lag])[lag : lag + 16] for lag in range(1, 4))
        from_next = lax.ppermute(dedge.astype(LOW), "seq", back).astype(WIDE)
        tail = (dy[-16:, :640].astype(WIDE) + from_next).astype(LOW)
        dy = lax.dynamic_update_slice(dy, tail, (length - 16, 0))

    out_rows = shard // heads

    blocks = [
        list(input_blocks(places, dy, grad_out, full_packed, own_rows, out_rows))
        for places in team_places(heads)
    ]
    turned_stage = []
    if not isinstance(brought[-1], tuple):
        beside(blocks[0][0])
        turned_stage = brought[-1] if isinstance(brought[-1], list) else []
    order = jnp.stack([member ^ o for o in near_order(fsdp)]).astype(jnp.int32)
    combined = weight_grads(
        order, normed_low, after(dy, blocks[0][0], *turned_stage), full_packed, full_gain_in[None],
        grad_gain_ffn[None], dgain, drate, dtaps, taps,
    )
    sent = scatter_stages(blocks, heads)
    queue = [next(sent)]
    combined = near_scatter(after(combined, queue[0][0]), "fsdp").astype(LOW)
    *more, joined = sent
    queue += more
    while not isinstance(brought[-1], tuple):
        beside(blocks[0][0])
    out_gate, out_up, out_down = brought[-1]
    down_part = near_scatter(dot_plain(after(hidden, queue[1][0]), w_down).astype(LOW), "fsdp")
    layer_out = (mixer_res + down_part).astype(LOW)
    grad_normed, own_out = joined[:own_rows], joined[own_rows:].astype(LOW)
    input_grad = (grad_res + rms_back(grad_normed * full_gain_in, inputs)).astype(LOW)
    if teams > 1:
        own_out = lax.psum(own_out, "seq", axis_index_groups=head_groups)
    found_out = last_of(gather_stages(own_out, heads))

    if teams > 1:
        combined = lax.psum(combined, "seq", axis_index_groups=head_groups)
    (out_query, out_key, out_value, out_gatew, out_beta, out_decay, out_gain_in, out_gain_ffn,
     out_gain_head, out_rate, out_cq, out_ck, out_cv, out_out) = mixer_outputs(
        last_of(gather_stages(combined, heads, lag=1)), found_out, shard, gain_head.shape[0], taps, fsdp, member
    )

    return (
        layer_out[None],
        input_grad[None],
        out_gain_in[0],
        out_query,
        out_key,
        out_value,
        out_beta.T,
        out_decay.T,
        out_gatew,
        out_cq,
        out_ck,
        out_cv,
        out_rate[0],
        out_gain_head[0],
        out_out,
        out_gain_ffn[0],
        out_gate,
        out_up,
        out_down,
    )


def solution(mesh):
    rows, lanes = P("fsdp", None), P(None, "fsdp")
    block = P("fsdp", "seq", None)
    return jax.shard_map(
        per_device,
        mesh=mesh,
        in_specs=(
            block, block, rows, P("fsdp"), rows, rows, rows, rows, rows, rows,
            lanes, lanes, lanes, P(), P("fsdp"), rows, P("fsdp"), rows, rows, rows,
        ),
        out_specs=(
            block, block, P("fsdp"), rows, rows, rows, rows, rows, rows,
            lanes, lanes, lanes, P(), P("fsdp"), rows, P("fsdp"), rows, rows, rows,
        ),
        check_vma=False,
    )
```
